32 devices in a mesh: dp: 4 (over y, x), fsdp: 8 (over z, core).
Axes of the slice: x: 2, y: 2, z: 4, core: 2. Of those that a mesh axis runs over, the one named last changes fastest.
Arguments:
- tokens: bfloat16 [32, 1024, 1024], P(('dp', 'fsdp')), may hold values from -6 to 6
- cotangent: bfloat16 [32, 1024, 1024], P(('dp', 'fsdp')), may hold values from -6 to 6
- segment_ids: int32 [32, 1024], P(('dp', 'fsdp')), may hold values from 0 to 3, never falling along the last dimension, each value on 1 to 512 neighbouring positions
- padding_mask: int32 [32, 1024], P(('dp', 'fsdp')), may hold values from 0 to 1, as said below
- w_qkv: bfloat16 [1024, 3072], P(('dp', 'fsdp')), may hold values from -0.1875 to 0.1875
- bias_qv: bfloat16 [2048], P(('dp', 'fsdp')), may hold values from -4 to 4
- w_out: bfloat16 [1024, 1024], P(('dp', 'fsdp')), may hold values from -0.75 to 0.75
- bias_out: bfloat16 [1024], P(('dp', 'fsdp')), may hold values from -4 to 4
- gain_attn: bfloat16 [1024], P(('dp', 'fsdp')), may hold values from 0.25 to 1.75
- gain_mlp: bfloat16 [1024], P(('dp', 'fsdp')), may hold values from 0.25 to 1.75
- w_up: bfloat16 [1024, 4096], P(('dp', 'fsdp')), may hold values from -0.1875 to 0.1875
- bias_up: bfloat16 [4096], P(('dp', 'fsdp')), may hold values from -6 to 6
- w_down: bfloat16 [4096, 1024], P(('dp', 'fsdp')), may hold values from -0.09375 to 0.09375
- bias_down: bfloat16 [1024], P(('dp', 'fsdp')), may hold values from -4 to 4
Outputs:
- output: bfloat16 [32, 1024, 1024], P(('dp', 'fsdp'))
- input_grad: bfloat16 [32, 1024, 1024], P(('dp', 'fsdp'))
- grad_w_qkv: float32 [1024, 3072], P(('dp', 'fsdp'))
- grad_bias_qv: float32 [2048], P(('dp', 'fsdp'))
- grad_w_out: float32 [1024, 1024], P(('dp', 'fsdp'))
- grad_bias_out: float32 [1024], P(('dp', 'fsdp'))
- grad_gain_attn: float32 [1024], P(('dp', 'fsdp'))
- grad_gain_mlp: float32 [1024], P(('dp', 'fsdp'))
- grad_w_up: float32 [1024, 4096], P(('dp', 'fsdp'))
- grad_bias_up: float32 [4096], P(('dp', 'fsdp'))
- grad_w_down: float32 [4096, 1024], P(('dp', 'fsdp'))
- grad_bias_down: float32 [1024], P(('dp', 'fsdp'))
- stats: float32 [5], replicated
- real_frames: float32 [1], replicated
The draws below stay inside these ranges and needn't reach their ends.
Inputs may be any that keep to these rules, and one draw needn't show every extreme that they name: `segment_ids`: along each packed row the ids never fall; an item covers at most 512 frames. `padding_mask`: the first frame of every row is real.
All inputs are finite; a program needn't handle non-finite values.
Results may differ from the reference program's by a relative error of at most 0.012.
Values may be sent and summed in bfloat16 or wider, within the bound.
No kernel may reach another device: no remote copies, remote signals or barrier semaphores. Data moves between devices by JAX's collectives and lax.ppermute only.
A program may use at most 256 MiB of HBM per device.

```python
import math
import jax
import jax.numpy as jnp
import numpy as np
from jax import lax

D = 1024
FF = 4096
HD = 64
LEN = 1024
ROWS = 32


def draw_tokens(key, part):
    row_rank = jnp.arange(ROWS, dtype=jnp.float32)[:, None, None] / max(ROWS - 1, 1)
    row_scale = 0.3 + 2.7 * row_rank
    values = jax.random.normal(key, (ROWS, LEN, D), jnp.float32)
    return jnp.clip(values * row_scale, -6.0, 6.0).astype(jnp.bfloat16)


def draw_padding_mask(key, part):
    levels = jax.random.randint(key, (ROWS, LEN), 0, 16)
    row_index = jnp.arange(ROWS, dtype=jnp.int32)[:, None]
    limit = 5 + 10 * row_index // max(ROWS - 1, 1)
    marked = (levels < limit).astype(jnp.int32)
    first_frame = (jnp.arange(LEN) == 0)[None, :]
    return jnp.where(first_frame, 1, marked).astype(jnp.int32)


def with_spikes(array, stream_key, source, target, shards_of, factor):
    def block_of(dim):
        return (jnp.arange(array.shape[dim]) // (array.shape[dim] // shards_of)).reshape((-1,) + (1,) * (array.ndim - 1 - dim))

    one_side = jax.random.permutation(stream_key, shards_of)[block_of(target)]
    second = (block_of(target) + shards_of // 2) % shards_of
    return jnp.where((block_of(source) == one_side) | (block_of(source) == second), factor * array, array)


def level_of(key, dims, cuts, low, high):
    def one(axis_at, shards_of):
        steps = jax.random.uniform(jax.random.fold_in(jax.random.fold_in(key, 6), axis_at), (shards_of,), jnp.float32, low / len(cuts), high / len(cuts))
        return jnp.repeat(jnp.exp(steps), dims[axis_at] // shards_of).reshape((-1,) + (1,) * (len(dims) - axis_at - 1))

    factor_of = one(*cuts[0])
    for cut in cuts[1:]:
        factor_of = factor_of * one(*cut)
    return factor_of


def profile(amount, total, most, lean):
    portions = [(1 << 20) // math.isqrt(standing ** lean) + 1 for standing in range(2, amount + 1)]
    surplus, holding = total - most - (amount - 1), [1] * (amount - 1)
    while surplus > 0:
        free = [i for i in range(amount - 1) if holding[i] < most]
        mass, budget = sum([portions[i] for i in free]), surplus
        for i in free:
            addition = min(most - holding[i], max(1, budget * portions[i] // mass), surplus)
            holding[i] = holding[i] + addition
            surplus = surplus - addition
    return np.array([most] + holding)


def uneven_parts(own_key, amount, total, most, slope):
    if amount == 2:
        one = jax.random.randint(own_key, (), max(1, total - most), min(most, total - 1) + 1)
        return jnp.stack([one, total - one])
    tallies = jnp.asarray(profile(amount, total, most, slope), jnp.int32)
    couples = (amount - 1) // 2
    donor, taker = tallies[1:1 + 2 * couples:2], tallies[2:2 + 2 * couples:2]
    room = jnp.minimum(donor - 1, most - taker)
    shifted = jax.random.randint(jax.random.fold_in(own_key, 1), (couples,), 0, 1 << 20) % (room + 1)
    tallies = tallies.at[1:1 + 2 * couples:2].set(donor - shifted).at[2:2 + 2 * couples:2].set(taker + shifted)
    return tallies[jax.random.permutation(jax.random.fold_in(own_key, 2), amount)]


def centred(stream_key, dims, scale, most, pieces=(), kind=jnp.bfloat16):
    loudness = level_of(stream_key, dims, pieces, -0.22, 0.18) if pieces else 1.0
    entries = jax.random.normal(stream_key, dims, jnp.float32) * scale * loudness
    return jnp.minimum(jnp.maximum(entries, -most), most).astype(kind)


def gaussian_with(rng, extent, scale, bound, cuts, heavy, held_as=jnp.bfloat16):
    drawn = scale * jax.random.normal(rng, extent, jnp.float32)
    if cuts:
        drawn = drawn * level_of(rng, extent, cuts, -0.22, 0.18)
    return jnp.clip(with_spikes(drawn, jax.random.fold_in(rng, 3), *heavy), -bound, bound).astype(held_as)


def setup_inputs(seed: int = 0) -> dict:
    arg_keys = jax.random.split(jax.random.key(seed), 15)
    return {
        "tokens": draw_tokens(jax.random.fold_in(arg_keys[14], 71), 0),
        "cotangent": gaussian_with(arg_keys[1], (ROWS, LEN, D), 1.0, 6.0, ((0, 32),), (0, 2, 32, 2.75)),
        "segment_ids": jax.vmap(lambda own: jnp.searchsorted(jnp.cumsum(uneven_parts(own, 4, LEN, LEN // 2, 0)), jnp.arange(LEN), side="right"))(jax.random.split(arg_keys[2], ROWS)).reshape((ROWS, LEN)).astype(jnp.int32),
        "padding_mask": draw_padding_mask(jax.random.fold_in(arg_keys[14], 71), 0),
        "w_qkv": centred(arg_keys[4], (D, 3 * D), D ** -0.5, 0.1875, ((0, 32),)),
        "bias_qv": centred(arg_keys[5], (2 * D,), 0.3, 4.0, ((0, 32),)),
        "w_out": centred(arg_keys[6], (D, D), (D // 16) ** -0.5, 0.75, ((0, 32),)),
        "bias_out": centred(arg_keys[7], (D,), 0.3, 4.0, ((0, 32),)),
        "gain_attn": jnp.clip(1.0 + 0.15 * jax.random.normal(arg_keys[8], (D,), jnp.float32), 0.25, 1.75).astype(jnp.bfloat16),
        "gain_mlp": jnp.clip(1.0 + 0.15 * jax.random.normal(arg_keys[9], (D,), jnp.float32), 0.25, 1.75).astype(jnp.bfloat16),
        "w_up": centred(arg_keys[10], (D, FF), D ** -0.5, 0.1875, ((0, 32),)),
        "bias_up": centred(arg_keys[11], (FF,), 0.5, 6.0, ((0, 32),)),
        "w_down": centred(arg_keys[12], (FF, D), FF ** -0.5, 0.09375, ((0, 32),)),
        "bias_down": centred(arg_keys[13], (D,), 0.3, 4.0, ((0, 32),)),
    }


@jax.custom_vjp
def low(v):
    return lax.optimization_barrier(v.astype(jnp.bfloat16)).astype(jnp.float32)

@jax.custom_vjp
def low_back(v):
    return v

def low_keep(v):
    return (low(v), None)

def low_pass(kept, grad):
    return (grad,)

def back_keep(v):
    return (v, None)

def back_low(kept, grad):
    return (low(grad),)
low.defvjp(low_keep, low_pass)
low_back.defvjp(back_keep, back_low)
highest = lax.Precision.HIGHEST

def matmul(left, right):
    return jnp.dot(left, right, precision=highest)

def rms_norm(values, gain):
    return values * lax.rsqrt(lax.optimization_barrier(jnp.mean(values * values, -1, keepdims=True)) + 1e-05) * gain

def gelu_tanh(values):
    return 0.5 * values * (1.0 + jnp.tanh(0.7978845608028654 * (values + 0.044715 * values * values * values)))

def layer_block(params, frames_in, seg_group, mask_group):
    qkv_w, qv_bias, out_w, out_bias, attn_gain, mlp_gain, up_w, up_bias, down_w, down_bias = params
    groups = frames_in.shape[0]
    heads = D // HD
    frames = frames_in.reshape(groups * LEN, D)
    normed_in = low(rms_norm(frames, attn_gain))
    projected = matmul(normed_in, qkv_w)

    def split_heads(values):
        return low_back(low(values)).reshape(groups, LEN, heads, HD)
    queries = split_heads(projected[:, :D] + qv_bias[:D])
    keys_all = split_heads(projected[:, D:2 * D])
    values_all = split_heads(projected[:, 2 * D:] + qv_bias[D:])
    scores = jnp.einsum('gqhd,gkhd->ghqk', queries, keys_all, precision=highest) * HD ** (-0.5)
    position = jnp.arange(LEN)
    same_item = seg_group[:, :, None] == seg_group[:, None, :]
    causal = position[None, None, :] <= position[None, :, None]
    itself = position[None, None, :] == position[None, :, None]
    usable = (mask_group[:, None, :] == 1) | itself
    allowed = (same_item & causal & usable)[:, None]
    scores = low_back(jnp.where(allowed, scores, -1e+30))
    highest_score = lax.optimization_barrier(jnp.max(scores, -1, keepdims=True))
    expanded = jnp.exp(scores - highest_score)
    probs = low(expanded / lax.optimization_barrier(jnp.sum(expanded, -1, keepdims=True)))
    mixed = jnp.einsum('ghqk,gkhd->gqhd', probs, values_all, precision=highest).reshape(groups * LEN, D)
    mixed = low_back(low(mixed))
    attn_branch = low_back(matmul(mixed, out_w) + out_bias)
    middle = frames + attn_branch
    normed_mid = low(rms_norm(middle, mlp_gain))
    pre_act = low_back(matmul(normed_mid, up_w) + up_bias)
    activated = low(gelu_tanh(pre_act))
    mlp_branch = low_back(matmul(activated, down_w) + down_bias)
    final = middle + mlp_branch
    weight = mask_group.reshape(groups * LEN).astype(jnp.float32)
    totals = [jnp.sum(weight * lax.optimization_barrier(jnp.sum(member * member, -1))) for member in (frames, middle, final, attn_branch, mlp_branch)]
    totals.append(jnp.sum(weight))
    return (final.reshape(groups, LEN, D), jnp.stack(totals))

def run_group(params, element):
    return layer_block(params, element[0], element[1], element[2])

def forward(params, frames_all, segment_ids, padding_mask):
    group_rows = math.gcd(ROWS, max(1, 2048 // LEN))
    group_count = ROWS // group_rows
    checked = jax.checkpoint(run_group)
    outputs, totals = lax.map(lambda element: checked(params, element), (frames_all.reshape(group_count, group_rows, LEN, D), segment_ids.reshape(group_count, group_rows, LEN), padding_mask.reshape(group_count, group_rows, LEN)))
    return (outputs.reshape(ROWS, LEN, D), lax.optimization_barrier(jnp.sum(totals, 0)))

def reference(tokens, cotangent, segment_ids, padding_mask, w_qkv, bias_qv, w_out, bias_out, gain_attn, gain_mlp, w_up, bias_up, w_down, bias_down):
    params = tuple((member.astype(jnp.float32) for member in (w_qkv, bias_qv, w_out, bias_out, gain_attn, gain_mlp, w_up, bias_up, w_down, bias_down)))
    frames = tokens.astype(jnp.float32)

    def wrapped(param_tuple, frames_in):
        return forward(param_tuple, frames_in, segment_ids, padding_mask)
    final, pull_back, totals = jax.vjp(wrapped, params, frames, has_aux=True)
    grad_params, grad_frames = pull_back(cotangent.astype(jnp.float32))
    count_all = totals[5]
    stats = jnp.sqrt(totals[:5] / (count_all * D))
    real_frames = totals[5:6]
    return (final.astype(jnp.bfloat16), grad_frames.astype(jnp.bfloat16), grad_params[0], grad_params[1], grad_params[2], grad_params[3], grad_params[4], grad_params[5], grad_params[6], grad_params[7], grad_params[8], grad_params[9], stats, real_frames)
```

```python
import functools

import jax
import jax.numpy as jnp
import numpy as np
from jax import lax
from jax.experimental import pallas as pl
from jax.experimental.pallas import tpu as pltpu
from jax.sharding import PartitionSpec as P

AXES = ("dp", "fsdp")
HD = 64
QB = 128
SPAN = 512
F32 = jnp.float32
BF16 = jnp.bfloat16

CORE = 1


def ladder_hops(mesh):
    if dict(mesh.shape) != {"dp": 4, "fsdp": 8}:
        return None
    return ((4, 2, 8, 16), (4, 2, 16, 8))


def slot_keys(hops):
    def own(bits):
        keys = [0]
        for bit in bits:
            keys = keys + [key ^ bit for key in keys]
        return keys

    first, second = own(hops[0]), own(hops[1])
    return np.array(
        [first + [key ^ CORE for key in second], second + [key ^ CORE for key in first]], np.int32
    )


def hop(value, bits, count):
    pairs = [(device, device ^ bits[device & CORE]) for device in range(count)]
    return lax.ppermute(value, AXES, pairs)


class Ladder:
    def __init__(self, mesh):
        self.hops = ladder_hops(mesh)
        self.count = int(np.prod(list(mesh.shape.values())))
        self.native = self.hops is None
        if not self.native:
            self.keys = slot_keys(self.hops)
            self.places = np.argsort(self.keys, 1).astype(np.int32)

    def tables(self):
        every = jnp.arange(self.count, dtype=jnp.int32)
        if self.native:
            return every, every
        me = lax.axis_index(AXES)
        odd = (me & CORE) == 1
        shard_of = me ^ jnp.where(odd, self.keys[1], self.keys[0])
        place = jnp.where(odd, self.places[1], self.places[0])
        return shard_of, place[every ^ me]

    def step(self, value, level):
        return hop(value, [self.hops[0][level], self.hops[1][level]], self.count)

    def across(self, value):
        return hop(value, [CORE, CORE], self.count)

    def gather(self, shard):
        if self.native:
            return [lax.all_gather(shard, AXES, axis=0, tiled=False)]
        held = shard[None]
        for level in range(3):
            held = jnp.concatenate([held, self.step(held, level)], 0)
        far = self.step(held, 3)
        return [held, far, self.across(held), self.across(far)]

    def scatter(self, keep, send, wire):
        parts = [keep, self.across(send)]
        for level in (3, 2, 1, 0):
            half = parts[0].shape[0] // 2
            total = sum(part[half:].astype(F32) for part in parts).astype(wire)
            parts = [part[:half] for part in parts] + [self.step(total, level)]
        return sum(part.astype(F32) for part in parts)[0]

    def reduce_blocks(self, blocks, shard_of, wire):
        if self.native:
            flat = blocks.reshape((blocks.shape[0] * blocks.shape[1],) + blocks.shape[2:])
            return lax.psum_scatter(flat.astype(F32), AXES, scatter_dimension=0, tiled=True)
        half = self.count // 2
        ordered = jnp.take(blocks.astype(wire), shard_of, axis=0)
        return self.scatter(ordered[:half], ordered[half:], wire)

def nt(a, b):
    return lax.dot_general(a, b, (((1,), (1,)), ((), ())), preferred_element_type=F32)


def nn(a, b):
    return lax.dot_general(a, b, (((1,), (0,)), ((), ())), preferred_element_type=F32)


def fill_bias(lo_ref, segc_ref, padc_ref, segr_ref, bias_ref, nblocks, most):
    def one(qb, _):
        lo = lo_ref[qb]
        q0 = pl.multiple_of(qb * QB, QB)
        segq = segr_ref[pl.ds(qb, 1), :]
        qpos = q0 + lax.broadcasted_iota(jnp.int32, (QB, QB), 1)

        def part(j, _):
            k0 = pl.multiple_of((lo + j) * QB, QB)
            kpos = k0 + lax.broadcasted_iota(jnp.int32, (QB, QB), 0)
            segk = segc_ref[pl.ds(k0, QB), :]
            padk = padc_ref[pl.ds(k0, QB), :]
            ok = (segk == segq) & (kpos <= qpos) & ((padk == 1) | (kpos == qpos))
            bias_ref[qb, pl.ds(pl.multiple_of(j * QB, QB), QB), :] = jnp.where(ok, 0.0, -1e30)
            return 0

        lax.fori_loop(0, qb - lo + 1, part, 0)
        return 0

    lax.fori_loop(0, nblocks, one, 0)


def head_pair(x, scale):
    lane = lax.broadcasted_iota(jnp.int32, x.shape, 1)
    first = jnp.where(lane < HD, scale, 0.0).astype(x.dtype)
    second = jnp.where(lane < HD, 0.0, scale).astype(x.dtype)
    return jnp.concatenate([x * first, x * second], 0)


def attn_fwd_kernel(nblocks, most, lo_ref, segc_ref, padc_ref, segr_ref, q_ref, k_ref, v_ref, o_ref, lse_ref, bias_ref, vt_ref):
    @pl.when(pl.program_id(0) == 0)
    def _():
        fill_bias(lo_ref, segc_ref, padc_ref, segr_ref, bias_ref, nblocks, most)

    vt_ref[...] = v_ref[...].astype(F32).T.astype(BF16)

    def block(qb, _):
        lo = lo_ref[qb]
        q0 = pl.multiple_of(qb * QB, QB)
        q2 = head_pair(q_ref[pl.ds(q0, QB), :], HD ** -0.5)
        k0 = pl.multiple_of(lo * QB, QB)
        for n in range(1, most + 1):
            @pl.when(qb - lo + 1 == n)
            def _(n=n):
                w = n * QB
                s = nt(k_ref[pl.ds(k0, w), :], q2)
                bias = bias_ref[qb, 0:w, :]
                s = s + jnp.concatenate([bias, bias], 1)
                m = jnp.max(s, 0, keepdims=True)
                p = jnp.exp(s - m)
                total = jnp.sum(p, 0, keepdims=True)
                p = p * (1.0 / total)
                o = nn(vt_ref[:, pl.ds(k0, w)], p.astype(BF16))
                o = jnp.concatenate([o[:HD, :QB], o[HD:, QB:]], 0)
                o_ref[pl.ds(q0, QB), :] = o.T.astype(BF16)
                lse_ref[pl.ds(qb, 1), :] = m + jnp.log(total)
        return 0

    lax.fori_loop(0, nblocks, block, 0)


def attn_bwd_kernel(nblocks, most, lo_ref, segc_ref, padc_ref, segr_ref, q_ref, k_ref, v_ref, do_ref, lse_ref,
                    dq_ref, dk_ref, dv_ref, sums_ref, bias_ref, kt_ref, dk_acc, dv_acc):
    @pl.when(pl.program_id(0) == 0)
    def _():
        fill_bias(lo_ref, segc_ref, padc_ref, segr_ref, bias_ref, nblocks, most)

    kt_ref[...] = k_ref[...].astype(F32).T.astype(BF16)
    dk_acc[...] = jnp.zeros_like(dk_acc)
    dv_acc[...] = jnp.zeros_like(dv_acc)
    sums_ref[...] = jnp.zeros_like(sums_ref)

    def block(qb, _):
        lo = lo_ref[qb]
        q0 = pl.multiple_of(qb * QB, QB)
        q2 = head_pair(q_ref[pl.ds(q0, QB), :], HD ** -0.5)
        do2 = head_pair(do_ref[pl.ds(q0, QB), :], 1.0)
        k0 = pl.multiple_of(lo * QB, QB)
        lse = lse_ref[pl.ds(qb, 1), :]
        for n in range(1, most + 1):
            @pl.when(qb - lo + 1 == n)
            def _(n=n):
                w = n * QB
                s = nt(k_ref[pl.ds(k0, w), :], q2)
                bias = bias_ref[qb, 0:w, :]
                p = jnp.exp(s + jnp.concatenate([bias, bias], 1) - lse)
                dp = nt(v_ref[pl.ds(k0, w), :], do2)
                inner = jnp.sum(p * dp, 0, keepdims=True)
                ds = (p * (dp - inner)).astype(BF16)
                dv_acc[pl.ds(k0, w), :] += nn(p.astype(BF16), do2)
                dk_acc[pl.ds(k0, w), :] += nn(ds, q2)
                dq = nn(kt_ref[:, pl.ds(k0, w)], ds)
                dq = jnp.concatenate([dq[:HD, :QB], dq[HD:, QB:]], 0) * (HD ** -0.5)
                dq = dq.T.astype(BF16)
                dq_ref[pl.ds(q0, QB), :] = dq
                sums_ref[0:1, :] += jnp.sum(dq.astype(F32), 0, keepdims=True)
        return 0

    lax.fori_loop(0, nblocks, block, 0)
    dk_ref[...] = dk_acc[...].astype(BF16)
    dv = dv_acc[...].astype(BF16)
    dv_ref[...] = dv
    sums_ref[1:2, :] = jnp.sum(dv.astype(F32), 0, keepdims=True)


def mask_inputs(segment_ids, padding_mask):
    length = segment_ids.shape[0]
    nblocks = length // QB
    first = segment_ids.reshape(nblocks, QB)[:, 0]
    start = jnp.sum((segment_ids[None, :] < first[:, None]).astype(jnp.int32), 1)
    lo = start // QB
    segc = jnp.broadcast_to(segment_ids[:, None], (length, QB))
    padc = jnp.broadcast_to(padding_mask[:, None], (length, QB))
    return lo.astype(jnp.int32), segc, padc, segment_ids.reshape(nblocks, QB)


def attn_forward(q, k, v, masks, first=0, pairs=None):
    length, width = q[0].shape[0], 128
    nblocks = length // QB
    most = min(nblocks, SPAN // QB + 1)
    pairs = pairs or 8
    lo, segc, padc, segr = masks
    (qa, qo), (ka, ko), (va, vo) = q, k, v
    whole = lambda p, lo: (0, 0)
    col = lambda off: pl.BlockSpec((length, width), lambda p, lo: (0, off + first + p))
    return pl.pallas_call(
        functools.partial(attn_fwd_kernel, nblocks, most),
        grid_spec=pltpu.PrefetchScalarGridSpec(
            num_scalar_prefetch=1, grid=(pairs,),
            in_specs=[pl.BlockSpec((length, QB), whole), pl.BlockSpec((length, QB), whole), pl.BlockSpec((nblocks, QB), whole),
                      col(qo), col(ko), col(vo)],
            out_specs=[pl.BlockSpec((length, width), lambda p, lo: (0, p)),
                       pl.BlockSpec((None, nblocks, 2 * QB), lambda p, lo: (p, 0, 0))],
            scratch_shapes=[pltpu.VMEM((nblocks, most * QB, QB), F32), pltpu.VMEM((width, length), BF16)]),
        out_shape=[jax.ShapeDtypeStruct((length, pairs * width), BF16), jax.ShapeDtypeStruct((pairs, nblocks, 2 * QB), F32)],
        compiler_params=pltpu.CompilerParams(vmem_limit_bytes=48 << 20),
        name="attn_forward",
    )(lo, segc, padc, segr, qa, ka, va)


def attn_backward(q, k, v, do, lse, masks, first=0, pairs=None):
    length, width = q[0].shape[0], 128
    nblocks = length // QB
    most = min(nblocks, SPAN // QB + 1)
    pairs = pairs or 8
    lo, segc, padc, segr = masks
    (qa, qo), (ka, ko), (va, vo) = q, k, v
    whole = lambda p, lo: (0, 0)
    col = lambda off: pl.BlockSpec((length, width), lambda p, lo: (0, off + first + p))
    out = pl.BlockSpec((length, width), lambda p, lo: (0, p))
    return pl.pallas_call(
        functools.partial(attn_bwd_kernel, nblocks, most),
        grid_spec=pltpu.PrefetchScalarGridSpec(
            num_scalar_prefetch=1, grid=(pairs,),
            in_specs=[pl.BlockSpec((length, QB), whole), pl.BlockSpec((length, QB), whole), pl.BlockSpec((nblocks, QB), whole),
                      col(qo), col(ko), col(vo), col(0),
                      pl.BlockSpec((None, nblocks, 2 * QB), lambda p, lo: (first + p, 0, 0))],
            out_specs=[out, out, out, pl.BlockSpec((8, width), lambda p, lo: (0, p))],
            scratch_shapes=[pltpu.VMEM((nblocks, most * QB, QB), F32), pltpu.VMEM((width, length), BF16),
                            pltpu.VMEM((length, width), F32), pltpu.VMEM((length, width), F32)]),
        out_shape=[jax.ShapeDtypeStruct((length, pairs * width), BF16)] * 3 + [jax.ShapeDtypeStruct((8, pairs * width), F32)],
        compiler_params=pltpu.CompilerParams(vmem_limit_bytes=48 << 20),
        name="attn_backward",
    )(lo, segc, padc, segr, qa, ka, va, do, lse)


def rms_norm(values, gain):
    return values * lax.rsqrt(jnp.mean(values * values, -1, keepdims=True) + 1e-05) * gain


def gelu_tanh(values):
    return (
        0.5
        * values
        * (1.0 + jnp.tanh(0.7978845608028654 * (values + 0.044715 * values * values * values)))
    )


def contract_rows(left, right):
    return lax.dot_general(left, right, (((0,), (0,)), ((), ())), preferred_element_type=F32)


def row_squares(values, valid):
    return jnp.sum(valid * jnp.sum(values * values, -1))


def local(ladder, tokens, cotangent, segment_ids, padding_mask, w_qkv, bias_qv, w_out, bias_out, gain_attn, gain_mlp,
          w_up, bias_up, w_down, bias_down):
    length, width = tokens.shape[1], tokens.shape[2]
    count = ladder.count
    shard_of, place = ladder.tables()

    def whole(pieces):
        full = pieces[0] if len(pieces) == 1 else jnp.take(jnp.concatenate(pieces, 0), place, axis=0)
        return full.reshape((full.shape[0] * full.shape[1],) + full.shape[2:])

    smalls = [bias_qv, bias_out, gain_attn, gain_mlp, bias_up, bias_down]
    sizes = [s.shape[0] for s in smalls]
    total = sum(sizes)
    rows = w_qkv.shape[0]
    extra = -(-total // (rows * 128)) * 128
    packed = jnp.pad(jnp.concatenate(smalls), (0, rows * extra - total)).reshape(rows, extra)
    qkv_packed = whole(ladder.gather(jnp.concatenate([w_qkv, packed], 1)))
    qkv_w = qkv_packed[:, : 3 * width]
    vectors = qkv_packed[:, 3 * width :].reshape(count, rows * extra).astype(F32)
    ends = np.cumsum([0] + sizes)
    qv_bias, out_bias, attn_gain, mlp_gain, up_bias, down_bias = [
        vectors[:, ends[i] : ends[i + 1]].reshape(-1) for i in range(6)
    ]
    out_w = whole(ladder.gather(w_out))
    up_w = whole(ladder.gather(w_up))
    down_w = whole(ladder.gather(w_down))

    masks = mask_inputs(segment_ids[0], padding_mask[0])
    valid = padding_mask[0].astype(F32)
    frames = tokens[0].astype(F32)
    normed_in = rms_norm(frames, attn_gain).astype(BF16)
    projected = jnp.dot(normed_in, qkv_w, preferred_element_type=F32)
    offset = jnp.concatenate([qv_bias[:width], jnp.zeros((width,), F32), qv_bias[width:]])
    projected = (projected + offset).astype(BF16)
    per = width // 128
    triple = ((projected, 0), (projected, per), (projected, 2 * per))
    mixed, lse = attn_forward(*triple, masks)
    attn_branch = jnp.dot(mixed, out_w, preferred_element_type=F32) + out_bias
    middle = frames + attn_branch
    normed_mid = rms_norm(middle, mlp_gain).astype(BF16)
    pre_act = jnp.dot(normed_mid, up_w, preferred_element_type=F32) + up_bias
    activated = gelu_tanh(pre_act).astype(BF16)
    mlp_branch = jnp.dot(activated, down_w, preferred_element_type=F32) + down_bias
    final = middle + mlp_branch
    output = final.astype(BF16)[None]

    grad_out = cotangent[0]
    grad_float = grad_out.astype(F32)
    blocks = lambda g: g.reshape((count, g.shape[0] // count) + g.shape[1:])
    own = lambda g: ladder.reduce_blocks(blocks(g), shard_of, BF16)
    own_down = own(contract_rows(activated, grad_out))
    grad_act = nt(grad_out, down_w)
    _, gelu_pull = jax.vjp(gelu_tanh, pre_act)
    grad_pre = gelu_pull(grad_act)[0].astype(BF16)
    own_up = own(contract_rows(normed_mid, grad_pre))
    grad_normed_mid = nt(grad_pre, up_w)
    _, mid_pull = jax.vjp(rms_norm, middle, mlp_gain)
    grad_middle_norm, grad_mlp_gain = mid_pull(grad_normed_mid)
    grad_middle = grad_float + grad_middle_norm
    grad_branch = grad_middle.astype(BF16)
    own_out = own(contract_rows(mixed, grad_branch))
    grad_mixed = nt(grad_branch, out_w).astype(BF16)
    dq, dk, dv, sums = attn_backward(*triple, grad_mixed, lse, masks)
    grad_projected = jnp.concatenate([dq, dk, dv], 1)
    own_qkv = own(contract_rows(normed_in, grad_projected))
    grad_normed_in = nt(grad_projected, qkv_w)
    _, first_pull = jax.vjp(rms_norm, frames, attn_gain)
    grad_input_norm, grad_attn_gain = first_pull(grad_normed_in)
    input_grad = (grad_middle + grad_input_norm).astype(BF16)[None]

    members = jnp.stack([row_squares(frames, valid), row_squares(middle, valid), row_squares(final, valid),
                         row_squares(attn_branch, valid), row_squares(mlp_branch, valid), jnp.sum(valid)])
    small_grads = [jnp.concatenate([sums[0], sums[1]]), jnp.sum(grad_branch.astype(F32), 0), grad_attn_gain, grad_mlp_gain,
                   jnp.sum(grad_pre.astype(F32), 0), jnp.sum(grad_float, 0)]
    table = jnp.concatenate([g.reshape(count, -1) for g in small_grads] + [jnp.broadcast_to(members, (count, 6))], 1)
    size = -(-table.shape[1] // 128) * 128
    table = jnp.pad(table, ((0, 0), (0, size - table.shape[1])))
    own_small = ladder.reduce_blocks(table[:, None], shard_of, F32).reshape(-1)
    owned = [own_small[ends[i] : ends[i + 1]] for i in range(6)]
    totals = own_small[total : total + 6]
    stats = jnp.sqrt(totals[:5] / (totals[5] * width))
    return (output, input_grad, own_qkv, owned[0], own_out, owned[1], owned[2], owned[3], own_up, owned[4], own_down,
            owned[5], stats, totals[5:6])


def solution(mesh):
    rows, wide, flat = P(AXES, None, None), P(AXES, None), P(AXES)
    return jax.shard_map(
        functools.partial(local, Ladder(mesh)),
        mesh=mesh,
        in_specs=(rows, rows, wide, wide, wide, flat, wide, flat, flat, flat, wide, flat, wide, flat),
        out_specs=(rows, rows, wide, flat, wide, flat, flat, flat, wide, flat, wide, flat, P(), P()),
        check_vma=False,
    )
```

```python
import functools

import jax
import jax.numpy as jnp
import numpy as np
from jax import lax
from jax.experimental import pallas as pl
from jax.experimental.pallas import tpu as pltpu
from jax.sharding import PartitionSpec as P

HD = 64
QB = 128
SPAN = 512
MANY = 4
WEIGH = 3
F32 = jnp.float32
BF16 = jnp.bfloat16

CORE = 1
Z_HOPS = (2, 4, 6)
MIX = ((0, 1, 2, 3), (0, 2, 1, 3))
FLIP = (0, 2, 1, 3)
HOPS = ((4, 2, 8, 16), (4, 2, 16, 8))


def tie(value, *others):
    return lax.optimization_barrier((value,) + others)[0]


def add_up(*terms):
    return sum(term.astype(F32) for term in terms)


def cost(microseconds):
    return pl.CostEstimate(flops=int(WEIGH * microseconds * 1.15e9), transcendentals=0, bytes_accessed=0)


class Ladder:
    def __init__(self, mesh):
        self.count = int(np.prod(list(mesh.shape.values())))
        self.native = dict(mesh.shape) != {"dp": 4, "fsdp": 8}
        self.axes = ("dp", "fsdp")
        if not self.native:
            keys = []
            for core in (0, 1):
                both = []
                for which, extra in ((core, 0), (1 - core, CORE)):
                    own = [extra]
                    for bit in HOPS[which]:
                        own = own + [key ^ bit for key in own]
                    both += own
                keys.append(both)
            self.keys = np.array(keys, np.int32)
            self.places = np.argsort(self.keys, 1).astype(np.int32)

    def place(self):
        if self.native:
            self.meta = jnp.array([0, 1, 2, 3, 0, 0], jnp.int32)
            self.order = jnp.arange(4)
            return
        me = lax.axis_index(self.axes)
        odd = (me & CORE) == 1
        mix = jnp.where(odd, jnp.array(MIX[1], jnp.int32), jnp.array(MIX[0], jnp.int32))
        self.meta = jnp.concatenate([(me >> 3) ^ mix, (me & CORE)[None], ((me >> 1) & 3)[None]])
        self.order = mix[jnp.arange(4) ^ (me >> 3)]
        every = jnp.arange(self.count, dtype=jnp.int32)
        self.shard_of = me ^ jnp.where(odd, self.keys[1], self.keys[0])
        self.slot_of = jnp.where(odd, self.places[1], self.places[0])[every ^ me]

    def flip(self, value, even, odd):
        bits = (even, odd)
        return lax.ppermute(value, self.axes, [(i, i ^ bits[i & CORE]) for i in range(self.count)])

    def step(self, value, level):
        return self.flip(value, HOPS[0][level], HOPS[1][level])

    def across(self, value):
        return self.flip(value, CORE, CORE)

    def gather_small(self, vector):
        if self.native:
            return lax.all_gather(vector, self.axes, axis=0, tiled=False)
        held = vector[None]
        for level in range(4):
            held = jnp.concatenate([held, self.step(held, level)], 0)
        return jnp.take(jnp.concatenate([held, self.across(held)], 0), self.slot_of, axis=0)

    def scatter_small(self, table):
        if self.native:
            return lax.psum_scatter(table, self.axes, scatter_dimension=0, tiled=True).reshape(-1)
        half = self.count // 2
        table = jnp.take(table, self.shard_of, axis=0)
        total = table[:half] + self.across(table[half:])
        for level in (3, 2, 1, 0):
            half = half // 2
            total = total[:half] + self.step(total[half:], level)
        return total[0]


def place_kernel(meta, *refs):
    pieces, out_ref = refs[:4], refs[4]
    for k in range(4):
        out_ref[meta[5] ^ k] = pieces[k][...]


def place_group(meta, pieces):
    rows, columns = pieces[0].shape
    tile = columns // 2
    return pl.pallas_call(
        place_kernel,
        grid_spec=pltpu.PrefetchScalarGridSpec(
            num_scalar_prefetch=1, grid=(2,), in_specs=[pl.BlockSpec((rows, tile), lambda n, meta: (0, n))] * 4,
            out_specs=pl.BlockSpec((4, rows, tile), lambda n, meta: (0, 0, n))),
        out_shape=jax.ShapeDtypeStruct((4, rows, columns), pieces[0].dtype),
        cost_estimate=cost(2),
        name="place_group",
    )(meta, *pieces)


def spread_kernel(meta, *refs):
    parts, outs = refs[:16], refs[16:]
    for k in range(4):
        total = sum(part[...].astype(F32) for part in parts[4 * k : 4 * k + 4])
        outs[k][...] = total.astype(outs[k].dtype)


def spread_sums(meta, keep, near, third, second):
    _, rows, columns = second.shape
    tile = columns // 2 if columns > 1024 else columns
    if rows > 32:
        tile = columns // 4
    specs, operands = [], []
    for k in range(4):
        group = pl.BlockSpec((None, rows, tile), lambda n, meta, k=k: (meta[5] ^ k, 0, n))
        pair = pl.BlockSpec((None, None, rows, tile), lambda n, meta, k=k: (0, meta[5] ^ k, 0, n))
        specs += [pair, pair, pair, group]
        operands += [keep, near, third, second]
    out = pl.BlockSpec((rows, tile), lambda n, meta: (0, n))
    return pl.pallas_call(
        spread_kernel,
        grid_spec=pltpu.PrefetchScalarGridSpec(num_scalar_prefetch=1, grid=(columns // tile,), in_specs=specs, out_specs=[out] * 4),
        out_shape=[jax.ShapeDtypeStruct((rows, columns), F32)] + [jax.ShapeDtypeStruct((rows, columns), BF16)] * 3,
        cost_estimate=cost(3),
        name="spread_sums",
    )(meta, *operands)


class Gather:
    def __init__(self, ladder, shard, direct):
        self.ladder, self.shard, self.native, self.direct = ladder, shard, ladder.native, direct
        self.sent = ()

    def start(self, *after):
        if not self.native:
            self.shard = tie(self.shard, *after)
            self.sent = (self.shard,)
            bits = Z_HOPS if self.direct else Z_HOPS[1:2]
            self.others = [self.ladder.flip(self.shard, bit, bit) for bit in bits]

    def low(self, *after):
        if not self.native:
            one, two = tie(self.others[0], *after), self.shard
            high = (self.ladder.meta[5] >> 1) == 1
            self.pair = jnp.where(high, jnp.stack([one, two]), jnp.stack([two, one]))
            self.sent = (self.pair,)
            self.others = [self.ladder.flip(self.pair, Z_HOPS[0], Z_HOPS[0])]

    def plane(self, *after):
        if not self.native:
            others = [tie(other, *after) for other in self.others]
            if self.direct:
                self.own = place_group(self.ladder.meta, [self.shard] + others)
            else:
                one, two = others[0], self.pair
                low = (self.ladder.meta[5] & 1) == 1
                own = jnp.where(low, jnp.stack([one, two], 1), jnp.stack([two, one], 1))
                self.own = own.reshape((4,) + self.shard.shape)
            self.sent = (self.own,)
            self.second = self.ladder.step(self.own, 2)
            self.third = self.ladder.step(self.own, 3)
            self.far = [self.ladder.across(self.own)]

    def corner(self, *after):
        if not self.native:
            self.second, self.third = tie(self.second, *after), tie(self.third, *after)
            self.sent = (self.second, self.third)
            self.fourth = self.ladder.step(self.second, 3)
            self.far += [self.ladder.across(self.third), self.ladder.across(self.second)]

    def finish(self, *after):
        if self.native:
            self.groups = [lax.all_gather(self.shard, self.ladder.axes, axis=0, tiled=True)]
        else:
            self.fourth = tie(self.fourth, *after)
            self.sent = (self.fourth,)
            self.far += [self.ladder.across(self.fourth)]
            self.groups = [self.own, self.second, self.third, self.fourth] + self.far
        return self.groups


class Scatter:
    def __init__(self, ladder, parts):
        self.ladder, self.native, self.parts = ladder, ladder.native, parts
        self.sent = ()
        if not self.native:
            self.keep = parts[0]
            self.near = ladder.across(parts[1])

    def corner(self, *after):
        if not self.native:
            self.near = tie(self.near, *after)
            total = add_up(self.keep[2:], self.near[2:]).astype(BF16)
            self.sent = (total,)
            self.third = self.ladder.step(total, 3)

    def plane(self, *after):
        if not self.native:
            self.third = tie(self.third, *after)
            total = add_up(self.keep[1], self.near[1], self.third[1]).astype(BF16)
            self.sent = (total,)
            self.second = self.ladder.step(total, 2)

    def spread(self, *after):
        if not self.native:
            second = tie(self.second, *after)
            self.mine, *away = spread_sums(self.ladder.meta, self.keep, self.near, self.third, second)
            self.sent = tuple(away)
            self.last = [self.ladder.flip(part, bit, bit) for part, bit in zip(away, Z_HOPS)]

    def finish(self, *after):
        if self.native:
            return lax.psum_scatter(self.parts[0].astype(F32), self.ladder.axes, scatter_dimension=0, tiled=True)
        total = add_up(self.mine, *[tie(part, *after) for part in self.last])
        self.sent = (total,)
        return total


def nt(a, b):
    return lax.dot_general(a, b, (((1,), (1,)), ((), ())), preferred_element_type=F32)


def nn(a, b):
    return lax.dot_general(a, b, (((1,), (0,)), ((), ())), preferred_element_type=F32)


def fill_bias(lo_ref, segc_ref, padc_ref, segr_ref, bias_ref, nblocks, most):
    def one(qb, _):
        lo = lo_ref[qb]
        q0 = pl.multiple_of(qb * QB, QB)
        segq = segr_ref[pl.ds(qb, 1), :]
        qpos = q0 + lax.broadcasted_iota(jnp.int32, (QB, QB), 1)

        def part(j, _):
            k0 = pl.multiple_of((lo + j) * QB, QB)
            kpos = k0 + lax.broadcasted_iota(jnp.int32, (QB, QB), 0)
            segk = segc_ref[pl.ds(k0, QB), :]
            padk = padc_ref[pl.ds(k0, QB), :]
            ok = (segk == segq) & (kpos <= qpos) & ((padk == 1) | (kpos == qpos))
            bias_ref[qb, pl.ds(pl.multiple_of(j * QB, QB), QB), :] = jnp.where(ok, 0.0, -1e30)
            return 0

        lax.fori_loop(0, qb - lo + 1, part, 0)
        return 0

    lax.fori_loop(0, nblocks, one, 0)


def head_pair(x, scale):
    lane = lax.broadcasted_iota(jnp.int32, x.shape, 1)
    first = jnp.where(lane < HD, scale, 0.0).astype(x.dtype)
    second = jnp.where(lane < HD, 0.0, scale).astype(x.dtype)
    return jnp.concatenate([x * first, x * second], 0)


def attn_fwd_kernel(nblocks, most, many, lo_ref, segc_ref, padc_ref, segr_ref, q_ref, k_ref, v_ref, o_ref, lse_ref, bias_ref, vt_ref):
    @pl.when(pl.program_id(0) == 0)
    def _():
        fill_bias(lo_ref, segc_ref, padc_ref, segr_ref, bias_ref, nblocks, most)

    vt_ref[...] = v_ref[...].T

    def block(qb, _):
        lo = lo_ref[qb]
        q0 = pl.multiple_of(qb * QB, QB)
        k0 = pl.multiple_of(lo * QB, QB)
        for n in range(1, most + 1):
            @pl.when(qb - lo + 1 == n)
            def _(n=n):
                w = n * QB
                bias = bias_ref[qb, 0:w, :]
                bias = jnp.concatenate([bias, bias], 1)
                cols = [slice(128 * i, 128 * (i + 1)) for i in range(many)]
                scores = [nt(k_ref[pl.ds(k0, w), c], head_pair(q_ref[pl.ds(q0, QB), c], HD ** -0.5)) + bias for c in cols]
                tops = [jnp.max(s, 0, keepdims=True) for s in scores]
                parts = [jnp.exp(s - m) for s, m in zip(scores, tops)]
                totals = [jnp.sum(p, 0, keepdims=True) for p in parts]
                outs = [nn(vt_ref[c, pl.ds(k0, w)], (p * (1.0 / t)).astype(BF16)) for c, p, t in zip(cols, parts, totals)]
                for i, (c, o, m, t) in enumerate(zip(cols, outs, tops, totals)):
                    o = jnp.concatenate([o[:HD, :QB], o[HD:, QB:]], 0)
                    o_ref[pl.ds(q0, QB), c] = o.T.astype(BF16)
                    lse_ref[i, pl.ds(qb, 1), :] = m + jnp.log(t)
        return 0

    lax.fori_loop(0, nblocks, block, 0)


def attn_bwd_kernel(nblocks, most, many, lo_ref, segc_ref, padc_ref, segr_ref, q_ref, k_ref, v_ref, do_ref, lse_ref,
                    out_ref, sums_ref, bias_ref, kt_ref, dk_acc, dv_acc):
    @pl.when(pl.program_id(0) == 0)
    def _():
        fill_bias(lo_ref, segc_ref, padc_ref, segr_ref, bias_ref, nblocks, most)

    kt_ref[...] = k_ref[...].T
    dk_acc[...] = jnp.zeros_like(dk_acc)
    dv_acc[...] = jnp.zeros_like(dv_acc)
    sums_ref[...] = jnp.zeros_like(sums_ref)

    def block(qb, _):
        lo = lo_ref[qb]
        q0 = pl.multiple_of(qb * QB, QB)
        k0 = pl.multiple_of(lo * QB, QB)
        for n in range(1, most + 1):
            @pl.when(qb - lo + 1 == n)
            def _(n=n):
                w = n * QB
                bias = bias_ref[qb, 0:w, :]
                bias = jnp.concatenate([bias, bias], 1)
                cols = [slice(128 * i, 128 * (i + 1)) for i in range(many)]
                rows, keys = pl.ds(q0, QB), pl.ds(k0, w)
                q2 = [head_pair(q_ref[rows, c], HD ** -0.5) for c in cols]
                do2 = [head_pair(do_ref[rows, c], 1.0) for c in cols]
                probs = [jnp.exp(nt(k_ref[keys, c], q) + bias - lse_ref[i, pl.ds(qb, 1), :]) for i, (c, q) in enumerate(zip(cols, q2))]
                dprobs = [nt(v_ref[keys, c], do) for c, do in zip(cols, do2)]
                inner = [jnp.sum(p * dp, 0, keepdims=True) for p, dp in zip(probs, dprobs)]
                ds = [(p * (dp - i)).astype(BF16) for p, dp, i in zip(probs, dprobs, inner)]
                for c, p, d, q, do in zip(cols, probs, ds, q2, do2):
                    dv_acc[keys, c] += nn(p.astype(BF16), do)
                    dk_acc[keys, c] += nn(d, q)
                    dq = nn(kt_ref[c, keys], d)
                    dq = jnp.concatenate([dq[:HD, :QB], dq[HD:, QB:]], 0) * (HD ** -0.5)
                    dq = dq.T.astype(BF16)
                    out_ref[0, rows, c] = dq
                    sums_ref[0:1, c] += jnp.sum(dq.astype(F32), 0, keepdims=True)
        return 0

    lax.fori_loop(0, nblocks, block, 0)
    out_ref[1] = dk_acc[...].astype(BF16)
    dv = dv_acc[...].astype(BF16)
    out_ref[2] = dv
    sums_ref[1:2, :] = jnp.sum(dv.astype(F32), 0, keepdims=True)


def mask_inputs(segment_ids, padding_mask):
    length = segment_ids.shape[0]
    nblocks = length // QB
    first = segment_ids.reshape(nblocks, QB)[:, 0]
    start = jnp.sum((segment_ids[None, :] < first[:, None]).astype(jnp.int32), 1)
    lo = start // QB
    segc = jnp.broadcast_to(segment_ids[:, None], (length, QB))
    padc = jnp.broadcast_to(padding_mask[:, None], (length, QB))
    return lo.astype(jnp.int32), segc, padc, segment_ids.reshape(nblocks, QB)


def attn_forward(q, k, v, masks, first=0, pairs=None):
    length, many = q[0].shape[0], MANY
    width = 128 * many
    nblocks = length // QB
    most = min(nblocks, SPAN // QB + 1)
    pairs = pairs or 8
    lo, segc, padc, segr = masks
    (qa, qo), (ka, ko), (va, vo) = q, k, v
    whole = lambda p, lo: (0, 0)
    col = lambda off: pl.BlockSpec((length, width), lambda p, lo: (0, (off + first) // many + p))
    return pl.pallas_call(
        functools.partial(attn_fwd_kernel, nblocks, most, many),
        grid_spec=pltpu.PrefetchScalarGridSpec(
            num_scalar_prefetch=1, grid=(pairs // many,),
            in_specs=[pl.BlockSpec((length, QB), whole), pl.BlockSpec((length, QB), whole), pl.BlockSpec((nblocks, QB), whole),
                      col(qo), col(ko), col(vo)],
            out_specs=[pl.BlockSpec((length, width), lambda p, lo: (0, p)),
                       pl.BlockSpec((many, nblocks, 2 * QB), lambda p, lo: (p, 0, 0))],
            scratch_shapes=[pltpu.VMEM((nblocks, most * QB, QB), F32), pltpu.VMEM((width, length), BF16)]),
        out_shape=[jax.ShapeDtypeStruct((length, pairs * 128), BF16), jax.ShapeDtypeStruct((pairs, nblocks, 2 * QB), F32)],
        compiler_params=pltpu.CompilerParams(vmem_limit_bytes=48 << 20),
        cost_estimate=cost(11),
        name="attn_forward",
    )(lo, segc, padc, segr, qa, ka, va)


def attn_backward(q, k, v, do, lse, masks, first=0, pairs=None):
    length, many = q[0].shape[0], MANY
    width = 128 * many
    nblocks = length // QB
    most = min(nblocks, SPAN // QB + 1)
    pairs = pairs or 8
    lo, segc, padc, segr = masks
    (qa, qo), (ka, ko), (va, vo) = q, k, v
    whole = lambda p, lo: (0, 0)
    col = lambda off: pl.BlockSpec((length, width), lambda p, lo: (0, (off + first) // many + p))
    return pl.pallas_call(
        functools.partial(attn_bwd_kernel, nblocks, most, many),
        grid_spec=pltpu.PrefetchScalarGridSpec(
            num_scalar_prefetch=1, grid=(pairs // many,),
            in_specs=[pl.BlockSpec((length, QB), whole), pl.BlockSpec((length, QB), whole), pl.BlockSpec((nblocks, QB), whole),
                      col(qo), col(ko), col(vo), col(0),
                      pl.BlockSpec((many, nblocks, 2 * QB), lambda p, lo: (first // many + p, 0, 0))],
            out_specs=[pl.BlockSpec((3, length, width), lambda p, lo: (0, 0, p)), pl.BlockSpec((8, width), lambda p, lo: (0, p))],
            scratch_shapes=[pltpu.VMEM((nblocks, most * QB, QB), F32), pltpu.VMEM((width, length), BF16),
                            pltpu.VMEM((length, width), F32), pltpu.VMEM((length, width), F32)]),
        out_shape=[jax.ShapeDtypeStruct((3, length, pairs * 128), BF16), jax.ShapeDtypeStruct((8, pairs * 128), F32)],
        compiler_params=pltpu.CompilerParams(vmem_limit_bytes=48 << 20),
        cost_estimate=cost(16),
        name="attn_backward",
    )(lo, segc, padc, segr, qa, ka, va, do, lse)


ANY = pl.BlockSpec(memory_space=pl.ANY)
META = 1


def params(megabytes=56):
    return pltpu.CompilerParams(vmem_limit_bytes=megabytes << 20)


def tile_shape(native, rows, columns):
    return (1, 1, 1, rows, columns) if native else (4, 4, 2, rows // 32, columns)


def fetch_columns(native, meta, groups, target, start, columns, sem):
    cols = pl.ds(start, columns)
    if native:
        pltpu.make_async_copy(groups[0].at[:, cols], target.at[0, 0, 0], sem).start()
        return
    core = meta[4]
    for t in range(4):
        pltpu.make_async_copy(groups[t].at[:, :, cols], target.at[meta[t], :, core], sem).start()
        pltpu.make_async_copy(groups[4 + t].at[:, :, cols], target.at[meta[t], :, 1 - core], sem).start()


def quarter_shape(native, rows, columns):
    return (1, 1, rows // 4, columns) if native else (4, 2, rows // 32, columns)


def fetch_quarter(native, meta, groups, target, t, sem):
    if native:
        rows = target.shape[-2]
        pltpu.make_async_copy(groups[0].at[pl.ds(t * rows, rows), :], target.at[0, 0], sem).start()
        return
    core = meta[4]
    pltpu.make_async_copy(groups[t], target.at[:, core], sem).start()
    pltpu.make_async_copy(groups[4 + t], target.at[:, 1 - core], sem).start()


def arrive(target, sem):
    pltpu.make_async_copy(target, target, sem).wait()


def group_specs(groups):
    return [ANY] * len(groups)


def flat(value):
    return value.reshape(-1, value.shape[-1])


def out_blocks(native, rows, columns):
    if native:
        return [jax.ShapeDtypeStruct((rows, columns), BF16)]
    return [jax.ShapeDtypeStruct((4, 4, rows // 32, columns), BF16)] * 2


def push_columns(native, meta, stage, outs, start, columns, sem):
    cols = pl.ds(start, columns)
    if native:
        pltpu.make_async_copy(stage.at[0, 0, 0], outs[0].at[:, cols], sem).start()
        return
    core = meta[4]
    for t in range(4):
        pltpu.make_async_copy(stage.at[meta[t], :, core], outs[0].at[t, :, :, cols], sem).start()
        pltpu.make_async_copy(stage.at[meta[t], :, 1 - core], outs[1].at[FLIP[t], :, :, cols], sem).start()


def squares(values, valid):
    return jnp.sum(values * values * valid, 0, keepdims=True)


def scale_of(values):
    return lax.rsqrt(jnp.mean(values * values, -1, keepdims=True) + 1e-05)


def project_kernel(native, tile, meta, tok_ref, gain_ref, valid_ref, bias_ref, *rest):
    groups, (out_ref, normed_ref, sq_ref, weight, sems) = rest[:-5], rest[-5:]
    n, steps = pl.program_id(0), pl.num_programs(0)

    @pl.when(n == 0)
    def _():
        fetch_columns(native, meta, groups, weight.at[0], 0, tile, sems.at[0])

    @pl.when(n + 1 < steps)
    def _():
        slot = (n + 1) % 2
        fetch_columns(native, meta, groups, weight.at[slot], pl.multiple_of((n + 1) * tile, tile), tile, sems.at[slot])

    @pl.when(n == 0)
    def _():
        frames = tok_ref[...].astype(F32)
        sq_ref[...] = squares(frames, valid_ref[...])
        normed_ref[...] = (frames * scale_of(frames) * gain_ref[...]).astype(BF16)

    arrive(weight.at[n % 2], sems.at[n % 2])
    out_ref[...] = (nn(normed_ref[...], flat(weight[n % 2])) + bias_ref[...]).astype(BF16)


def project(ladder, tokens, gain, valid, bias, groups):
    length, width = tokens.shape
    columns, tile = bias.shape[1], 512
    whole = lambda n, meta: (0, 0)
    return pl.pallas_call(
        functools.partial(project_kernel, ladder.native, tile),
        grid_spec=pltpu.PrefetchScalarGridSpec(
            num_scalar_prefetch=1, grid=(columns // tile,),
            in_specs=[pl.BlockSpec((length, width), whole), pl.BlockSpec((1, width), whole), pl.BlockSpec((length, 1), whole),
                      pl.BlockSpec((1, tile), lambda n, meta: (0, n))] + group_specs(groups),
            out_specs=[pl.BlockSpec((length, tile), lambda n, meta: (0, n)), pl.BlockSpec((length, width), whole),
                       pl.BlockSpec((1, width), whole)],
            scratch_shapes=[pltpu.VMEM((2,) + tile_shape(ladder.native, width, tile), BF16), pltpu.SemaphoreType.DMA((2,))]),
        out_shape=[jax.ShapeDtypeStruct((length, columns), BF16), jax.ShapeDtypeStruct((length, width), BF16),
                   jax.ShapeDtypeStruct((1, width), F32)],
        compiler_params=params(),
        cost_estimate=cost(14),
        name="project",
    )(ladder.meta, tokens, gain, valid, bias, *groups)


def gelu_pair(u):
    c, d = 0.7978845608028654, 0.044715
    square = u * u
    bend = 0.5 * jnp.tanh(u * (c + c * d * square))
    half = 0.5 + bend
    slope = half * (1.0 + (0.5 - bend) * (u * (2.0 * c + 6.0 * c * d * square)))
    return (u * half).astype(BF16), slope.astype(BF16)


def expand_kernel(native, tile, count, meta, mixed_ref, tok_ref, bias_ref, gain_ref, valid_ref, up_bias_ref, *rest):
    groups, rest = rest[:count], rest[count:]
    middle_ref, normed_ref, sq_ref, act_ref, slope_ref, middle, out_weight, weight, sems = rest
    n, steps = pl.program_id(0), pl.num_programs(0)
    half = out_weight.shape[-1]
    first = 2 * half
    store = pltpu.make_async_copy(middle, middle_ref, sems.at[4])

    @pl.when(n == 0)
    def _():
        for side in range(2):
            fetch_columns(native, meta, groups, out_weight.at[side], side * half, half, sems.at[2 + side])
        fetch_columns(native, meta, groups, weight.at[0], first, tile, sems.at[0])

    @pl.when(n + 1 < steps)
    def _():
        slot = (n + 1) % 2
        fetch_columns(native, meta, groups, weight.at[slot], pl.multiple_of(first + (n + 1) * tile, tile), tile, sems.at[slot])

    @pl.when(n == 0)
    def _():
        for side in range(2):
            arrive(out_weight.at[side], sems.at[2 + side])
        sq_ref[...] = jnp.zeros_like(sq_ref)
        rows = 256

        def part(i, _):
            at = pl.ds(pl.multiple_of(i * rows, rows), rows)
            branch = jnp.concatenate([nn(mixed_ref[at, :], flat(out_weight[side])) for side in range(2)], 1) + bias_ref[...]
            total = tok_ref[at, :].astype(F32) + branch
            middle[at, :] = total
            normed_ref[at, :] = (total * scale_of(total) * gain_ref[...]).astype(BF16)
            sq_ref[0:1, :] += squares(branch, valid_ref[at, :])
            sq_ref[1:2, :] += squares(total, valid_ref[at, :])
            return 0

        lax.fori_loop(0, middle.shape[0] // rows, part, 0)
        store.start()

    arrive(weight.at[n % 2], sems.at[n % 2])
    act_ref[...], slope_ref[...] = gelu_pair(nn(normed_ref[...], flat(weight[n % 2])) + up_bias_ref[...])

    @pl.when(n == steps - 1)
    def _():
        store.wait()


def expand(ladder, mixed, tokens, bias, gain, valid, up_bias, groups):
    length, width = tokens.shape
    columns, tile = up_bias.shape[1], 512
    whole = lambda n, meta: (0, 0)
    column = lambda n, meta: (0, n)
    square, line = pl.BlockSpec((length, width), whole), pl.BlockSpec((1, width), whole)
    return pl.pallas_call(
        functools.partial(expand_kernel, ladder.native, tile, len(groups)),
        grid_spec=pltpu.PrefetchScalarGridSpec(
            num_scalar_prefetch=1, grid=(columns // tile,),
            in_specs=[square, square, line, line, pl.BlockSpec((length, 1), whole), pl.BlockSpec((1, tile), column)]
            + group_specs(groups),
            out_specs=[ANY, square, pl.BlockSpec((8, width), whole), pl.BlockSpec((length, tile), column),
                       pl.BlockSpec((length, tile), column)],
            scratch_shapes=[pltpu.VMEM((length, width), F32),
                            pltpu.VMEM((2,) + tile_shape(ladder.native, width, width // 2), BF16),
                            pltpu.VMEM((2,) + tile_shape(ladder.native, width, tile), BF16), pltpu.SemaphoreType.DMA((5,))]),
        out_shape=[jax.ShapeDtypeStruct((length, width), F32), jax.ShapeDtypeStruct((length, width), BF16),
                   jax.ShapeDtypeStruct((8, width), F32)] + [jax.ShapeDtypeStruct((length, columns), BF16)] * 2,
        compiler_params=params(),
        cost_estimate=cost(29),
        name="expand",
    )(ladder.meta, mixed, tokens, bias, gain, valid, up_bias, *groups)


def fetch_turn(native, meta, groups, weight, sems, t, first=0, last=3):
    for at in range(first, last + 1):
        @pl.when(t == max(at - 1, first))
        def _(at=at):
            fetch_quarter(native, meta, groups, weight.at[at % 2], at, sems.at[at % 2])

    arrive(weight.at[t % 2], sems.at[t % 2])


def tn(a, b):
    return lax.dot_general(a, b, (((0,), (0,)), ((), ())), preferred_element_type=F32)


def down_grad_kernel(native, count, meta, act_ref, cot_ref, *rest):
    outs, (sum_ref, stage, sems) = rest[:count], rest[count:]
    t = pl.program_id(0)
    slot = t % 2

    @pl.when(t >= 2)
    def _():
        arrive(stage.at[slot], sems.at[slot])

    stage[slot] = tn(act_ref[...], cot_ref[...]).astype(BF16).reshape(stage.shape[1:])
    if native:
        rows = stage.shape[-2]
        pltpu.make_async_copy(stage.at[slot, 0, 0], outs[0].at[pl.ds(t * rows, rows), :], sems.at[slot]).start()
    else:
        for k in range(4):
            @pl.when(t == k)
            def _(k=k):
                pltpu.make_async_copy(stage.at[slot, :, meta[4]], outs[0].at[k], sems.at[slot]).start()
                pltpu.make_async_copy(stage.at[slot, :, 1 - meta[4]], outs[1].at[FLIP[k]], sems.at[slot]).start()

    @pl.when(t == 0)
    def _():
        sum_ref[...] = jnp.sum(cot_ref[...].astype(F32), 0, keepdims=True)

    @pl.when(t == 3)
    def _():
        arrive(stage.at[1 - slot], sems.at[1 - slot])
        arrive(stage.at[slot], sems.at[slot])


def down_grad(ladder, act, cot):
    length, width = cot.shape
    hidden = act.shape[1]
    outs = out_blocks(ladder.native, hidden, width)
    whole = lambda t, meta: (0, 0)
    return pl.pallas_call(
        functools.partial(down_grad_kernel, ladder.native, len(outs)),
        grid_spec=pltpu.PrefetchScalarGridSpec(
            num_scalar_prefetch=1, grid=(4,),
            in_specs=[pl.BlockSpec((length, hidden // 4), lambda t, meta: (0, meta[t])), pl.BlockSpec((length, width), whole)],
            out_specs=[ANY] * len(outs) + [pl.BlockSpec((1, width), whole)],
            scratch_shapes=[pltpu.VMEM((2,) + quarter_shape(ladder.native, hidden, width), BF16), pltpu.SemaphoreType.DMA((2,))]),
        out_shape=outs + [jax.ShapeDtypeStruct((1, width), F32)],
        compiler_params=params(),
        cost_estimate=cost(14),
        name="down_grad",
    )(ladder.meta, act, cot)


def row_grad_kernel(native, tile, count, meta, left_ref, right_ref, *rest):
    outs, (stage, sems) = rest[:count], rest[count:]
    n, steps = pl.program_id(0), pl.num_programs(0)
    slot = n % 2

    @pl.when(n >= 2)
    def _():
        arrive(stage.at[slot], sems.at[slot])

    stage[slot] = tn(left_ref[...], right_ref[...]).astype(BF16).reshape(stage.shape[1:])
    push_columns(native, meta, stage.at[slot], outs, pl.multiple_of(n * tile, tile), tile, sems.at[slot])

    @pl.when(n == steps - 1)
    def _():
        arrive(stage.at[1 - slot], sems.at[1 - slot])
        arrive(stage.at[slot], sems.at[slot])


def row_grad(ladder, left, right, name):
    length, width = left.shape
    parts, _, each = right.shape
    tile = 512
    per = each // tile
    outs = out_blocks(ladder.native, width, parts * each)
    return pl.pallas_call(
        functools.partial(row_grad_kernel, ladder.native, tile, len(outs)),
        grid_spec=pltpu.PrefetchScalarGridSpec(
            num_scalar_prefetch=1, grid=(parts * per,),
            in_specs=[pl.BlockSpec((length, width), lambda n, meta: (0, 0)),
                      pl.BlockSpec((None, length, tile), lambda n, meta: (n // per, 0, n % per))],
            out_specs=[ANY] * len(outs),
            scratch_shapes=[pltpu.VMEM((2,) + tile_shape(ladder.native, width, tile), BF16), pltpu.SemaphoreType.DMA((2,))]),
        out_shape=outs,
        compiler_params=params(),
        cost_estimate=cost(8),
        name=name,
    )(ladder.meta, left, right)


def norm_grad(grad, source, gain):
    r = scale_of(source)
    hat = source * r
    gain_grad = jnp.sum(grad * hat, 0, keepdims=True)
    scaled = grad * gain
    return r * (scaled - hat * jnp.mean(scaled * hat, -1, keepdims=True)), gain_grad


def back_kernel(native, last, counts, meta, cot_ref, slope_ref, normed_ref, gain_ref, middle_ref, mixed_ref, *rest):
    down_groups, rest = rest[: counts[0]], rest[counts[0] :]
    groups, rest = rest[: counts[0]], rest[counts[0] :]
    if last:
        before, rest = rest[0], rest[1 + counts[1] :]
    pushed, rest = rest[: counts[1]], rest[counts[1] :]
    if last:
        out_ref, branch_ref, mixed_out_ref, sum_ref, up_sum_ref, rest = *rest[:5], rest[5:]
        acc, down_weight, weight, stage, sems, middle, out_weight, out_stage = rest
    else:
        after, up_sum_ref, acc, down_weight, weight, stage, sems = rest
    base = 2 if last else 0
    step = pl.program_id(0)
    t = step + base
    width, tile = normed_ref.shape[1], slope_ref.shape[1]
    slot = step

    def columns(at):
        return pl.multiple_of(width + meta[at] * tile, 512)

    @pl.when(step == 0)
    def _():
        for at in range(2):
            fetch_columns(native, meta, groups, weight.at[at], columns(base + at), tile, sems.at[2 + at])
        if last:
            pltpu.make_async_copy(before, acc, sems.at[6]).start()
            pltpu.make_async_copy(middle_ref, middle, sems.at[7]).start()
            fetch_columns(native, meta, groups, out_weight, 0, width, sems.at[8])

    fetch_turn(native, meta, down_groups, down_weight, sems, t, base, base + 1)
    grad = (nt(cot_ref[...], flat(down_weight[t % 2])) * slope_ref[...].astype(F32)).astype(BF16)
    up_sum_ref[...] = jnp.sum(grad.astype(F32), 0, keepdims=True)
    stage[slot] = tn(normed_ref[...], grad).astype(BF16).reshape(stage.shape[1:])
    push_columns(native, meta, stage.at[slot], pushed, columns(t), tile, sems.at[4 + slot])
    arrive(weight.at[slot], sems.at[2 + slot])
    product = nt(grad, flat(weight[slot]))

    @pl.when(step == 0)
    def _():
        if last:
            pltpu.make_async_copy(before, acc, sems.at[6]).wait()
            acc[...] += product
        else:
            acc[...] = product

    @pl.when(step == 1)
    def _():
        acc[...] += product
        if last:
            pltpu.make_async_copy(middle_ref, middle, sems.at[7]).wait()
            sum_ref[...] = jnp.zeros_like(sum_ref)
            rows = 256

            def part(i, _):
                at = pl.ds(pl.multiple_of(i * rows, rows), rows)
                back, gain_grad = norm_grad(acc[at, :], middle[at, :], gain_ref[...])
                total = cot_ref[at, :].astype(F32) + back
                acc[at, :] = total
                branch = total.astype(BF16)
                branch_ref[at, :] = branch
                sum_ref[0:1, :] += gain_grad
                sum_ref[1:2, :] += jnp.sum(branch.astype(F32), 0, keepdims=True)
                return 0

            lax.fori_loop(0, acc.shape[0] // rows, part, 0)
            pltpu.make_async_copy(acc, out_ref, sems.at[6]).start()
            out_stage[...] = tn(mixed_ref[...], branch_ref[...]).astype(BF16).reshape(out_stage.shape)
            push_columns(native, meta, out_stage, pushed, 0, width, sems.at[7])
            arrive(out_weight, sems.at[8])
            mixed_out_ref[...] = nt(branch_ref[...], flat(out_weight[...])).astype(BF16)
            arrive(out_stage, sems.at[7])
            pltpu.make_async_copy(acc, out_ref, sems.at[6]).wait()
        else:
            pltpu.make_async_copy(acc, after, sems.at[6]).start()
            pltpu.make_async_copy(acc, after, sems.at[6]).wait()
        for at in range(2):
            arrive(stage.at[at], sems.at[4 + at])


def back(ladder, cot, slope, normed, gain, middle, mixed, down_groups, groups, before=None):
    length, width = cot.shape
    hidden, tile = slope.shape[1], slope.shape[1] // 4
    last = before is not None
    base = 2 if last else 0
    whole = lambda t, meta: (0, 0)
    part = lambda t, meta: (0, meta[t + base])
    square = pl.BlockSpec((length, width), whole)
    once = pl.BlockSpec((length, width), whole, pipeline_mode=pl.Buffered(1))
    outs = out_blocks(ladder.native, width, hidden + width)
    counts = (len(groups), len(outs))
    full, wide = jax.ShapeDtypeStruct((length, width), F32), jax.ShapeDtypeStruct((length, width), BF16)
    sums = jax.ShapeDtypeStruct((1, hidden), F32)
    in_specs = [once, pl.BlockSpec((length, tile), part), once, pl.BlockSpec((1, width), whole), ANY, once if last else ANY]
    in_specs += [ANY] * (2 * counts[0])
    operands = [ladder.meta, cot, slope, normed, gain, middle, mixed, *down_groups, *groups]
    scratch = [pltpu.VMEM((length, width), F32), pltpu.VMEM((2,) + quarter_shape(ladder.native, hidden, width), BF16),
               pltpu.VMEM((2,) + tile_shape(ladder.native, width, tile), BF16),
               pltpu.VMEM((2,) + tile_shape(ladder.native, width, tile), BF16), pltpu.SemaphoreType.DMA((9,))]
    aliases = {}
    if last:
        aliases = {len(operands) + 1 + i: i for i in range(counts[1])}
        operands += list(before)
        in_specs += [ANY] * (1 + counts[1])
        out_specs = [ANY] * counts[1] + [ANY, square, square, pl.BlockSpec((8, width), whole)]
        out_shape = outs + [full, wide, wide, jax.ShapeDtypeStruct((8, width), F32)]
        scratch += [pltpu.VMEM((length, width), F32), pltpu.VMEM(tile_shape(ladder.native, width, width), BF16),
                    pltpu.VMEM(tile_shape(ladder.native, width, width), BF16)]
    else:
        out_specs, out_shape = [ANY] * counts[1] + [ANY], outs + [full]
    return pl.pallas_call(
        functools.partial(back_kernel, ladder.native, last, counts),
        grid_spec=pltpu.PrefetchScalarGridSpec(
            num_scalar_prefetch=1, grid=(2,), in_specs=in_specs, out_specs=out_specs + [pl.BlockSpec((1, tile), lambda t, meta: (0, t))],
            scratch_shapes=scratch),
        out_shape=out_shape + [jax.ShapeDtypeStruct((1, hidden // 2), F32)],
        input_output_aliases=aliases,
        compiler_params=params(),
        cost_estimate=cost(30 if last else 20),
        name="back",
    )(*operands)


def contract_kernel(native, meta, act_ref, bias_ref, valid_ref, middle_ref, *rest):
    groups, (out_ref, sq_ref, acc, middle, weight, sems) = rest[:-6], rest[-6:]
    t = pl.program_id(0)
    load = pltpu.make_async_copy(middle_ref, middle, sems.at[2])

    @pl.when(t == 0)
    def _():
        load.start()

    fetch_turn(native, meta, groups, weight, sems, t)
    product = nn(act_ref[...], flat(weight[t % 2]))

    @pl.when(t == 0)
    def _():
        acc[...] = product

    @pl.when(t > 0)
    def _():
        acc[...] += product

    @pl.when(t == 3)
    def _():
        load.wait()
        sq_ref[...] = jnp.zeros_like(sq_ref)
        rows = 256

        def part(i, _):
            at = pl.ds(pl.multiple_of(i * rows, rows), rows)
            branch = acc[at, :] + bias_ref[...]
            final = middle[at, :] + branch
            out_ref[at, :] = final.astype(BF16)
            sq_ref[0:1, :] += squares(branch, valid_ref[at, :])
            sq_ref[1:2, :] += squares(final, valid_ref[at, :])
            return 0

        lax.fori_loop(0, acc.shape[0] // rows, part, 0)


def contract(ladder, act, middle, bias, valid, groups):
    length, width = middle.shape
    hidden = act.shape[1]
    whole = lambda t, meta: (0, 0)
    return pl.pallas_call(
        functools.partial(contract_kernel, ladder.native),
        grid_spec=pltpu.PrefetchScalarGridSpec(
            num_scalar_prefetch=1, grid=(4,),
            in_specs=[pl.BlockSpec((length, hidden // 4), lambda t, meta: (0, meta[t])), pl.BlockSpec((1, width), whole),
                      pl.BlockSpec((length, 1), whole), ANY] + group_specs(groups),
            out_specs=[pl.BlockSpec((length, width), whole), pl.BlockSpec((8, width), whole)],
            scratch_shapes=[pltpu.VMEM((length, width), F32), pltpu.VMEM((length, width), F32),
                            pltpu.VMEM((2,) + quarter_shape(ladder.native, hidden, width), BF16), pltpu.SemaphoreType.DMA((3,))]),
        out_shape=[jax.ShapeDtypeStruct((length, width), BF16), jax.ShapeDtypeStruct((8, width), F32)],
        compiler_params=params(),
        cost_estimate=cost(16),
        name="contract",
    )(ladder.meta, act, bias, valid, middle, *groups)


def input_grad_kernel(native, calls, meta, *rest):
    grads, (tok_ref, middle_ref, gain_ref), rest = rest[:calls], rest[calls : calls + 3], rest[calls + 3 :]
    groups, (out_ref, sum_ref, acc, middle, weight, sems) = rest[:-6], rest[-6:]
    t = pl.program_id(0)
    load = pltpu.make_async_copy(middle_ref, middle, sems.at[2])

    @pl.when(t == 0)
    def _():
        load.start()

    fetch_turn(native, meta, groups, weight, sems, t)
    width = acc.shape[1]
    quarter = width // 4
    rows = flat(weight[t % 2])
    each = width // calls
    product = 0.0
    for part in range(3):
        for call in range(calls):
            first = part * width + call * each
            product += nt(grads[call][part], rows[:, first : first + each])
    acc[:, pl.ds(pl.multiple_of(meta[t] * quarter, quarter), quarter)] = product

    @pl.when(t == 3)
    def _():
        load.wait()
        sum_ref[...] = jnp.zeros_like(sum_ref)
        rows = 256

        def part(i, _):
            at = pl.ds(pl.multiple_of(i * rows, rows), rows)
            back, gain_grad = norm_grad(acc[at, :], tok_ref[at, :].astype(F32), gain_ref[...])
            out_ref[at, :] = (middle[at, :] + back).astype(BF16)
            sum_ref[0:1, :] += gain_grad
            return 0

        lax.fori_loop(0, acc.shape[0] // rows, part, 0)


def input_grad(ladder, grads, tokens, grad_middle, gain, groups):
    length, width = tokens.shape
    calls = len(grads)
    whole = lambda t, meta: (0, 0)
    square = pl.BlockSpec((length, width), whole)
    return pl.pallas_call(
        functools.partial(input_grad_kernel, ladder.native, calls),
        grid_spec=pltpu.PrefetchScalarGridSpec(
            num_scalar_prefetch=1, grid=(4,),
            in_specs=[pl.BlockSpec((3, length, width // calls), lambda t, meta: (0, 0, 0))] * calls + [square, ANY, pl.BlockSpec((1, width), whole)]
            + group_specs(groups),
            out_specs=[square, pl.BlockSpec((8, width), whole)],
            scratch_shapes=[pltpu.VMEM((length, width), F32), pltpu.VMEM((length, width), F32),
                            pltpu.VMEM((2,) + quarter_shape(ladder.native, width, 3 * width), BF16), pltpu.SemaphoreType.DMA((3,))]),
        out_shape=[jax.ShapeDtypeStruct((length, width), BF16), jax.ShapeDtypeStruct((8, width), F32)],
        compiler_params=params(),
        cost_estimate=cost(18),
        name="input_grad",
    )(ladder.meta, *grads, tokens, grad_middle, gain, *groups)


def local(ladder, tokens, cotangent, segment_ids, padding_mask, w_qkv, bias_qv, w_out, bias_out, gain_attn, gain_mlp,
          w_up, bias_up, w_down, bias_down):
    length, width = tokens.shape[1], tokens.shape[2]
    count = ladder.count
    ladder.place()
    tokens, cotangent = tokens[0], cotangent[0]

    def sent(*flows):
        return [value for flow in flows for value in flow.sent]

    out_up = jnp.concatenate([w_out, w_up], 1)
    qkv = Gather(ladder, w_qkv, True)
    rest, down = Gather(ladder, out_up, False), Gather(ladder, w_down, False)
    qkv.start()
    smalls = [bias_qv, bias_out, gain_attn, gain_mlp, bias_up, bias_down]
    sizes = [s.shape[0] for s in smalls]
    total = sum(sizes)
    ends = np.cumsum([0] + sizes)
    packed = jnp.pad(jnp.concatenate(smalls), (0, -total % 128))
    vectors = ladder.gather_small(packed).astype(F32)
    qv_bias, out_bias, attn_gain, mlp_gain, up_bias, down_bias = [
        vectors[:, ends[i] : ends[i + 1]].reshape(1, -1) for i in range(6)
    ]
    offset = jnp.concatenate([qv_bias[:, :width], jnp.zeros((1, width), F32), qv_bias[:, width:]], 1)
    masks = mask_inputs(segment_ids[0], padding_mask[0])
    valid = padding_mask[0].astype(F32)[:, None]
    qkv.plane(vectors)
    rest.start(*qkv.sent)
    qkv.corner()
    rest.low(*qkv.sent)
    qkv_groups = qkv.finish()
    rest.plane(*qkv.sent)
    projected, normed_in, sq_frames = project(ladder, tie(tokens, *sent(rest)), attn_gain, valid, offset, qkv_groups)
    down.start(projected)
    per = width // 128
    calls = 2
    each = per // calls

    def triple():
        return (projected, 0), (projected, per), (projected, 2 * per)

    mixed_parts, lse_parts = [], []
    for call in range(calls):
        mixed_part, lse_part = attn_forward(*triple(), masks, call * each, each)
        mixed_parts.append(mixed_part)
        lse_parts.append(lse_part)
        if call == 0:
            rest.corner(mixed_part)
            down.low(mixed_part)
            projected = tie(projected, mixed_part, *sent(rest, down))
    down.plane(mixed_parts[-1])
    rest_groups = rest.finish(mixed_parts[-1])
    mixed = jnp.concatenate(mixed_parts, 1)
    lse = jnp.concatenate(lse_parts, 0)
    middle, normed_mid, sq_middle, act, slope = expand(
        ladder, tie(mixed, *sent(down)), tokens, out_bias, mlp_gain, valid, up_bias, rest_groups)

    down.corner(act)
    *down_parts, sum_down = down_grad(ladder, tie(act, *sent(down)), cotangent)
    flow_down = Scatter(ladder, down_parts)
    down_groups = down.finish(sum_down)
    *first_parts, first_acc, first_sum = back(
        ladder, tie(cotangent, sum_down), slope, normed_mid, mlp_gain, middle, mixed, down_groups, rest_groups)
    flow_down.corner(first_acc)
    *rest_parts, grad_middle, grad_branch, grad_mixed, sum_middle, second_sum = back(
        ladder, tie(cotangent, *sent(flow_down)), slope, normed_mid, mlp_gain, middle, mixed, down_groups, rest_groups,
        [first_acc, *first_parts])
    sum_up = jnp.concatenate([first_sum, second_sum], 1).reshape(4, -1)[ladder.order].reshape(1, -1)
    flow_rest = Scatter(ladder, rest_parts)
    flow_down.plane(grad_mixed)
    grad_mixed = tie(grad_mixed, *sent(flow_down))
    grad_parts, sums, flow_qkv = [], [], []
    for call in range(calls):
        part, sum_part = attn_backward(*triple(), grad_mixed, lse, masks, call * each, each)
        if call == 0:
            flow_down.spread(part)
            flow_rest.corner(part)
            part = tie(part, *sent(flow_down, flow_rest))
        else:
            own_down = flow_down.finish(part)
            flow_rest.plane(part)
            flow_qkv[0].corner(part)
            part = tie(part, *sent(flow_down, flow_rest, flow_qkv[0]))
        grad_parts.append(part)
        sums.append(sum_part)
        flow_qkv.append(Scatter(ladder, row_grad(ladder, normed_in, part, "qkv_grad")))
        if call == 0:
            grad_mixed = tie(grad_mixed, *flow_qkv[0].parts)
    sum_qv = jnp.concatenate(sums, 1)
    tail = tie(tokens, *flow_qkv[1].parts)
    grad_tokens, sum_in = input_grad(ladder, grad_parts, tail, grad_middle, attn_gain, qkv_groups)
    flow_rest.spread(grad_tokens)
    flow_qkv[0].plane(grad_tokens)
    flow_qkv[1].corner(grad_tokens)
    act_last = tie(act, grad_tokens, *sent(flow_rest, *flow_qkv))
    output, sq_final = contract(ladder, act_last, middle, down_bias, valid, down_groups)
    own_rest = flow_rest.finish(output)
    flow_qkv[0].spread(output)
    flow_qkv[1].plane(output)
    members = [sq_frames[0], sq_middle[1], sq_final[1], sq_middle[0], sq_final[0]]
    members = jnp.stack([jnp.sum(member) for member in members] + [jnp.sum(valid)])
    small_grads = [sum_qv[:2].reshape(-1), sum_middle[1], sum_in[0], sum_middle[0], sum_up[0], sum_down[0]]
    table = jnp.concatenate([g.reshape(count, -1) for g in small_grads] + [jnp.broadcast_to(members, (count, 6))], 1)
    table = jnp.pad(table, ((0, 0), (0, -table.shape[1] % 128)))
    own_small = ladder.scatter_small(tie(table, *sent(*flow_qkv)))
    flow_qkv[1].spread()
    owns = [flow.finish().reshape(-1, 3, width // calls) for flow in flow_qkv]
    own_qkv = jnp.concatenate(owns, 2).reshape(-1, 3 * width)

    owned = [own_small[ends[i] : ends[i + 1]] for i in range(6)]
    totals = own_small[total : total + 6]
    stats = jnp.sqrt(totals[:5] / (totals[5] * width))
    own_out, own_up = own_rest[:, :width], own_rest[:, width:]
    return (output[None], grad_tokens[None], own_qkv, owned[0], own_out, owned[1], owned[2], owned[3], own_up, owned[4],
            own_down, owned[5], stats, totals[5:6])


def solution(mesh):
    rows, wide, flat = P(("dp", "fsdp"), None, None), P(("dp", "fsdp"), None), P(("dp", "fsdp"))
    return jax.shard_map(
        functools.partial(local, Ladder(mesh)),
        mesh=mesh,
        in_specs=(rows, rows, wide, wide, wide, flat, wide, flat, flat, flat, wide, flat, wide, flat),
        out_specs=(rows, rows, wide, flat, wide, flat, flat, flat, wide, flat, wide, flat, P(), P()),
        check_vma=False,
    )
```

```python
import functools

import jax
import jax.numpy as jnp
import numpy as np
from jax import lax
from jax.experimental import pallas as pl
from jax.experimental.pallas import tpu as pltpu
from jax.sharding import PartitionSpec as P

HD = 64
QB = 128
SPAN = 512
MANY = 4
WEIGH = 2
F32 = jnp.float32
BF16 = jnp.bfloat16

CORE = 1
Z_HOPS = (2, 4, 6)
MIX = ((0, 1, 2, 3), (0, 2, 1, 3))
FLIP = (0, 2, 1, 3)
HOPS = ((4, 2, 8, 16), (4, 2, 16, 8))


def tie(value, *others):
    return lax.optimization_barrier((value,) + others)[0]


def add_up(*terms):
    return sum(term.astype(F32) for term in terms)


def cost(microseconds):
    return pl.CostEstimate(flops=int(WEIGH * microseconds * 1.15e9), transcendentals=0, bytes_accessed=0)


class Ladder:
    def __init__(self, mesh):
        self.count = int(np.prod(list(mesh.shape.values())))
        self.native = dict(mesh.shape) != {"dp": 4, "fsdp": 8}
        self.axes = ("dp", "fsdp")
        if not self.native:
            keys = []
            for core in (0, 1):
                both = []
                for which, extra in ((core, 0), (1 - core, CORE)):
                    own = [extra]
                    for bit in HOPS[which]:
                        own = own + [key ^ bit for key in own]
                    both += own
                keys.append(both)
            self.keys = np.array(keys, np.int32)

    def place(self):
        if self.native:
            self.meta = jnp.array([0, 1, 2, 3, 0, 0], jnp.int32)
            self.order = jnp.arange(4)
            self.tables = ()
            return
        me = lax.axis_index(self.axes)
        odd = (me & CORE) == 1
        mix = jnp.where(odd, jnp.array(MIX[1], jnp.int32), jnp.array(MIX[0], jnp.int32))
        self.meta = jnp.concatenate([(me >> 3) ^ mix, (me & CORE)[None], ((me >> 1) & 3)[None]])
        self.order = mix[jnp.arange(4) ^ (me >> 3)]
        self.shard_of = me ^ jnp.where(odd, self.keys[1], self.keys[0])
        self.tables = (self.order, self.shard_of)

    def flip(self, value, even, odd):
        bits = (even, odd)
        return lax.ppermute(value, self.axes, [(i, i ^ bits[i & CORE]) for i in range(self.count)])

    def step(self, value, level):
        return self.flip(value, HOPS[0][level], HOPS[1][level])

    def across(self, value):
        return self.flip(value, CORE, CORE)

    def scatter_small(self, table):
        if self.native:
            own = lax.psum_scatter(table, self.axes, scatter_dimension=0, tiled=True).reshape(-1)
            return own, own
        half = self.count // 2
        table = jnp.take(table, self.shard_of, axis=0)
        total = table[:half] + self.across(table[half:])
        for level in (3, 2, 1, 0):
            half, before = half // 2, total
            total = total[:half] + self.step(total[half:], level)
        return total[0], before


def place_kernel(meta, *refs):
    pieces, out_ref = refs[:4], refs[4]
    for k in range(4):
        out_ref[meta[5] ^ k] = pieces[k][...]


def place_group(meta, pieces):
    rows, columns = pieces[0].shape
    tile = columns
    return pl.pallas_call(
        place_kernel,
        grid_spec=pltpu.PrefetchScalarGridSpec(
            num_scalar_prefetch=1, grid=(1,), in_specs=[pl.BlockSpec((rows, tile), lambda n, meta: (0, n))] * 4,
            out_specs=pl.BlockSpec((4, rows, tile), lambda n, meta: (0, 0, n))),
        out_shape=jax.ShapeDtypeStruct((4, rows, columns), pieces[0].dtype),
        cost_estimate=cost(2),
        name="place_group",
    )(meta, *pieces)


def spread_kernel(meta, *refs):
    parts, outs = refs[:16], refs[16:]
    for k in range(4):
        total = sum(part[...].astype(F32) for part in parts[4 * k : 4 * k + 4])
        outs[k][...] = total.astype(outs[k].dtype)


def spread_sums(meta, keep, near, third, second):
    _, rows, columns = second.shape
    tile = columns // 2 if columns > 1024 else columns
    if rows > 32:
        tile = columns // 4
    specs, operands = [], []
    for k in range(4):
        group = pl.BlockSpec((None, rows, tile), lambda n, meta, k=k: (meta[5] ^ k, 0, n))
        pair = pl.BlockSpec((None, None, rows, tile), lambda n, meta, k=k: (0, meta[5] ^ k, 0, n))
        specs += [pair, pair, pair, group]
        operands += [keep, near, third, second]
    out = pl.BlockSpec((rows, tile), lambda n, meta: (0, n))
    return pl.pallas_call(
        spread_kernel,
        grid_spec=pltpu.PrefetchScalarGridSpec(num_scalar_prefetch=1, grid=(columns // tile,), in_specs=specs, out_specs=[out] * 4),
        out_shape=[jax.ShapeDtypeStruct((rows, columns), F32)] + [jax.ShapeDtypeStruct((rows, columns), BF16)] * 3,
        cost_estimate=cost(3),
        name="spread_sums",
    )(meta, *operands)


class Gather:
    def __init__(self, ladder, shard, direct):
        self.ladder, self.shard, self.native, self.direct = ladder, shard, ladder.native, direct
        self.sent, self.others = (), []

    def start(self, *after):
        if not self.native:
            self.shard = tie(self.shard, *after)
            self.sent = (self.shard,)
            bits = Z_HOPS if self.direct else Z_HOPS[1:2]
            self.others = [self.ladder.flip(self.shard, bit, bit) for bit in bits]

    def low(self, *after):
        if not self.native:
            one, two = tie(self.others[0], *after), self.shard
            high = (self.ladder.meta[5] >> 1) == 1
            self.pair = jnp.where(high, jnp.stack([one, two]), jnp.stack([two, one]))
            self.sent = (self.pair,)
            self.others = [self.ladder.flip(self.pair, Z_HOPS[0], Z_HOPS[0])]

    def plane(self, *after):
        if not self.native:
            others = [tie(other, *after) for other in self.others]
            if self.direct:
                self.own = place_group(self.ladder.meta, [self.shard] + others)
            else:
                one, two = others[0], self.pair
                low = (self.ladder.meta[5] & 1) == 1
                own = jnp.where(low, jnp.stack([one, two], 1), jnp.stack([two, one], 1))
                self.own = own.reshape((4,) + self.shard.shape)
            self.sent = (self.own,)
            self.second = self.ladder.step(self.own, 2)
            self.third = self.ladder.step(self.own, 3)
            self.far = [self.ladder.across(self.own)]

    def corner(self, *after):
        if not self.native:
            self.second, self.third = tie(self.second, *after), tie(self.third, *after)
            self.sent = (self.second, self.third)
            self.fourth = self.ladder.step(self.second, 3)
            self.far += [self.ladder.across(self.third), self.ladder.across(self.second)]

    def finish(self, *after):
        if self.native:
            self.groups = [lax.all_gather(self.shard, self.ladder.axes, axis=0, tiled=True)]
        else:
            self.fourth = tie(self.fourth, *after)
            self.sent = (self.fourth,)
            self.far += [self.ladder.across(self.fourth)]
            self.groups = [self.own, self.second, self.third, self.fourth] + self.far
        return self.groups


class Scatter:
    def __init__(self, ladder, parts):
        self.ladder, self.native, self.parts = ladder, ladder.native, parts
        self.sent = ()
        if not self.native:
            self.keep = parts[0]
            self.near = ladder.across(parts[1])

    def corner(self, *after):
        if not self.native:
            self.near = tie(self.near, *after)
            total = add_up(self.keep[2:], self.near[2:]).astype(BF16)
            self.sent = (total,)
            self.third = self.ladder.step(total, 3)

    def plane(self, *after):
        if not self.native:
            self.third = tie(self.third, *after)
            total = add_up(self.keep[1], self.near[1], self.third[1]).astype(BF16)
            self.sent = (total,)
            self.second = self.ladder.step(total, 2)

    def spread(self, *after):
        if not self.native:
            second = tie(self.second, *after)
            self.mine, *away = spread_sums(self.ladder.meta, self.keep, self.near, self.third, second)
            self.sent = tuple(away)
            self.last = [self.ladder.flip(part, bit, bit) for part, bit in zip(away, Z_HOPS)]

    def finish(self, *after):
        if self.native:
            return lax.psum_scatter(self.parts[0].astype(F32), self.ladder.axes, scatter_dimension=0, tiled=True)
        total = add_up(self.mine, *[tie(part, *after) for part in self.last])
        self.sent = (total,)
        return total


def nt(a, b):
    return lax.dot_general(a, b, (((1,), (1,)), ((), ())), preferred_element_type=F32)


def nn(a, b):
    return lax.dot_general(a, b, (((1,), (0,)), ((), ())), preferred_element_type=F32)


def fill_bias(lo_ref, segc_ref, padc_ref, segr_ref, bias_ref, nblocks, most):
    def one(qb, _):
        lo = lo_ref[qb]
        q0 = pl.multiple_of(qb * QB, QB)
        segq = segr_ref[pl.ds(qb, 1), :]
        qpos = q0 + lax.broadcasted_iota(jnp.int32, (QB, QB), 1)

        def part(j, _):
            k0 = pl.multiple_of((lo + j) * QB, QB)
            kpos = k0 + lax.broadcasted_iota(jnp.int32, (QB, QB), 0)
            segk = segc_ref[pl.ds(k0, QB), :]
            padk = padc_ref[pl.ds(k0, QB), :]
            ok = (segk == segq) & (kpos <= qpos) & ((padk == 1) | (kpos == qpos))
            bias_ref[qb, pl.ds(pl.multiple_of(j * QB, QB), QB), :] = jnp.where(ok, 0.0, -1e30)
            return 0

        lax.fori_loop(0, qb - lo + 1, part, 0)
        return 0

    lax.fori_loop(0, nblocks, one, 0)


def head_pair(x, scale):
    lane = lax.broadcasted_iota(jnp.int32, x.shape, 1)
    first = jnp.where(lane < HD, scale, 0.0).astype(x.dtype)
    second = jnp.where(lane < HD, 0.0, scale).astype(x.dtype)
    return jnp.concatenate([x * first, x * second], 0)


def attn_fwd_kernel(nblocks, most, many, lo_ref, segc_ref, padc_ref, segr_ref, q_ref, k_ref, v_ref, o_ref, lse_ref, bias_ref, vt_ref):
    @pl.when(pl.program_id(0) == 0)
    def _():
        fill_bias(lo_ref, segc_ref, padc_ref, segr_ref, bias_ref, nblocks, most)

    vt_ref[...] = v_ref[...].T

    def block(qb, _):
        lo = lo_ref[qb]
        q0 = pl.multiple_of(qb * QB, QB)
        k0 = pl.multiple_of(lo * QB, QB)
        for n in range(1, most + 1):
            @pl.when(qb - lo + 1 == n)
            def _(n=n):
                w = n * QB
                bias = bias_ref[qb, 0:w, :]
                bias = jnp.concatenate([bias, bias], 1)
                cols = [slice(128 * i, 128 * (i + 1)) for i in range(many)]
                scores = [nt(k_ref[pl.ds(k0, w), c], head_pair(q_ref[pl.ds(q0, QB), c], HD ** -0.5)) + bias for c in cols]
                tops = [jnp.max(s, 0, keepdims=True) for s in scores]
                parts = [jnp.exp(s - m) for s, m in zip(scores, tops)]
                totals = [jnp.sum(p, 0, keepdims=True) for p in parts]
                outs = [nn(vt_ref[c, pl.ds(k0, w)], (p * (1.0 / t)).astype(BF16)) for c, p, t in zip(cols, parts, totals)]
                for i, (c, o, m, t) in enumerate(zip(cols, outs, tops, totals)):
                    o = jnp.concatenate([o[:HD, :QB], o[HD:, QB:]], 0)
                    o_ref[pl.ds(q0, QB), c] = o.T.astype(BF16)
                    lse_ref[i, pl.ds(qb, 1), :] = m + jnp.log(t)
        return 0

    lax.fori_loop(0, nblocks, block, 0)


def attn_bwd_kernel(nblocks, most, many, lo_ref, segc_ref, padc_ref, segr_ref, q_ref, k_ref, v_ref, do_ref, lse_ref,
                    out_ref, sums_ref, bias_ref, kt_ref, dk_acc, dv_acc):
    @pl.when(pl.program_id(0) == 0)
    def _():
        fill_bias(lo_ref, segc_ref, padc_ref, segr_ref, bias_ref, nblocks, most)

    kt_ref[...] = k_ref[...].T
    dk_acc[...] = jnp.zeros_like(dk_acc)
    dv_acc[...] = jnp.zeros_like(dv_acc)
    sums_ref[...] = jnp.zeros_like(sums_ref)

    def block(qb, _):
        lo = lo_ref[qb]
        q0 = pl.multiple_of(qb * QB, QB)
        k0 = pl.multiple_of(lo * QB, QB)
        for n in range(1, most + 1):
            @pl.when(qb - lo + 1 == n)
            def _(n=n):
                w = n * QB
                bias = bias_ref[qb, 0:w, :]
                bias = jnp.concatenate([bias, bias], 1)
                cols = [slice(128 * i, 128 * (i + 1)) for i in range(many)]
                rows, keys = pl.ds(q0, QB), pl.ds(k0, w)
                q2 = [head_pair(q_ref[rows, c], HD ** -0.5) for c in cols]
                do2 = [head_pair(do_ref[rows, c], 1.0) for c in cols]
                probs = [jnp.exp(nt(k_ref[keys, c], q) + bias - lse_ref[i, pl.ds(qb, 1), :]) for i, (c, q) in enumerate(zip(cols, q2))]
                dprobs = [nt(v_ref[keys, c], do) for c, do in zip(cols, do2)]
                inner = [jnp.sum(p * dp, 0, keepdims=True) for p, dp in zip(probs, dprobs)]
                ds = [(p * (dp - i)).astype(BF16) for p, dp, i in zip(probs, dprobs, inner)]
                for c, p, d, q, do in zip(cols, probs, ds, q2, do2):
                    dv_acc[keys, c] += nn(p.astype(BF16), do)
                    dk_acc[keys, c] += nn(d, q)
                    dq = nn(kt_ref[c, keys], d)
                    dq = jnp.concatenate([dq[:HD, :QB], dq[HD:, QB:]], 0) * (HD ** -0.5)
                    dq = dq.T.astype(BF16)
                    out_ref[0, rows, c] = dq
                    sums_ref[0:1, c] += jnp.sum(dq.astype(F32), 0, keepdims=True)
        return 0

    lax.fori_loop(0, nblocks, block, 0)
    out_ref[1] = dk_acc[...].astype(BF16)
    dv = dv_acc[...].astype(BF16)
    out_ref[2] = dv
    sums_ref[1:2, :] = jnp.sum(dv.astype(F32), 0, keepdims=True)


def mask_inputs(segment_ids, padding_mask):
    length = segment_ids.shape[0]
    nblocks = length // QB
    first = segment_ids.reshape(nblocks, QB)[:, 0]
    start = jnp.sum((segment_ids[None, :] < first[:, None]).astype(jnp.int32), 1)
    lo = start // QB
    segc = jnp.broadcast_to(segment_ids[:, None], (length, QB))
    padc = jnp.broadcast_to(padding_mask[:, None], (length, QB))
    return lo.astype(jnp.int32), segc, padc, segment_ids.reshape(nblocks, QB)


def attn_call(kernel, name, each, operands, specs, shapes, out_specs, scratch, masks, first, pairs, before):
    lo, segc, padc, segr = masks
    length = segc.shape[0]
    nblocks = length // QB
    most = min(nblocks, SPAN // QB + 1)
    whole = lambda p, lo: (0, 0)
    in_specs = [pl.BlockSpec((length, QB), whole), pl.BlockSpec((length, QB), whole), pl.BlockSpec((nblocks, QB), whole)] + specs
    arguments = [lo, segc, padc, segr] + operands
    aliases = {}
    if before is not None:
        aliases = {len(arguments) + i: i for i in range(len(before))}
        in_specs, arguments = in_specs + [pl.BlockSpec(memory_space=pl.ANY)] * len(before), arguments + list(before)

    def body(*refs):
        inputs, rest = refs[: len(arguments) - len(aliases)], refs[len(arguments) :]
        kernel(nblocks, most, MANY, *inputs, *rest)

    return pl.pallas_call(
        body,
        grid_spec=pltpu.PrefetchScalarGridSpec(
            num_scalar_prefetch=1, grid=(pairs // MANY,), in_specs=in_specs, out_specs=out_specs,
            scratch_shapes=[pltpu.VMEM((nblocks, most * QB, QB), F32)] + scratch),
        out_shape=shapes,
        input_output_aliases=aliases,
        compiler_params=pltpu.CompilerParams(vmem_limit_bytes=48 << 20),
        cost_estimate=cost(each * pairs),
        name=name,
    )(*arguments)


def attn_forward(q, k, v, masks, first, pairs, before=None):
    (qa, qo), (ka, ko), (va, vo) = q, k, v
    length, width = qa.shape[0], 128 * MANY
    at = first // MANY
    col = lambda off: pl.BlockSpec((length, width), lambda p, lo: (0, off // MANY + at + p))
    stat = pl.BlockSpec((MANY, length // QB, 2 * QB), lambda p, lo: (at + p, 0, 0))
    total = ko - qo
    return attn_call(
        attn_fwd_kernel, "attn_forward", 2.7, [qa, ka, va], [col(qo), col(ko), col(vo)],
        [jax.ShapeDtypeStruct((length, 128 * total), BF16), jax.ShapeDtypeStruct((total, length // QB, 2 * QB), F32)],
        [col(0), stat], [pltpu.VMEM((width, length), BF16)], masks, first, pairs, before)


def attn_backward(q, k, v, do, lse, masks, first, pairs, before=None):
    (qa, qo), (ka, ko), (va, vo) = q, k, v
    length, width = qa.shape[0], 128 * MANY
    at = first // MANY
    col = lambda off: pl.BlockSpec((length, width), lambda p, lo: (0, off // MANY + at + p))
    stat = pl.BlockSpec((MANY, length // QB, 2 * QB), lambda p, lo: (at + p, 0, 0))
    total = ko - qo
    return attn_call(
        attn_bwd_kernel, "attn_backward", 3.4, [qa, ka, va, do, lse], [col(qo), col(ko), col(vo), col(0), stat],
        [jax.ShapeDtypeStruct((3, length, 128 * total), BF16), jax.ShapeDtypeStruct((8, 128 * total), F32)],
        [pl.BlockSpec((3, length, width), lambda p, lo: (0, 0, at + p)), pl.BlockSpec((8, width), lambda p, lo: (0, at + p))],
        [pltpu.VMEM((width, length), BF16), pltpu.VMEM((length, width), F32), pltpu.VMEM((length, width), F32)],
        masks, first, pairs, before)


ANY = pl.BlockSpec(memory_space=pl.ANY)
META = 1


def params(megabytes=56):
    return pltpu.CompilerParams(vmem_limit_bytes=megabytes << 20)


def tile_shape(native, rows, columns):
    return (1, 1, 1, rows, columns) if native else (4, 4, 2, rows // 32, columns)


def fetch_columns(native, meta, groups, target, start, columns, sem):
    cols = pl.ds(start, columns)
    if native:
        pltpu.make_async_copy(groups[0].at[:, cols], target.at[0, 0, 0], sem).start()
        return
    core = meta[4]
    for t in range(4):
        pltpu.make_async_copy(groups[t].at[:, :, cols], target.at[meta[t], :, core], sem).start()
        pltpu.make_async_copy(groups[4 + t].at[:, :, cols], target.at[meta[t], :, 1 - core], sem).start()


def quarter_shape(native, rows, columns):
    return (1, 1, rows // 4, columns) if native else (4, 2, rows // 32, columns)


def fetch_quarter(native, meta, groups, target, t, sem):
    cols = pl.ds(0, target.shape[-1])
    if native:
        rows = target.shape[-2]
        pltpu.make_async_copy(groups[0].at[pl.ds(t * rows, rows), cols], target.at[0, 0], sem).start()
        return
    core = meta[4]
    pltpu.make_async_copy(groups[t].at[:, :, cols], target.at[:, core], sem).start()
    pltpu.make_async_copy(groups[4 + t].at[:, :, cols], target.at[:, 1 - core], sem).start()


def arrive(target, sem):
    pltpu.make_async_copy(target, target, sem).wait()


def group_specs(groups):
    return [ANY] * len(groups)


def flat(value):
    return value.reshape(-1, value.shape[-1])


def out_blocks(native, rows, columns):
    if native:
        return [jax.ShapeDtypeStruct((rows, columns), BF16)]
    return [jax.ShapeDtypeStruct((4, 4, rows // 32, columns), BF16)] * 2


def push_columns(native, meta, stage, outs, start, columns, sem):
    cols = pl.ds(start, columns)
    if native:
        pltpu.make_async_copy(stage.at[0, 0, 0], outs[0].at[:, cols], sem).start()
        return
    core = meta[4]
    for t in range(4):
        pltpu.make_async_copy(stage.at[meta[t], :, core], outs[0].at[t, :, :, cols], sem).start()
        pltpu.make_async_copy(stage.at[meta[t], :, 1 - core], outs[1].at[FLIP[t], :, :, cols], sem).start()


def each_rows(total, rows, body):
    def step(i, _):
        body(i, pl.ds(pl.multiple_of(i * rows, rows), rows))
        return 0

    lax.fori_loop(0, total // rows, step, 0)


def squares(values, valid):
    return jnp.sum(values * values * valid, 0, keepdims=True)


def scale_of(values):
    return lax.rsqrt(jnp.mean(values * values, -1, keepdims=True) + 1e-05)


SMALL = 16


def pack_smalls(bias_up, bias_qv, bias_out, gain_attn, gain_mlp, bias_down, rows):
    at = lax.broadcasted_iota(jnp.int32, (rows, 128), 0)
    block = jnp.zeros((rows, 128), bias_up.dtype)
    for row, part in enumerate((bias_up, bias_qv, bias_out, gain_attn, gain_mlp, bias_down)):
        block = jnp.where(at == row, jnp.pad(part, (0, 128 - part.shape[0]))[None], block)
    return block


def unpack_smalls(held, up_ref, qkv_ref, lines_ref):
    width = lines_ref.shape[1]
    for shard in range(32):
        up_ref[0:1, shard * 128 : (shard + 1) * 128] = held[shard, 0:1].astype(F32)
    halves = held[...].astype(F32).reshape(16, 2, SMALL, 128)
    halves = halves[:, 0] + pltpu.roll(halves[:, 1], 64, 2)
    fours = held[...].astype(F32).reshape(8, 4, SMALL, 128)
    fours = fours[:, 0] + sum(pltpu.roll(fours[:, i], 32 * i, 2) for i in range(1, 4))
    qkv_ref[...] = jnp.zeros_like(qkv_ref)
    for i in range(16):
        first = i * 128 + (width if i >= 8 else 0)
        qkv_ref[0:1, first : first + 128] = halves[i, 1:2]
    for i in range(8):
        lines_ref[0:4, i * 128 : (i + 1) * 128] = fours[i, 2:6]


def project_kernel(native, tile, count, meta, tok_ref, valid_ref, *rest):
    groups, rest = rest[:count], rest[count:]
    if native:
        up_in, qkv_in, lines_in, out_ref, normed_ref, sq_ref, weight, sems = rest
    else:
        out_ref, normed_ref, sq_ref, up_ref, lines_ref, weight, held, qkv_in, sems = rest
        lines_in = lines_ref
    n, steps = pl.program_id(0), pl.num_programs(0)
    columns = steps * tile

    @pl.when(n == 0)
    def _():
        if not native:
            last = pl.ds(columns, 128)
            for t in range(4):
                for first, side in ((0, meta[4]), (4, 1 - meta[4])):
                    source = groups[first + t].at[:, pl.ds(0, SMALL), last]
                    pltpu.make_async_copy(source, held.at[meta[t], :, side], sems.at[2]).start()
        fetch_columns(native, meta, groups, weight.at[0], 0, tile, sems.at[0])

    @pl.when(n + 1 < steps)
    def _():
        slot = (n + 1) % 2
        fetch_columns(native, meta, groups, weight.at[slot], pl.multiple_of((n + 1) * tile, tile), tile, sems.at[slot])

    @pl.when(n == 0)
    def _():
        if not native:
            arrive(held, sems.at[2])
            unpack_smalls(held[...].reshape(32, SMALL, 128), up_ref, qkv_in, lines_ref)
        sq_ref[...] = jnp.zeros_like(sq_ref)

        def norm(i, at):
            frames = tok_ref[at, :].astype(F32)
            sq_ref[...] += squares(frames, valid_ref[at, :])
            normed_ref[at, :] = (frames * scale_of(frames) * lines_in[1:2, :]).astype(BF16)

        each_rows(tok_ref.shape[0], 256, norm)

    arrive(weight.at[n % 2], sems.at[n % 2])
    bias = qkv_in[0:1, pl.ds(pl.multiple_of(n * tile, tile), tile)]
    out_ref[...] = (nn(normed_ref[...], flat(weight[n % 2])) + bias).astype(BF16)


def project(ladder, tokens, valid, groups, known=None):
    length, width = tokens.shape
    columns, tile, hidden = 3 * width, 512, 4 * width
    native = ladder.native
    whole = lambda n, meta: (0, 0)
    up, lines = pl.BlockSpec((1, hidden), whole), pl.BlockSpec((4, width), whole)
    out_specs = [pl.BlockSpec((length, tile), lambda n, meta: (0, n)), pl.BlockSpec((length, width), whole), pl.BlockSpec((1, width), whole)]
    out_shape = [jax.ShapeDtypeStruct((length, columns), BF16), jax.ShapeDtypeStruct((length, width), BF16),
                 jax.ShapeDtypeStruct((1, width), F32)]
    scratch = [pltpu.VMEM((2,) + tile_shape(native, width, tile), BF16)]
    vectors = [jax.ShapeDtypeStruct((1, hidden), F32), jax.ShapeDtypeStruct((4, width), F32)]
    extra = []
    if native:
        extra = [up, pl.BlockSpec((1, columns), whole), lines]
    else:
        out_specs, out_shape = out_specs + [up, lines], out_shape + vectors
        scratch += [pltpu.VMEM((4, 4, 2, SMALL, 128), BF16), pltpu.VMEM((1, columns), F32)]
    results = pl.pallas_call(
        functools.partial(project_kernel, native, tile, len(groups)),
        grid_spec=pltpu.PrefetchScalarGridSpec(
            num_scalar_prefetch=1, grid=(columns // tile,),
            in_specs=[pl.BlockSpec((length, width), whole), pl.BlockSpec((length, 1), whole)] + group_specs(groups) + extra,
            out_specs=out_specs, scratch_shapes=scratch + [pltpu.SemaphoreType.DMA((3,))]),
        out_shape=out_shape,
        compiler_params=params(),
        cost_estimate=cost(14),
        name="project",
    )(ladder.meta, tokens, valid, *groups, *(known or ()))
    return results if not native else list(results) + [known[0], known[2]]


def gelu_pair(u):
    c, d = 0.7978845608028654, 0.044715
    square = u * u
    bend = 0.5 * jnp.tanh(u * (c + c * d * square))
    half = 0.5 + bend
    slope = half * (1.0 + (0.5 - bend) * (u * (2.0 * c + 6.0 * c * d * square)))
    return (u * half).astype(BF16), slope.astype(BF16)


def expand_kernel(native, tile, count, meta, mixed_ref, tok_ref, lines_ref, valid_ref, up_bias_ref, *rest):
    groups, rest = rest[:count], rest[count:]
    middle_ref, normed_ref, sq_ref, act_ref, slope_ref, middle, out_weight, weight, sems = rest
    n, steps = pl.program_id(0), pl.num_programs(0)
    half = out_weight.shape[-1]
    first = 2 * half
    store = pltpu.make_async_copy(middle, middle_ref, sems.at[4])

    @pl.when(n == 0)
    def _():
        for side in range(2):
            fetch_columns(native, meta, groups, out_weight.at[side], side * half, half, sems.at[2 + side])
        fetch_columns(native, meta, groups, weight.at[0], first, tile, sems.at[0])

    @pl.when(n + 1 < steps)
    def _():
        slot = (n + 1) % 2
        fetch_columns(native, meta, groups, weight.at[slot], pl.multiple_of(first + (n + 1) * tile, tile), tile, sems.at[slot])

    @pl.when(n == 0)
    def _():
        for side in range(2):
            arrive(out_weight.at[side], sems.at[2 + side])
        sq_ref[...] = jnp.zeros_like(sq_ref)

        def part(i, at):
            branch = jnp.concatenate([nn(mixed_ref[at, :], flat(out_weight[side])) for side in range(2)], 1) + lines_ref[0:1, :]
            total = tok_ref[at, :].astype(F32) + branch
            middle[at, :] = total
            normed_ref[at, :] = (total * scale_of(total) * lines_ref[2:3, :]).astype(BF16)
            sq_ref[0:1, :] += squares(branch, valid_ref[at, :])
            sq_ref[1:2, :] += squares(total, valid_ref[at, :])

        each_rows(middle.shape[0], 256, part)
        store.start()

    arrive(weight.at[n % 2], sems.at[n % 2])
    act_ref[...], slope_ref[...] = gelu_pair(nn(normed_ref[...], flat(weight[n % 2])) + up_bias_ref[...])

    @pl.when(n == steps - 1)
    def _():
        store.wait()


def expand(ladder, mixed, tokens, lines, valid, up_bias, groups):
    length, width = tokens.shape
    columns, tile = up_bias.shape[1], 512
    whole = lambda n, meta: (0, 0)
    column = lambda n, meta: (0, n)
    square = pl.BlockSpec((length, width), whole)
    return pl.pallas_call(
        functools.partial(expand_kernel, ladder.native, tile, len(groups)),
        grid_spec=pltpu.PrefetchScalarGridSpec(
            num_scalar_prefetch=1, grid=(columns // tile,),
            in_specs=[square, square, pl.BlockSpec((4, width), whole), pl.BlockSpec((length, 1), whole), pl.BlockSpec((1, tile), column)]
            + group_specs(groups),
            out_specs=[ANY, square, pl.BlockSpec((8, width), whole), pl.BlockSpec((length, tile), column),
                       pl.BlockSpec((length, tile), column)],
            scratch_shapes=[pltpu.VMEM((length, width), F32),
                            pltpu.VMEM((2,) + tile_shape(ladder.native, width, width // 2), BF16),
                            pltpu.VMEM((2,) + tile_shape(ladder.native, width, tile), BF16), pltpu.SemaphoreType.DMA((5,))]),
        out_shape=[jax.ShapeDtypeStruct((length, width), F32), jax.ShapeDtypeStruct((length, width), BF16),
                   jax.ShapeDtypeStruct((8, width), F32)] + [jax.ShapeDtypeStruct((length, columns), BF16)] * 2,
        compiler_params=params(),
        cost_estimate=cost(29),
        name="expand",
    )(ladder.meta, mixed, tokens, lines, valid, up_bias, *groups)


def fetch_turn(native, meta, groups, weight, sems, t, first=0, last=3):
    for at in range(first, last + 1):
        @pl.when(t == max(at - 1, first))
        def _(at=at):
            fetch_quarter(native, meta, groups, weight.at[at % 2], at, sems.at[at % 2])

    arrive(weight.at[t % 2], sems.at[t % 2])


def tn(a, b):
    return lax.dot_general(a, b, (((0,), (0,)), ((), ())), preferred_element_type=F32)


def down_grad_kernel(native, count, meta, act_ref, cot_ref, *rest):
    outs, (sum_ref, stage, sems) = rest[:count], rest[count:]
    t = pl.program_id(0)
    slot = t % 2

    @pl.when(t >= 2)
    def _():
        arrive(stage.at[slot], sems.at[slot])

    stage[slot] = tn(act_ref[...], cot_ref[...]).astype(BF16).reshape(stage.shape[1:])
    if native:
        rows = stage.shape[-2]
        pltpu.make_async_copy(stage.at[slot, 0, 0], outs[0].at[pl.ds(t * rows, rows), :], sems.at[slot]).start()
    else:
        for k in range(4):
            @pl.when(t == k)
            def _(k=k):
                pltpu.make_async_copy(stage.at[slot, :, meta[4]], outs[0].at[k], sems.at[slot]).start()
                pltpu.make_async_copy(stage.at[slot, :, 1 - meta[4]], outs[1].at[FLIP[k]], sems.at[slot]).start()

    @pl.when(t == 0)
    def _():
        sum_ref[...] = jnp.sum(cot_ref[...].astype(F32), 0, keepdims=True)

    @pl.when(t == 3)
    def _():
        arrive(stage.at[1 - slot], sems.at[1 - slot])
        arrive(stage.at[slot], sems.at[slot])


def down_grad(ladder, act, cot):
    length, width = cot.shape
    hidden = act.shape[1]
    outs = out_blocks(ladder.native, hidden, width)
    whole = lambda t, meta: (0, 0)
    return pl.pallas_call(
        functools.partial(down_grad_kernel, ladder.native, len(outs)),
        grid_spec=pltpu.PrefetchScalarGridSpec(
            num_scalar_prefetch=1, grid=(4,),
            in_specs=[pl.BlockSpec((length, hidden // 4), lambda t, meta: (0, meta[t])), pl.BlockSpec((length, width), whole)],
            out_specs=[ANY] * len(outs) + [pl.BlockSpec((1, width), whole)],
            scratch_shapes=[pltpu.VMEM((2,) + quarter_shape(ladder.native, hidden, width), BF16), pltpu.SemaphoreType.DMA((2,))]),
        out_shape=outs + [jax.ShapeDtypeStruct((1, width), F32)],
        compiler_params=params(),
        cost_estimate=cost(14),
        name="down_grad",
    )(ladder.meta, act, cot)


def row_grad_kernel(native, tile, count, meta, left_ref, right_ref, *rest):
    outs, (stage, sems) = rest[:count], rest[count:]
    n, steps = pl.program_id(0), pl.num_programs(0)
    slot = n % 2

    @pl.when(n >= 2)
    def _():
        arrive(stage.at[slot], sems.at[slot])

    stage[slot] = tn(left_ref[...], right_ref[...]).astype(BF16).reshape(stage.shape[1:])
    push_columns(native, meta, stage.at[slot], outs, pl.multiple_of(n * tile, tile), tile, sems.at[slot])

    @pl.when(n == steps - 1)
    def _():
        arrive(stage.at[1 - slot], sems.at[1 - slot])
        arrive(stage.at[slot], sems.at[slot])


def row_grad(ladder, left, right, name):
    length, width = left.shape
    parts, _, each = right.shape
    tile = 512
    per = each // tile
    outs = out_blocks(ladder.native, width, parts * each)
    return pl.pallas_call(
        functools.partial(row_grad_kernel, ladder.native, tile, len(outs)),
        grid_spec=pltpu.PrefetchScalarGridSpec(
            num_scalar_prefetch=1, grid=(parts * per,),
            in_specs=[pl.BlockSpec((length, width), lambda n, meta: (0, 0)),
                      pl.BlockSpec((None, length, tile), lambda n, meta: (n // per, 0, n % per))],
            out_specs=[ANY] * len(outs),
            scratch_shapes=[pltpu.VMEM((2,) + tile_shape(ladder.native, width, tile), BF16), pltpu.SemaphoreType.DMA((2,))]),
        out_shape=outs,
        compiler_params=params(),
        cost_estimate=cost(8),
        name=name,
    )(ladder.meta, left, right)


def norm_grad(grad, source, gain):
    r = scale_of(source)
    hat = source * r
    gain_grad = jnp.sum(grad * hat, 0, keepdims=True)
    scaled = grad * gain
    return r * (scaled - hat * jnp.mean(scaled * hat, -1, keepdims=True)), gain_grad


def back_kernel(native, last, counts, meta, cot_ref, slope_ref, normed_ref, lines_ref, middle_ref, mixed_ref, *rest):
    down_groups, rest = rest[: counts[0]], rest[counts[0] :]
    groups, rest = rest[: counts[0]], rest[counts[0] :]
    if last:
        before, rest = rest[0], rest[1 + counts[1] :]
    pushed, rest = rest[: counts[1]], rest[counts[1] :]
    if last:
        out_ref, branch_ref, mixed_out_ref, sum_ref, up_sum_ref, rest = *rest[:5], rest[5:]
        acc, down_weight, weight, stage, sems, middle, out_weight = rest
    else:
        after, up_sum_ref, acc, down_weight, weight, stage, sems = rest
    base = 2 if last else 0
    step = pl.program_id(0)
    t = step + base
    width, tile = normed_ref.shape[1], slope_ref.shape[1]
    slot = step

    def columns(at):
        return pl.multiple_of(width + meta[at] * tile, 512)

    @pl.when(step == 0)
    def _():
        for at in range(2):
            fetch_columns(native, meta, groups, weight.at[at], columns(base + at), tile, sems.at[2 + at])
        if last:
            pltpu.make_async_copy(before, acc, sems.at[6]).start()
            pltpu.make_async_copy(middle_ref, middle, sems.at[7]).start()
            fetch_columns(native, meta, groups, out_weight, 0, width, sems.at[8])

    fetch_turn(native, meta, down_groups, down_weight, sems, t, base, base + 1)
    length = acc.shape[0]
    grad = (nt(cot_ref[...], flat(down_weight[t % 2])) * slope_ref[...].astype(F32)).astype(BF16)
    up_sum_ref[...] = jnp.sum(grad.astype(F32), 0, keepdims=True)
    stage[slot] = tn(normed_ref[...], grad).astype(BF16).reshape(stage.shape[1:])
    push_columns(native, meta, stage.at[slot], pushed, columns(t), tile, sems.at[4 + slot])
    arrive(weight.at[slot], sems.at[2 + slot])
    product = nt(grad, flat(weight[slot]))

    @pl.when(step == 0)
    def _():
        if last:
            pltpu.make_async_copy(before, acc, sems.at[6]).wait()
            acc[...] += product
        else:
            acc[...] = product

    @pl.when(step == 1)
    def _():
        acc[...] += product
        if last:
            pltpu.make_async_copy(middle_ref, middle, sems.at[7]).wait()
            sum_ref[...] = jnp.zeros_like(sum_ref)

            def part(i, at):
                back, gain_grad = norm_grad(acc[at, :], middle[at, :], lines_ref[2:3, :])
                total = cot_ref[at, :].astype(F32) + back
                acc[at, :] = total
                branch = total.astype(BF16)
                branch_ref[at, :] = branch
                sum_ref[0:1, :] += gain_grad
                sum_ref[1:2, :] += jnp.sum(branch.astype(F32), 0, keepdims=True)

            each_rows(length, 256, part)
            pltpu.make_async_copy(acc, out_ref, sems.at[6]).start()
            arrive(stage.at[0], sems.at[4])
            stage[0] = tn(mixed_ref[...], branch_ref[...]).astype(BF16).reshape(stage.shape[1:])
            push_columns(native, meta, stage.at[0], pushed, 0, width, sems.at[4])
            arrive(out_weight, sems.at[8])
            mixed_out_ref[...] = nt(branch_ref[...], flat(out_weight[...])).astype(BF16)
            pltpu.make_async_copy(acc, out_ref, sems.at[6]).wait()
        else:
            pltpu.make_async_copy(acc, after, sems.at[6]).start()
            pltpu.make_async_copy(acc, after, sems.at[6]).wait()
        for at in range(2):
            arrive(stage.at[at], sems.at[4 + at])


def back(ladder, cot, slope, normed, lines, middle, mixed, down_groups, groups, before=None):
    length, width = cot.shape
    hidden, tile = slope.shape[1], slope.shape[1] // 4
    last = before is not None
    base = 2 if last else 0
    whole = lambda t, meta: (0, 0)
    part = lambda t, meta: (0, meta[t + base])
    square = pl.BlockSpec((length, width), whole)
    once = pl.BlockSpec((length, width), whole, pipeline_mode=pl.Buffered(1))
    outs = out_blocks(ladder.native, width, hidden + width)
    counts = (len(groups), len(outs))
    full, wide = jax.ShapeDtypeStruct((length, width), F32), jax.ShapeDtypeStruct((length, width), BF16)
    sums = jax.ShapeDtypeStruct((1, hidden), F32)
    in_specs = [once, pl.BlockSpec((length, tile), part), once, pl.BlockSpec((4, width), whole), ANY, once if last else ANY]
    in_specs += [ANY] * (2 * counts[0])
    operands = [ladder.meta, cot, slope, normed, lines, middle, mixed, *down_groups, *groups]
    scratch = [pltpu.VMEM((length, width), F32), pltpu.VMEM((2,) + quarter_shape(ladder.native, hidden, width), BF16),
               pltpu.VMEM((2,) + tile_shape(ladder.native, width, tile), BF16),
               pltpu.VMEM((2,) + tile_shape(ladder.native, width, tile), BF16), pltpu.SemaphoreType.DMA((9,))]
    aliases = {}
    if last:
        aliases = {len(operands) + 1 + i: i for i in range(counts[1])}
        operands += list(before)
        in_specs += [ANY] * (1 + counts[1])
        out_specs = [ANY] * counts[1] + [ANY, square, square, pl.BlockSpec((8, width), whole)]
        out_shape = outs + [full, wide, wide, jax.ShapeDtypeStruct((8, width), F32)]
        scratch += [pltpu.VMEM((length, width), F32), pltpu.VMEM(tile_shape(ladder.native, width, width), BF16)]
    else:
        out_specs, out_shape = [ANY] * counts[1] + [ANY], outs + [full]
    return pl.pallas_call(
        functools.partial(back_kernel, ladder.native, last, counts),
        grid_spec=pltpu.PrefetchScalarGridSpec(
            num_scalar_prefetch=1, grid=(2,), in_specs=in_specs, out_specs=out_specs + [pl.BlockSpec((1, tile), lambda t, meta: (0, t))],
            scratch_shapes=scratch),
        out_shape=out_shape + [jax.ShapeDtypeStruct((1, hidden // 2), F32)],
        input_output_aliases=aliases,
        compiler_params=params(),
        cost_estimate=cost(30 if last else 20),
        name="back",
    )(*operands)


def contract_kernel(native, first, meta, act_ref, lines_ref, valid_ref, middle_ref, *rest):
    groups, (out_ref, sq_ref, acc, middle, weight, sems) = rest[:-6], rest[-6:]
    t = pl.program_id(0)
    load = pltpu.make_async_copy(middle_ref.at[pl.ds(first, acc.shape[0]), :], middle, sems.at[2])

    @pl.when(t == 0)
    def _():
        load.start()

    fetch_turn(native, meta, groups, weight, sems, t)
    product = nn(act_ref[...], flat(weight[t % 2]))

    @pl.when(t == 0)
    def _():
        acc[...] = product

    @pl.when(t > 0)
    def _():
        acc[...] += product

    @pl.when(t == 3)
    def _():
        load.wait()
        sq_ref[...] = jnp.zeros_like(sq_ref)
        rows = 256

        def part(i, _):
            at = pl.ds(pl.multiple_of(i * rows, rows), rows)
            branch = acc[at, :] + lines_ref[3:4, :]
            final = middle[at, :] + branch
            out_ref[at, :] = final.astype(BF16)
            sq_ref[0:1, :] += squares(branch, valid_ref[at, :])
            sq_ref[1:2, :] += squares(final, valid_ref[at, :])
            return 0

        lax.fori_loop(0, acc.shape[0] // rows, part, 0)


def contract(ladder, act, middle, lines, valid, groups, part, parts):
    length, width = middle.shape
    length //= parts
    hidden = act.shape[1]
    whole = lambda t, meta: (0, 0)
    return pl.pallas_call(
        functools.partial(contract_kernel, ladder.native, part * length),
        grid_spec=pltpu.PrefetchScalarGridSpec(
            num_scalar_prefetch=1, grid=(4,),
            in_specs=[pl.BlockSpec((length, hidden // 4), lambda t, meta: (part, meta[t])), pl.BlockSpec((4, width), whole),
                      pl.BlockSpec((length, 1), lambda t, meta: (part, 0)), ANY] + group_specs(groups),
            out_specs=[pl.BlockSpec((length, width), whole), pl.BlockSpec((8, width), whole)],
            scratch_shapes=[pltpu.VMEM((length, width), F32), pltpu.VMEM((length, width), F32),
                            pltpu.VMEM((2,) + quarter_shape(ladder.native, hidden, width), BF16), pltpu.SemaphoreType.DMA((3,))]),
        out_shape=[jax.ShapeDtypeStruct((length, width), BF16), jax.ShapeDtypeStruct((8, width), F32)],
        compiler_params=params(),
        cost_estimate=cost(16 // parts),
        name="contract",
    )(ladder.meta, act, lines, valid, middle, *groups)


def input_grad_kernel(native, calls, meta, *rest):
    grads, (tok_ref, middle_ref, lines_ref), rest = rest[:calls], rest[calls : calls + 3], rest[calls + 3 :]
    groups, (out_ref, sum_ref, acc, middle, weight, sems) = rest[:-6], rest[-6:]
    t = pl.program_id(0)
    load = pltpu.make_async_copy(middle_ref, middle, sems.at[2])

    @pl.when(t == 0)
    def _():
        load.start()

    fetch_turn(native, meta, groups, weight, sems, t)
    width = acc.shape[1]
    quarter = width // 4
    rows = flat(weight[t % 2])
    each = width // calls
    product = 0.0
    for part in range(3):
        for call in range(calls):
            first = part * width + call * each
            product += nt(grads[call][part], rows[:, first : first + each])
    acc[:, pl.ds(pl.multiple_of(meta[t] * quarter, quarter), quarter)] = product

    @pl.when(t == 3)
    def _():
        load.wait()
        sum_ref[...] = jnp.zeros_like(sum_ref)
        rows = 256

        def part(i, _):
            at = pl.ds(pl.multiple_of(i * rows, rows), rows)
            back, gain_grad = norm_grad(acc[at, :], tok_ref[at, :].astype(F32), lines_ref[1:2, :])
            out_ref[at, :] = (middle[at, :] + back).astype(BF16)
            sum_ref[0:1, :] += gain_grad
            return 0

        lax.fori_loop(0, acc.shape[0] // rows, part, 0)


def input_grad(ladder, grads, tokens, grad_middle, lines, groups):
    length, width = tokens.shape
    calls = len(grads)
    whole = lambda t, meta: (0, 0)
    square = pl.BlockSpec((length, width), whole)
    return pl.pallas_call(
        functools.partial(input_grad_kernel, ladder.native, calls),
        grid_spec=pltpu.PrefetchScalarGridSpec(
            num_scalar_prefetch=1, grid=(4,),
            in_specs=[pl.BlockSpec((3, length, width // calls), lambda t, meta: (0, 0, 0))] * calls + [square, ANY, pl.BlockSpec((4, width), whole)]
            + group_specs(groups),
            out_specs=[square, pl.BlockSpec((8, width), whole)],
            scratch_shapes=[pltpu.VMEM((length, width), F32), pltpu.VMEM((length, width), F32),
                            pltpu.VMEM((2,) + quarter_shape(ladder.native, width, 3 * width), BF16), pltpu.SemaphoreType.DMA((3,))]),
        out_shape=[jax.ShapeDtypeStruct((length, width), BF16), jax.ShapeDtypeStruct((8, width), F32)],
        compiler_params=params(),
        cost_estimate=cost(18),
        name="input_grad",
    )(ladder.meta, *grads, tokens, grad_middle, lines, *groups)


def local(ladder, tokens, cotangent, segment_ids, padding_mask, w_qkv, bias_qv, w_out, bias_out, gain_attn, gain_mlp,
          w_up, bias_up, w_down, bias_down):
    length, width = tokens.shape[1], tokens.shape[2]
    count = ladder.count
    ladder.place()
    tokens, cotangent = tokens[0], cotangent[0]

    def sent(*flows):
        return [value for flow in flows for value in flow.sent]

    sizes = [part.shape[0] for part in (bias_qv, bias_out, gain_attn, gain_mlp, bias_up, bias_down)]
    total = sum(sizes)
    ends = np.cumsum([0] + sizes)
    known = None
    first = w_qkv
    if ladder.native:
        every = lambda part: lax.all_gather(part, ladder.axes, axis=0, tiled=True).astype(F32)[None]
        qv = every(bias_qv)
        known = [every(bias_up), jnp.concatenate([qv[:, :width], jnp.zeros((1, width), F32), qv[:, width:]], 1),
                 jnp.concatenate([every(bias_out), every(gain_attn), every(gain_mlp), every(bias_down)], 0)]
    else:
        first = jnp.concatenate([w_qkv, pack_smalls(bias_up, bias_qv, bias_out, gain_attn, gain_mlp, bias_down, w_qkv.shape[0])], 1)
    qkv, down = Gather(ladder, first, True), Gather(ladder, w_down, False)
    qkv.start()
    rest = Gather(ladder, jnp.concatenate([w_out, w_up], 1), False)
    masks = mask_inputs(segment_ids[0], padding_mask[0])
    valid = padding_mask[0].astype(F32)[:, None]
    qkv.plane()
    rest.start(*qkv.sent)
    qkv.corner()
    rest.low()
    qkv_groups = qkv.finish()
    rest.plane()
    down.start(*rest.sent)
    projected, normed_in, sq_frames, up_bias, lines = project(ladder, tie(tokens, *sent(rest), *masks, *ladder.tables), valid, qkv_groups, known)
    per = width // 128
    calls = 2
    each = per // calls

    down.low(projected)
    projected = tie(projected, *sent(down))
    per = width // 128
    calls = 2
    each = per // calls

    def triple():
        return (projected, 0), (projected, per), (projected, 2 * per)

    heads = None
    for call in range(calls):
        heads = attn_forward(*triple(), masks, call * each, each, heads)
        if call == 0:
            rest.corner(heads[0])
            projected = tie(projected, heads[0], *sent(rest), *down.others)
    mixed, lse = heads
    rest_groups = rest.finish(mixed)
    down.plane(*rest.sent)
    middle, normed_mid, sq_middle, act, slope = expand(
        ladder, tie(mixed, *sent(down)), tokens, lines, valid, up_bias, rest_groups)

    down.corner(act)
    *down_parts, sum_down = down_grad(ladder, tie(act, *sent(down)), cotangent)
    flow_down = Scatter(ladder, down_parts)
    down_groups = down.finish(sum_down)
    *first_parts, first_acc, first_sum = back(
        ladder, tie(cotangent, sum_down), slope, normed_mid, lines, middle, mixed, down_groups, rest_groups)
    flow_down.corner(first_acc)
    *rest_parts, grad_middle, grad_branch, grad_mixed, sum_middle, second_sum = back(
        ladder, tie(cotangent, *sent(flow_down)), slope, normed_mid, lines, middle, mixed, down_groups, rest_groups,
        [first_acc, *first_parts])
    sum_up = jnp.concatenate([first_sum, second_sum], 1).reshape(4, -1)[ladder.order].reshape(1, -1)
    flow_rest = Scatter(ladder, rest_parts)
    flow_down.plane(grad_mixed)
    grad_mixed = tie(grad_mixed, *sent(flow_down))
    heads = None
    for call in range(calls):
        heads = attn_backward(*triple(), grad_mixed, lse, masks, call * each, each, heads)
        if call == 0:
            flow_down.spread(heads[0])
            flow_rest.corner(heads[0])
            grad_mixed = tie(grad_mixed, heads[0], *sent(flow_down, flow_rest))
    grad_projected, sum_qv = heads
    own_down = flow_down.finish(grad_projected)
    flow_qkv = Scatter(ladder, row_grad(ladder, normed_in, tie(grad_projected, *sent(flow_down)), "qkv_grad"))
    flow_rest.plane(*flow_qkv.parts)
    finals = []

    def finish_rows(part, *after):
        out, squares_out = contract(ladder, tie(act, *after), middle, lines, valid, down_groups, part, 2)
        finals.append(squares_out)
        return out

    outputs = [finish_rows(0, *flow_qkv.parts, *sent(flow_rest))]
    flow_rest.spread(outputs[0])
    flow_qkv.corner(outputs[0])
    tail = tie(tokens, *sent(flow_rest, flow_qkv))
    grad_tokens, sum_in = input_grad(ladder, [grad_projected], tail, grad_middle, lines, qkv_groups)
    flow_qkv.plane(grad_tokens)
    outputs.append(finish_rows(1, *sent(flow_qkv)))
    own_rest = flow_rest.finish(outputs[1])
    flow_qkv.spread(outputs[1], own_rest)
    output = jnp.concatenate(outputs, 0)

    sq_final = finals[0] + finals[1]
    members = [sq_frames, sq_middle[1:2], sq_final[1:2], sq_middle[:1], sq_final[:1], valid.reshape(1, -1)]
    members = jnp.sum(jnp.concatenate(members, 0), 1)
    small_grads = [sum_qv[:2].reshape(-1), sum_middle[1], sum_in[0], sum_middle[0], sum_up[0], sum_down[0]]
    table = jnp.concatenate([g.reshape(count, -1) for g in small_grads] + [jnp.broadcast_to(members, (count, 6))], 1)
    table = jnp.pad(table, ((0, 0), (0, -table.shape[1] % 128)))
    own_small, nearly = ladder.scatter_small(tie(table, *sent(flow_qkv)))
    own_qkv = flow_qkv.finish(nearly)

    owned = [own_small[ends[i] : ends[i + 1]] for i in range(6)]
    totals = own_small[total : total + 6]
    stats = jnp.sqrt(totals[:5] / (totals[5] * width))
    own_out, own_up = own_rest[:, :width], own_rest[:, width:]
    return (output[None], grad_tokens[None], own_qkv, owned[0], own_out, owned[1], owned[2], owned[3], own_up, owned[4],
            own_down, owned[5], stats, totals[5:6])


def solution(mesh):
    rows, wide, flat = P(("dp", "fsdp"), None, None), P(("dp", "fsdp"), None), P(("dp", "fsdp"))
    return jax.shard_map(
        functools.partial(local, Ladder(mesh)),
        mesh=mesh,
        in_specs=(rows, rows, wide, wide, wide, flat, wide, flat, flat, flat, wide, flat, wide, flat),
        out_specs=(rows, rows, wide, flat, wide, flat, flat, flat, wide, flat, wide, flat, P(), P()),
        check_vma=False,
    )
```

```python
import functools

import jax
import jax.numpy as jnp
import numpy as np
from jax import lax
from jax.experimental import pallas as pl
from jax.experimental.pallas import tpu as pltpu
from jax.sharding import PartitionSpec as P

HD = 64
QB = 128
SPAN = 512
MANY = 4
WEIGH = 2
PARTS = 1
F32 = jnp.float32
BF16 = jnp.bfloat16

CORE = 1
Z_HOPS = (2, 4, 6)
MIX = ((0, 1, 2, 3), (0, 2, 1, 3))
FLIP = (0, 2, 1, 3)
HOPS = ((4, 2, 8, 16), (4, 2, 16, 8))


def tie(value, *others):
    return lax.optimization_barrier((value,) + others)[0]


def add_up(*terms):
    return sum(term.astype(F32) for term in terms)


def cost(microseconds):
    return pl.CostEstimate(flops=int(WEIGH * microseconds * 1.15e9), transcendentals=0, bytes_accessed=0)


class Ladder:
    def __init__(self, mesh):
        self.count = int(np.prod(list(mesh.shape.values())))
        self.native = dict(mesh.shape) != {"dp": 4, "fsdp": 8}
        self.axes = ("dp", "fsdp")

    def place(self):
        if self.native:
            self.meta = jnp.array([0, 1, 2, 3, 0, 0], jnp.int32)
            self.order = jnp.arange(4)
            self.tables = ()
            return
        me = lax.axis_index(self.axes)
        odd = (me & CORE) == 1
        mix = jnp.where(odd, jnp.array(MIX[1], jnp.int32), jnp.array(MIX[0], jnp.int32))
        self.meta = jnp.concatenate([(me >> 3) ^ mix, (me & CORE)[None], ((me >> 1) & 3)[None]])
        self.order = mix[jnp.arange(4) ^ (me >> 3)]
        self.tables = (self.order,)

    def flip(self, value, even, odd):
        bits = (even, odd)
        return lax.ppermute(value, self.axes, [(i, i ^ bits[i & CORE]) for i in range(self.count)])

    def step(self, value, level):
        return self.flip(value, HOPS[0][level], HOPS[1][level])

    def across(self, value):
        return self.flip(value, CORE, CORE)

    def scatter_small(self, table):
        return jnp.sum(lax.all_to_all(table, self.axes, 0, 0, tiled=True), 0)


def place_kernel(meta, *refs):
    pieces, beside, out_ref = refs[:4], refs[4:-1], refs[-1]
    columns = pieces[0].shape[1]
    for k in range(4):
        out_ref[meta[5] ^ k, :, :columns] = pieces[k][...]
        if beside:
            out_ref[meta[5] ^ k, :, columns:] = beside[k][...]


def place_group(meta, pieces, beside):
    rows = pieces[0].shape[0]
    operands = list(pieces) + list(beside)
    columns = sum(part[0].shape[1] for part in (pieces, beside) if part)
    whole = lambda n, meta: (0, 0)
    return pl.pallas_call(
        place_kernel,
        grid_spec=pltpu.PrefetchScalarGridSpec(
            num_scalar_prefetch=1, grid=(1,), in_specs=[pl.BlockSpec(part.shape, whole) for part in operands],
            out_specs=pl.BlockSpec((4, rows, columns), lambda n, meta: (0, 0, 0))),
        out_shape=jax.ShapeDtypeStruct((4, rows, columns), pieces[0].dtype),
        cost_estimate=cost(2),
        name="place_group",
    )(meta, *operands)


def spread_kernel(meta, *refs):
    parts, outs = refs[:16], refs[16:]
    for k in range(4):
        total = sum(part[...].astype(F32) for part in parts[4 * k : 4 * k + 4])
        outs[k][...] = total.astype(outs[k].dtype)


def spread_sums(meta, keep, near, third, second):
    _, rows, columns = second.shape
    tile = columns // PARTS
    specs, operands = [], []
    for k in range(4):
        group = pl.BlockSpec((None, rows, tile), lambda n, meta, k=k: (meta[5] ^ k, 0, n))
        pair = pl.BlockSpec((None, None, rows, tile), lambda n, meta, k=k: (0, meta[5] ^ k, 0, n))
        specs += [pair, pair, pair, group]
        operands += [keep, near, third, second]
    out = pl.BlockSpec((rows, tile), lambda n, meta: (0, n))
    return pl.pallas_call(
        spread_kernel,
        grid_spec=pltpu.PrefetchScalarGridSpec(num_scalar_prefetch=1, grid=(columns // tile,), in_specs=specs, out_specs=[out] * 4),
        out_shape=[jax.ShapeDtypeStruct((rows, columns), F32)] + [jax.ShapeDtypeStruct((rows, columns), BF16)] * 3,
        cost_estimate=cost(3),
        name="spread_sums",
    )(meta, *operands)


class Gather:
    def __init__(self, ladder, shard, direct, beside=None):
        self.beside = beside
        self.ladder, self.shard, self.native, self.direct = ladder, shard, ladder.native, direct
        self.sent, self.others = (), []

    def start(self, *after):
        if not self.native:
            self.shard = tie(self.shard, *after)
            self.sent = (self.shard,)
            bits = Z_HOPS if self.direct else Z_HOPS[1:2]
            self.others = [self.ladder.flip(self.shard, bit, bit) for bit in bits]
            self.sides = []
            if self.beside is not None:
                beside = tie(self.beside, self.others[0])
                self.sides = [beside] + [self.ladder.flip(beside, bit, bit) for bit in bits]

    def low(self, *after):
        if not self.native:
            one, two = tie(self.others[0], *after), self.shard
            high = (self.ladder.meta[5] >> 1) == 1
            self.pair = jnp.where(high, jnp.stack([one, two]), jnp.stack([two, one]))
            self.sent = (self.pair,)
            self.others = [self.ladder.flip(self.pair, Z_HOPS[0], Z_HOPS[0])]

    def plane(self, *after):
        if not self.native:
            others = [tie(other, *after) for other in self.others]
            if self.direct:
                self.own = place_group(self.ladder.meta, [self.shard] + others, self.sides)
            else:
                one, two = others[0], self.pair
                low = (self.ladder.meta[5] & 1) == 1
                own = jnp.where(low, jnp.stack([one, two], 1), jnp.stack([two, one], 1))
                self.own = own.reshape((4,) + self.shard.shape)
            self.sent = (self.own,)
            self.second = self.ladder.step(self.own, 2)
            self.third = self.ladder.step(self.own, 3)
            self.far = [self.ladder.across(self.own)]

    def corner(self, *after):
        if not self.native:
            self.second, self.third = tie(self.second, *after), tie(self.third, *after)
            self.sent = (self.second, self.third)
            self.fourth = self.ladder.step(self.second, 3)
            self.far += [self.ladder.across(self.third), self.ladder.across(self.second)]

    def finish(self, *after):
        if self.native:
            self.groups = [lax.all_gather(self.shard, self.ladder.axes, axis=0, tiled=True)]
        else:
            self.fourth = tie(self.fourth, *after)
            self.sent = (self.fourth,)
            self.far += [self.ladder.across(self.fourth)]
            self.groups = [self.own, self.second, self.third, self.fourth] + self.far
        return self.groups


class Scatter:
    def __init__(self, ladder, parts):
        self.ladder, self.native, self.parts = ladder, ladder.native, parts
        self.sent = ()
        if not self.native:
            self.keep = parts[0]
            self.near = ladder.across(parts[1])

    def corner(self, *after):
        if not self.native:
            self.near = tie(self.near, *after)
            total = add_up(self.keep[2:], self.near[2:]).astype(BF16)
            self.sent = (total,)
            self.third = self.ladder.step(total, 3)

    def plane(self, *after):
        if not self.native:
            self.third = tie(self.third, *after)
            total = add_up(self.keep[1], self.near[1], self.third[1]).astype(BF16)
            self.sent = (total,)
            self.second = self.ladder.step(total, 2)

    def spread(self, *after):
        if not self.native:
            second = tie(self.second, *after)
            self.mine, *away = spread_sums(self.ladder.meta, self.keep, self.near, self.third, second)
            self.sent = tuple(away)
            self.last = [self.ladder.flip(part, bit, bit) for part, bit in zip(away, Z_HOPS)]

    def finish(self, *after):
        if self.native:
            return lax.psum_scatter(self.parts[0].astype(F32), self.ladder.axes, scatter_dimension=0, tiled=True)
        total = add_up(self.mine, *[tie(part, *after) for part in self.last])
        self.sent = (total,)
        return total


def nt(a, b):
    return lax.dot_general(a, b, (((1,), (1,)), ((), ())), preferred_element_type=F32)


def nn(a, b):
    return lax.dot_general(a, b, (((1,), (0,)), ((), ())), preferred_element_type=F32)


def fill_bias(lo_ref, segc_ref, padc_ref, segr_ref, bias_ref, nblocks, most):
    def one(qb, _):
        lo = lo_ref[qb]
        q0 = pl.multiple_of(qb * QB, QB)
        segq = segr_ref[pl.ds(qb, 1), :]
        qpos = q0 + lax.broadcasted_iota(jnp.int32, (QB, QB), 1)

        def part(j, _):
            k0 = pl.multiple_of((lo + j) * QB, QB)
            kpos = k0 + lax.broadcasted_iota(jnp.int32, (QB, QB), 0)
            segk = segc_ref[pl.ds(k0, QB), :]
            padk = padc_ref[pl.ds(k0, QB), :]
            ok = (segk == segq) & (kpos <= qpos) & ((padk == 1) | (kpos == qpos))
            bias_ref[qb, pl.ds(pl.multiple_of(j * QB, QB), QB), :] = jnp.where(ok, 0.0, -1e30)
            return 0

        lax.fori_loop(0, qb - lo + 1, part, 0)
        return 0

    lax.fori_loop(0, nblocks, one, 0)


def head_pair(x, scale):
    lane = lax.broadcasted_iota(jnp.int32, x.shape, 1)
    first = jnp.where(lane < HD, scale, 0.0).astype(x.dtype)
    second = jnp.where(lane < HD, 0.0, scale).astype(x.dtype)
    return jnp.concatenate([x * first, x * second], 0)


def attn_fwd_kernel(nblocks, most, many, lo_ref, segc_ref, padc_ref, segr_ref, q_ref, k_ref, v_ref, o_ref, lse_ref, bias_ref, vt_ref):
    @pl.when(pl.program_id(0) == 0)
    def _():
        fill_bias(lo_ref, segc_ref, padc_ref, segr_ref, bias_ref, nblocks, most)

    vt_ref[...] = v_ref[...].T

    def block(qb, _):
        lo = lo_ref[qb]
        q0 = pl.multiple_of(qb * QB, QB)
        k0 = pl.multiple_of(lo * QB, QB)
        for n in range(1, most + 1):
            @pl.when(qb - lo + 1 == n)
            def _(n=n):
                w = n * QB
                bias = bias_ref[qb, 0:w, :]
                bias = jnp.concatenate([bias, bias], 1)
                cols = [slice(128 * i, 128 * (i + 1)) for i in range(many)]
                scores = [nt(k_ref[pl.ds(k0, w), c], head_pair(q_ref[pl.ds(q0, QB), c], HD ** -0.5)) + bias for c in cols]
                tops = [jnp.max(s, 0, keepdims=True) for s in scores]
                parts = [jnp.exp(s - m) for s, m in zip(scores, tops)]
                totals = [jnp.sum(p, 0, keepdims=True) for p in parts]
                outs = [nn(vt_ref[c, pl.ds(k0, w)], (p * (1.0 / t)).astype(BF16)) for c, p, t in zip(cols, parts, totals)]
                for i, (c, o, m, t) in enumerate(zip(cols, outs, tops, totals)):
                    o = jnp.concatenate([o[:HD, :QB], o[HD:, QB:]], 0)
                    o_ref[pl.ds(q0, QB), c] = o.T.astype(BF16)
                    lse_ref[i, pl.ds(qb, 1), :] = m + jnp.log(t)
        return 0

    lax.fori_loop(0, nblocks, block, 0)


def attn_bwd_kernel(nblocks, most, many, lo_ref, segc_ref, padc_ref, segr_ref, q_ref, k_ref, v_ref, do_ref, lse_ref,
                    out_ref, sums_ref, bias_ref, kt_ref, dk_acc, dv_acc):
    @pl.when(pl.program_id(0) == 0)
    def _():
        fill_bias(lo_ref, segc_ref, padc_ref, segr_ref, bias_ref, nblocks, most)

    kt_ref[...] = k_ref[...].T
    dk_acc[...] = jnp.zeros_like(dk_acc)
    dv_acc[...] = jnp.zeros_like(dv_acc)
    sums_ref[...] = jnp.zeros_like(sums_ref)

    def block(qb, _):
        lo = lo_ref[qb]
        q0 = pl.multiple_of(qb * QB, QB)
        k0 = pl.multiple_of(lo * QB, QB)
        for n in range(1, most + 1):
            @pl.when(qb - lo + 1 == n)
            def _(n=n):
                w = n * QB
                bias = bias_ref[qb, 0:w, :]
                bias = jnp.concatenate([bias, bias], 1)
                cols = [slice(128 * i, 128 * (i + 1)) for i in range(many)]
                rows, keys = pl.ds(q0, QB), pl.ds(k0, w)
                q2 = [head_pair(q_ref[rows, c], HD ** -0.5) for c in cols]
                do2 = [head_pair(do_ref[rows, c], 1.0) for c in cols]
                probs = [jnp.exp(nt(k_ref[keys, c], q) + bias - lse_ref[i, pl.ds(qb, 1), :]) for i, (c, q) in enumerate(zip(cols, q2))]
                dprobs = [nt(v_ref[keys, c], do) for c, do in zip(cols, do2)]
                inner = [jnp.sum(p * dp, 0, keepdims=True) for p, dp in zip(probs, dprobs)]
                ds = [(p * (dp - i)).astype(BF16) for p, dp, i in zip(probs, dprobs, inner)]
                for c, p, d, q, do in zip(cols, probs, ds, q2, do2):
                    dv_acc[keys, c] += nn(p.astype(BF16), do)
                    dk_acc[keys, c] += nn(d, q)
                    dq = nn(kt_ref[c, keys], d)
                    dq = jnp.concatenate([dq[:HD, :QB], dq[HD:, QB:]], 0) * (HD ** -0.5)
                    dq = dq.T.astype(BF16)
                    out_ref[0, rows, c] = dq
                    sums_ref[0:1, c] += jnp.sum(dq.astype(F32), 0, keepdims=True)
        return 0

    lax.fori_loop(0, nblocks, block, 0)
    out_ref[1] = dk_acc[...].astype(BF16)
    dv = dv_acc[...].astype(BF16)
    out_ref[2] = dv
    sums_ref[1:2, :] = jnp.sum(dv.astype(F32), 0, keepdims=True)


def mask_inputs(segment_ids, padding_mask):
    length = segment_ids.shape[0]
    nblocks = length // QB
    first = segment_ids.reshape(nblocks, QB)[:, 0]
    start = jnp.sum((segment_ids[None, :] < first[:, None]).astype(jnp.int32), 1)
    lo = start // QB
    segc = jnp.broadcast_to(segment_ids[:, None], (length, QB))
    padc = jnp.broadcast_to(padding_mask[:, None], (length, QB))
    return lo.astype(jnp.int32), segc, padc, segment_ids.reshape(nblocks, QB)


def attn_call(kernel, name, each, operands, specs, shapes, out_specs, scratch, masks, first, pairs, before):
    lo, segc, padc, segr = masks
    length = segc.shape[0]
    nblocks = length // QB
    most = min(nblocks, SPAN // QB + 1)
    whole = lambda p, lo: (0, 0)
    in_specs = [pl.BlockSpec((length, QB), whole), pl.BlockSpec((length, QB), whole), pl.BlockSpec((nblocks, QB), whole)] + specs
    arguments = [lo, segc, padc, segr] + operands
    aliases = {}
    if before is not None:
        aliases = {len(arguments) + i: i for i in range(len(before))}
        in_specs, arguments = in_specs + [pl.BlockSpec(memory_space=pl.ANY)] * len(before), arguments + list(before)

    def body(*refs):
        inputs, rest = refs[: len(arguments) - len(aliases)], refs[len(arguments) :]
        kernel(nblocks, most, MANY, *inputs, *rest)

    return pl.pallas_call(
        body,
        grid_spec=pltpu.PrefetchScalarGridSpec(
            num_scalar_prefetch=1, grid=(pairs // MANY,), in_specs=in_specs, out_specs=out_specs,
            scratch_shapes=[pltpu.VMEM((nblocks, most * QB, QB), F32)] + scratch),
        out_shape=shapes,
        input_output_aliases=aliases,
        compiler_params=pltpu.CompilerParams(vmem_limit_bytes=48 << 20),
        cost_estimate=cost(each * pairs),
        name=name,
    )(*arguments)


def attn_forward(q, k, v, masks, first, pairs, before=None):
    (qa, qo), (ka, ko), (va, vo) = q, k, v
    length, width = qa.shape[0], 128 * MANY
    at = first // MANY
    col = lambda off: pl.BlockSpec((length, width), lambda p, lo: (0, off // MANY + at + p))
    stat = pl.BlockSpec((MANY, length // QB, 2 * QB), lambda p, lo: (at + p, 0, 0))
    total = ko - qo
    return attn_call(
        attn_fwd_kernel, "attn_forward", 2.7, [qa, ka, va], [col(qo), col(ko), col(vo)],
        [jax.ShapeDtypeStruct((length, 128 * total), BF16), jax.ShapeDtypeStruct((total, length // QB, 2 * QB), F32)],
        [col(0), stat], [pltpu.VMEM((width, length), BF16)], masks, first, pairs, before)


def attn_backward(q, k, v, do, lse, masks, first, pairs, before=None):
    (qa, qo), (ka, ko), (va, vo) = q, k, v
    length, width = qa.shape[0], 128 * MANY
    at = first // MANY
    col = lambda off: pl.BlockSpec((length, width), lambda p, lo: (0, off // MANY + at + p))
    stat = pl.BlockSpec((MANY, length // QB, 2 * QB), lambda p, lo: (at + p, 0, 0))
    total = ko - qo
    return attn_call(
        attn_bwd_kernel, "attn_backward", 3.4, [qa, ka, va, do, lse], [col(qo), col(ko), col(vo), col(0), stat],
        [jax.ShapeDtypeStruct((3, length, 128 * total), BF16), jax.ShapeDtypeStruct((8, 128 * total), F32)],
        [pl.BlockSpec((3, length, width), lambda p, lo: (0, 0, at + p)), pl.BlockSpec((8, width), lambda p, lo: (0, at + p))],
        [pltpu.VMEM((width, length), BF16), pltpu.VMEM((length, width), F32), pltpu.VMEM((length, width), F32)],
        masks, first, pairs, before)


ANY = pl.BlockSpec(memory_space=pl.ANY)
META = 1


def params(megabytes=56):
    return pltpu.CompilerParams(vmem_limit_bytes=megabytes << 20)


def tile_shape(native, rows, columns):
    return (1, 1, 1, rows, columns) if native else (4, 4, 2, rows // 32, columns)


def fetch_columns(native, meta, groups, target, start, columns, sem):
    cols = pl.ds(start, columns)
    if native:
        pltpu.make_async_copy(groups[0].at[:, cols], target.at[0, 0, 0], sem).start()
        return
    core = meta[4]
    for t in range(4):
        pltpu.make_async_copy(groups[t].at[:, :, cols], target.at[meta[t], :, core], sem).start()
        pltpu.make_async_copy(groups[4 + t].at[:, :, cols], target.at[meta[t], :, 1 - core], sem).start()


def quarter_shape(native, rows, columns):
    return (1, 1, rows // 4, columns) if native else (4, 2, rows // 32, columns)


def fetch_quarter(native, meta, groups, target, t, sem):
    cols = pl.ds(0, target.shape[-1])
    if native:
        rows = target.shape[-2]
        pltpu.make_async_copy(groups[0].at[pl.ds(t * rows, rows), cols], target.at[0, 0], sem).start()
        return
    core = meta[4]
    pltpu.make_async_copy(groups[t].at[:, :, cols], target.at[:, core], sem).start()
    pltpu.make_async_copy(groups[4 + t].at[:, :, cols], target.at[:, 1 - core], sem).start()


def arrive(target, sem):
    pltpu.make_async_copy(target, target, sem).wait()


def group_specs(groups):
    return [ANY] * len(groups)


def flat(value):
    return value.reshape(-1, value.shape[-1])


def out_blocks(native, rows, columns):
    if native:
        return [jax.ShapeDtypeStruct((rows, columns), BF16)]
    return [jax.ShapeDtypeStruct((4, 4, rows // 32, columns), BF16)] * 2


def push_columns(native, meta, stage, outs, start, columns, sem):
    cols = pl.ds(start, columns)
    if native:
        pltpu.make_async_copy(stage.at[0, 0, 0], outs[0].at[:, cols], sem).start()
        return
    core = meta[4]
    for t in range(4):
        pltpu.make_async_copy(stage.at[meta[t], :, core], outs[0].at[t, :, :, cols], sem).start()
        pltpu.make_async_copy(stage.at[meta[t], :, 1 - core], outs[1].at[FLIP[t], :, :, cols], sem).start()


def each_rows(total, rows, body):
    def step(i, _):
        body(i, pl.ds(pl.multiple_of(i * rows, rows), rows))
        return 0

    lax.fori_loop(0, total // rows, step, 0)


def squares(values, valid):
    return jnp.sum(values * values * valid, 0, keepdims=True)


def scale_of(values):
    return lax.rsqrt(jnp.mean(values * values, -1, keepdims=True) + 1e-05)


SMALL = 16


def pack_smalls(bias_up, bias_qv, bias_out, gain_attn, gain_mlp, bias_down, rows):
    at = lax.broadcasted_iota(jnp.int32, (rows, 128), 0)
    block = jnp.zeros((rows, 128), bias_up.dtype)
    for row, part in enumerate((bias_up, bias_qv, bias_out, gain_attn, gain_mlp, bias_down)):
        block = jnp.where(at == row, jnp.pad(part, (0, 128 - part.shape[0]))[None], block)
    return block


def unpack_smalls(held, up_ref, qkv_ref, lines_ref):
    width = lines_ref.shape[1]
    for shard in range(32):
        up_ref[0:1, shard * 128 : (shard + 1) * 128] = held[shard, 0:1].astype(F32)
    halves = held[...].astype(F32).reshape(16, 2, SMALL, 128)
    halves = halves[:, 0] + pltpu.roll(halves[:, 1], 64, 2)
    fours = held[...].astype(F32).reshape(8, 4, SMALL, 128)
    fours = fours[:, 0] + sum(pltpu.roll(fours[:, i], 32 * i, 2) for i in range(1, 4))
    qkv_ref[...] = jnp.zeros_like(qkv_ref)
    for i in range(16):
        first = i * 128 + (width if i >= 8 else 0)
        qkv_ref[0:1, first : first + 128] = halves[i, 1:2]
    for i in range(8):
        lines_ref[0:4, i * 128 : (i + 1) * 128] = fours[i, 2:6]


def project_kernel(native, tile, count, meta, tok_ref, valid_ref, *rest):
    groups, rest = rest[:count], rest[count:]
    if native:
        up_in, qkv_in, lines_in, out_ref, normed_ref, sq_ref, weight, sems = rest
    else:
        out_ref, normed_ref, sq_ref, up_ref, lines_ref, weight, held, qkv_in, sems = rest
        lines_in = lines_ref
    n, steps = pl.program_id(0), pl.num_programs(0)
    columns = steps * tile

    @pl.when(n == 0)
    def _():
        if not native:
            last = pl.ds(columns, 128)
            for t in range(4):
                for first, side in ((0, meta[4]), (4, 1 - meta[4])):
                    source = groups[first + t].at[:, pl.ds(0, SMALL), last]
                    pltpu.make_async_copy(source, held.at[meta[t], :, side], sems.at[2]).start()
        fetch_columns(native, meta, groups, weight.at[0], 0, tile, sems.at[0])

    @pl.when(n + 1 < steps)
    def _():
        slot = (n + 1) % 2
        fetch_columns(native, meta, groups, weight.at[slot], pl.multiple_of((n + 1) * tile, tile), tile, sems.at[slot])

    @pl.when(n == 0)
    def _():
        if not native:
            arrive(held, sems.at[2])
            unpack_smalls(held[...].reshape(32, SMALL, 128), up_ref, qkv_in, lines_ref)
        sq_ref[...] = jnp.zeros_like(sq_ref)

        def norm(i, at):
            frames = tok_ref[at, :].astype(F32)
            sq_ref[...] += squares(frames, valid_ref[at, :])
            normed_ref[at, :] = (frames * scale_of(frames) * lines_in[1:2, :]).astype(BF16)

        each_rows(tok_ref.shape[0], 256, norm)

    arrive(weight.at[n % 2], sems.at[n % 2])
    bias = qkv_in[0:1, pl.ds(pl.multiple_of(n * tile, tile), tile)]
    out_ref[...] = (nn(normed_ref[...], flat(weight[n % 2])) + bias).astype(BF16)


def project(ladder, tokens, valid, groups, known=None):
    length, width = tokens.shape
    columns, tile, hidden = 3 * width, 512, 4 * width
    native = ladder.native
    whole = lambda n, meta: (0, 0)
    up, lines = pl.BlockSpec((1, hidden), whole), pl.BlockSpec((4, width), whole)
    out_specs = [pl.BlockSpec((length, tile), lambda n, meta: (0, n)), pl.BlockSpec((length, width), whole), pl.BlockSpec((1, width), whole)]
    out_shape = [jax.ShapeDtypeStruct((length, columns), BF16), jax.ShapeDtypeStruct((length, width), BF16),
                 jax.ShapeDtypeStruct((1, width), F32)]
    scratch = [pltpu.VMEM((2,) + tile_shape(native, width, tile), BF16)]
    vectors = [jax.ShapeDtypeStruct((1, hidden), F32), jax.ShapeDtypeStruct((4, width), F32)]
    extra = []
    if native:
        extra = [up, pl.BlockSpec((1, columns), whole), lines]
    else:
        out_specs, out_shape = out_specs + [up, lines], out_shape + vectors
        scratch += [pltpu.VMEM((4, 4, 2, SMALL, 128), BF16), pltpu.VMEM((1, columns), F32)]
    results = pl.pallas_call(
        functools.partial(project_kernel, native, tile, len(groups)),
        grid_spec=pltpu.PrefetchScalarGridSpec(
            num_scalar_prefetch=1, grid=(columns // tile,),
            in_specs=[pl.BlockSpec((length, width), whole), pl.BlockSpec((length, 1), whole)] + group_specs(groups) + extra,
            out_specs=out_specs, scratch_shapes=scratch + [pltpu.SemaphoreType.DMA((3,))]),
        out_shape=out_shape,
        compiler_params=params(),
        cost_estimate=cost(14),
        name="project",
    )(ladder.meta, tokens, valid, *groups, *(known or ()))
    return results if not native else list(results) + [known[0], known[2]]


def gelu_pair(u):
    c, d = 0.7978845608028654, 0.044715
    square = u * u
    bend = 0.5 * jnp.tanh(u * (c + c * d * square))
    half = 0.5 + bend
    slope = half * (1.0 + (0.5 - bend) * (u * (2.0 * c + 6.0 * c * d * square)))
    return (u * half).astype(BF16), slope.astype(BF16)


def expand_kernel(native, tile, count, meta, mixed_ref, tok_ref, lines_ref, valid_ref, up_bias_ref, *rest):
    groups, rest = rest[:count], rest[count:]
    middle_ref, normed_ref, sq_ref, act_ref, slope_ref, middle, out_weight, weight, sems = rest
    n, steps = pl.program_id(0), pl.num_programs(0)
    half = out_weight.shape[-1]
    first = 2 * half
    store = pltpu.make_async_copy(middle, middle_ref, sems.at[4])

    @pl.when(n == 0)
    def _():
        for side in range(2):
            fetch_columns(native, meta, groups, out_weight.at[side], side * half, half, sems.at[2 + side])
        fetch_columns(native, meta, groups, weight.at[0], first, tile, sems.at[0])

    @pl.when(n + 1 < steps)
    def _():
        slot = (n + 1) % 2
        fetch_columns(native, meta, groups, weight.at[slot], pl.multiple_of(first + (n + 1) * tile, tile), tile, sems.at[slot])

    @pl.when(n == 0)
    def _():
        for side in range(2):
            arrive(out_weight.at[side], sems.at[2 + side])
        sq_ref[...] = jnp.zeros_like(sq_ref)

        def part(i, at):
            branch = jnp.concatenate([nn(mixed_ref[at, :], flat(out_weight[side])) for side in range(2)], 1) + lines_ref[0:1, :]
            total = tok_ref[at, :].astype(F32) + branch
            middle[at, :] = total
            normed_ref[at, :] = (total * scale_of(total) * lines_ref[2:3, :]).astype(BF16)
            sq_ref[0:1, :] += squares(branch, valid_ref[at, :])
            sq_ref[1:2, :] += squares(total, valid_ref[at, :])

        each_rows(middle.shape[0], 256, part)
        store.start()

    arrive(weight.at[n % 2], sems.at[n % 2])
    act_ref[...], slope_ref[...] = gelu_pair(nn(normed_ref[...], flat(weight[n % 2])) + up_bias_ref[...])

    @pl.when(n == steps - 1)
    def _():
        store.wait()


def expand(ladder, mixed, tokens, lines, valid, up_bias, groups):
    length, width = tokens.shape
    columns, tile = up_bias.shape[1], 512
    whole = lambda n, meta: (0, 0)
    column = lambda n, meta: (0, n)
    square = pl.BlockSpec((length, width), whole)
    return pl.pallas_call(
        functools.partial(expand_kernel, ladder.native, tile, len(groups)),
        grid_spec=pltpu.PrefetchScalarGridSpec(
            num_scalar_prefetch=1, grid=(columns // tile,),
            in_specs=[square, square, pl.BlockSpec((4, width), whole), pl.BlockSpec((length, 1), whole), pl.BlockSpec((1, tile), column)]
            + group_specs(groups),
            out_specs=[ANY, square, pl.BlockSpec((8, width), whole), pl.BlockSpec((length, tile), column),
                       pl.BlockSpec((length, tile), column)],
            scratch_shapes=[pltpu.VMEM((length, width), F32),
                            pltpu.VMEM((2,) + tile_shape(ladder.native, width, width // 2), BF16),
                            pltpu.VMEM((2,) + tile_shape(ladder.native, width, tile), BF16), pltpu.SemaphoreType.DMA((5,))]),
        out_shape=[jax.ShapeDtypeStruct((length, width), F32), jax.ShapeDtypeStruct((length, width), BF16),
                   jax.ShapeDtypeStruct((8, width), F32)] + [jax.ShapeDtypeStruct((length, columns), BF16)] * 2,
        compiler_params=params(),
        cost_estimate=cost(29),
        name="expand",
    )(ladder.meta, mixed, tokens, lines, valid, up_bias, *groups)


def fetch_turn(native, meta, groups, weight, sems, t, first=0, last=3):
    for at in range(first, last + 1):
        @pl.when(t == max(at - 1, first))
        def _(at=at):
            fetch_quarter(native, meta, groups, weight.at[at % 2], at, sems.at[at % 2])

    arrive(weight.at[t % 2], sems.at[t % 2])


def tn(a, b):
    return lax.dot_general(a, b, (((0,), (0,)), ((), ())), preferred_element_type=F32)


def down_grad_kernel(native, count, meta, act_ref, cot_ref, *rest):
    outs, (sum_ref, stage, sems) = rest[:count], rest[count:]
    t = pl.program_id(0)
    slot = t % 2

    @pl.when(t >= 2)
    def _():
        arrive(stage.at[slot], sems.at[slot])

    stage[slot] = tn(act_ref[...], cot_ref[...]).astype(BF16).reshape(stage.shape[1:])
    if native:
        rows = stage.shape[-2]
        pltpu.make_async_copy(stage.at[slot, 0, 0], outs[0].at[pl.ds(t * rows, rows), :], sems.at[slot]).start()
    else:
        for k in range(4):
            @pl.when(t == k)
            def _(k=k):
                pltpu.make_async_copy(stage.at[slot, :, meta[4]], outs[0].at[k], sems.at[slot]).start()
                pltpu.make_async_copy(stage.at[slot, :, 1 - meta[4]], outs[1].at[FLIP[k]], sems.at[slot]).start()

    @pl.when(t == 0)
    def _():
        sum_ref[...] = jnp.sum(cot_ref[...].astype(F32), 0, keepdims=True)

    @pl.when(t == 3)
    def _():
        arrive(stage.at[1 - slot], sems.at[1 - slot])
        arrive(stage.at[slot], sems.at[slot])


def down_grad(ladder, act, cot):
    length, width = cot.shape
    hidden = act.shape[1]
    outs = out_blocks(ladder.native, hidden, width)
    whole = lambda t, meta: (0, 0)
    return pl.pallas_call(
        functools.partial(down_grad_kernel, ladder.native, len(outs)),
        grid_spec=pltpu.PrefetchScalarGridSpec(
            num_scalar_prefetch=1, grid=(4,),
            in_specs=[pl.BlockSpec((length, hidden // 4), lambda t, meta: (0, meta[t])), pl.BlockSpec((length, width), whole)],
            out_specs=[ANY] * len(outs) + [pl.BlockSpec((1, width), whole)],
            scratch_shapes=[pltpu.VMEM((2,) + quarter_shape(ladder.native, hidden, width), BF16), pltpu.SemaphoreType.DMA((2,))]),
        out_shape=outs + [jax.ShapeDtypeStruct((1, width), F32)],
        compiler_params=params(),
        cost_estimate=cost(14),
        name="down_grad",
    )(ladder.meta, act, cot)


def row_grad_kernel(native, tile, count, meta, left_ref, right_ref, *rest):
    outs, (stage, sems) = rest[:count], rest[count:]
    n, steps = pl.program_id(0), pl.num_programs(0)
    slot = n % 2

    @pl.when(n >= 2)
    def _():
        arrive(stage.at[slot], sems.at[slot])

    stage[slot] = tn(left_ref[...], right_ref[...]).astype(BF16).reshape(stage.shape[1:])
    push_columns(native, meta, stage.at[slot], outs, pl.multiple_of(n * tile, tile), tile, sems.at[slot])

    @pl.when(n == steps - 1)
    def _():
        arrive(stage.at[1 - slot], sems.at[1 - slot])
        arrive(stage.at[slot], sems.at[slot])


def row_grad(ladder, left, right, name):
    length, width = left.shape
    parts, _, each = right.shape
    tile = 512
    per = each // tile
    outs = out_blocks(ladder.native, width, parts * each)
    return pl.pallas_call(
        functools.partial(row_grad_kernel, ladder.native, tile, len(outs)),
        grid_spec=pltpu.PrefetchScalarGridSpec(
            num_scalar_prefetch=1, grid=(parts * per,),
            in_specs=[pl.BlockSpec((length, width), lambda n, meta: (0, 0)),
                      pl.BlockSpec((None, length, tile), lambda n, meta: (n // per, 0, n % per))],
            out_specs=[ANY] * len(outs),
            scratch_shapes=[pltpu.VMEM((2,) + tile_shape(ladder.native, width, tile), BF16), pltpu.SemaphoreType.DMA((2,))]),
        out_shape=outs,
        compiler_params=params(),
        cost_estimate=cost(8),
        name=name,
    )(ladder.meta, left, right)


def norm_grad(grad, source, gain):
    r = scale_of(source)
    hat = source * r
    gain_grad = jnp.sum(grad * hat, 0, keepdims=True)
    scaled = grad * gain
    return r * (scaled - hat * jnp.mean(scaled * hat, -1, keepdims=True)), gain_grad


def back_kernel(native, last, counts, meta, cot_ref, slope_ref, normed_ref, lines_ref, middle_ref, mixed_ref, *rest):
    down_groups, rest = rest[: counts[0]], rest[counts[0] :]
    groups, rest = rest[: counts[0]], rest[counts[0] :]
    if last:
        before, rest = rest[0], rest[1 + counts[1] :]
    pushed, rest = rest[: counts[1]], rest[counts[1] :]
    if last:
        out_ref, branch_ref, mixed_out_ref, sum_ref, up_sum_ref, rest = *rest[:5], rest[5:]
        acc, down_weight, weight, stage, sems, middle, out_weight = rest
    else:
        after, up_sum_ref, acc, down_weight, weight, stage, sems = rest
    base = 2 if last else 0
    step = pl.program_id(0)
    t = step + base
    width, tile = normed_ref.shape[1], slope_ref.shape[1]
    slot = step

    def columns(at):
        return pl.multiple_of(width + meta[at] * tile, 512)

    @pl.when(step == 0)
    def _():
        for at in range(2):
            fetch_columns(native, meta, groups, weight.at[at], columns(base + at), tile, sems.at[2 + at])
        if last:
            pltpu.make_async_copy(before, acc, sems.at[6]).start()
            pltpu.make_async_copy(middle_ref, middle, sems.at[7]).start()
            fetch_columns(native, meta, groups, out_weight, 0, width, sems.at[8])

    fetch_turn(native, meta, down_groups, down_weight, sems, t, base, base + 1)
    length = acc.shape[0]
    grad = (nt(cot_ref[...], flat(down_weight[t % 2])) * slope_ref[...].astype(F32)).astype(BF16)
    up_sum_ref[...] = jnp.sum(grad.astype(F32), 0, keepdims=True)
    stage[slot] = tn(normed_ref[...], grad).astype(BF16).reshape(stage.shape[1:])
    push_columns(native, meta, stage.at[slot], pushed, columns(t), tile, sems.at[4 + slot])
    arrive(weight.at[slot], sems.at[2 + slot])
    product = nt(grad, flat(weight[slot]))

    @pl.when(step == 0)
    def _():
        if last:
            pltpu.make_async_copy(before, acc, sems.at[6]).wait()
            acc[...] += product
        else:
            acc[...] = product

    @pl.when(step == 1)
    def _():
        acc[...] += product
        if last:
            pltpu.make_async_copy(middle_ref, middle, sems.at[7]).wait()
            sum_ref[...] = jnp.zeros_like(sum_ref)

            def part(i, at):
                back, gain_grad = norm_grad(acc[at, :], middle[at, :], lines_ref[2:3, :])
                total = cot_ref[at, :].astype(F32) + back
                acc[at, :] = total
                branch = total.astype(BF16)
                branch_ref[at, :] = branch
                sum_ref[0:1, :] += gain_grad
                sum_ref[1:2, :] += jnp.sum(branch.astype(F32), 0, keepdims=True)

            each_rows(length, 256, part)
            pltpu.make_async_copy(acc, out_ref, sems.at[6]).start()
            arrive(stage.at[0], sems.at[4])
            stage[0] = tn(mixed_ref[...], branch_ref[...]).astype(BF16).reshape(stage.shape[1:])
            push_columns(native, meta, stage.at[0], pushed, 0, width, sems.at[4])
            arrive(out_weight, sems.at[8])
            mixed_out_ref[...] = nt(branch_ref[...], flat(out_weight[...])).astype(BF16)
            pltpu.make_async_copy(acc, out_ref, sems.at[6]).wait()
        else:
            pltpu.make_async_copy(acc, after, sems.at[6]).start()
            pltpu.make_async_copy(acc, after, sems.at[6]).wait()
        for at in range(2):
            arrive(stage.at[at], sems.at[4 + at])


def back(ladder, cot, slope, normed, lines, middle, mixed, down_groups, groups, before=None):
    length, width = cot.shape
    hidden, tile = slope.shape[1], slope.shape[1] // 4
    last = before is not None
    base = 2 if last else 0
    whole = lambda t, meta: (0, 0)
    part = lambda t, meta: (0, meta[t + base])
    square = pl.BlockSpec((length, width), whole)
    once = pl.BlockSpec((length, width), whole, pipeline_mode=pl.Buffered(1))
    outs = out_blocks(ladder.native, width, hidden + width)
    counts = (len(groups), len(outs))
    full, wide = jax.ShapeDtypeStruct((length, width), F32), jax.ShapeDtypeStruct((length, width), BF16)
    sums = jax.ShapeDtypeStruct((1, hidden), F32)
    in_specs = [once, pl.BlockSpec((length, tile), part), once, pl.BlockSpec((4, width), whole), ANY, once if last else ANY]
    in_specs += [ANY] * (2 * counts[0])
    operands = [ladder.meta, cot, slope, normed, lines, middle, mixed, *down_groups, *groups]
    scratch = [pltpu.VMEM((length, width), F32), pltpu.VMEM((2,) + quarter_shape(ladder.native, hidden, width), BF16),
               pltpu.VMEM((2,) + tile_shape(ladder.native, width, tile), BF16),
               pltpu.VMEM((2,) + tile_shape(ladder.native, width, tile), BF16), pltpu.SemaphoreType.DMA((9,))]
    aliases = {}
    if last:
        aliases = {len(operands) + 1 + i: i for i in range(counts[1])}
        operands += list(before)
        in_specs += [ANY] * (1 + counts[1])
        out_specs = [ANY] * counts[1] + [ANY, square, square, pl.BlockSpec((8, width), whole)]
        out_shape = outs + [full, wide, wide, jax.ShapeDtypeStruct((8, width), F32)]
        scratch += [pltpu.VMEM((length, width), F32), pltpu.VMEM(tile_shape(ladder.native, width, width), BF16)]
    else:
        out_specs, out_shape = [ANY] * counts[1] + [ANY], outs + [full]
    return pl.pallas_call(
        functools.partial(back_kernel, ladder.native, last, counts),
        grid_spec=pltpu.PrefetchScalarGridSpec(
            num_scalar_prefetch=1, grid=(2,), in_specs=in_specs, out_specs=out_specs + [pl.BlockSpec((1, tile), lambda t, meta: (0, t))],
            scratch_shapes=scratch),
        out_shape=out_shape + [jax.ShapeDtypeStruct((1, hidden // 2), F32)],
        input_output_aliases=aliases,
        compiler_params=params(),
        cost_estimate=cost(30 if last else 20),
        name="back",
    )(*operands)


def contract_kernel(native, first, meta, act_ref, lines_ref, valid_ref, middle_ref, *rest):
    groups, (out_ref, sq_ref, acc, middle, weight, sems) = rest[:-6], rest[-6:]
    t = pl.program_id(0)
    load = pltpu.make_async_copy(middle_ref.at[pl.ds(first, acc.shape[0]), :], middle, sems.at[2])

    @pl.when(t == 0)
    def _():
        load.start()

    fetch_turn(native, meta, groups, weight, sems, t)
    product = nn(act_ref[...], flat(weight[t % 2]))

    @pl.when(t == 0)
    def _():
        acc[...] = product

    @pl.when(t > 0)
    def _():
        acc[...] += product

    @pl.when(t == 3)
    def _():
        load.wait()
        sq_ref[...] = jnp.zeros_like(sq_ref)
        rows = 256

        def part(i, _):
            at = pl.ds(pl.multiple_of(i * rows, rows), rows)
            branch = acc[at, :] + lines_ref[3:4, :]
            final = middle[at, :] + branch
            out_ref[at, :] = final.astype(BF16)
            sq_ref[0:1, :] += squares(branch, valid_ref[at, :])
            sq_ref[1:2, :] += squares(final, valid_ref[at, :])
            return 0

        lax.fori_loop(0, acc.shape[0] // rows, part, 0)


def contract(ladder, act, middle, lines, valid, groups, part, parts):
    length, width = middle.shape
    length //= parts
    hidden = act.shape[1]
    whole = lambda t, meta: (0, 0)
    return pl.pallas_call(
        functools.partial(contract_kernel, ladder.native, part * length),
        grid_spec=pltpu.PrefetchScalarGridSpec(
            num_scalar_prefetch=1, grid=(4,),
            in_specs=[pl.BlockSpec((length, hidden // 4), lambda t, meta: (part, meta[t])), pl.BlockSpec((4, width), whole),
                      pl.BlockSpec((length, 1), lambda t, meta: (part, 0)), ANY] + group_specs(groups),
            out_specs=[pl.BlockSpec((length, width), whole), pl.BlockSpec((8, width), whole)],
            scratch_shapes=[pltpu.VMEM((length, width), F32), pltpu.VMEM((length, width), F32),
                            pltpu.VMEM((2,) + quarter_shape(ladder.native, hidden, width), BF16), pltpu.SemaphoreType.DMA((3,))]),
        out_shape=[jax.ShapeDtypeStruct((length, width), BF16), jax.ShapeDtypeStruct((8, width), F32)],
        compiler_params=params(),
        cost_estimate=cost(16 // parts),
        name="contract",
    )(ladder.meta, act, lines, valid, middle, *groups)


def input_grad_kernel(native, calls, meta, *rest):
    grads, (tok_ref, middle_ref, lines_ref), rest = rest[:calls], rest[calls : calls + 3], rest[calls + 3 :]
    groups, (out_ref, sum_ref, acc, middle, weight, sems) = rest[:-6], rest[-6:]
    t = pl.program_id(0)
    load = pltpu.make_async_copy(middle_ref, middle, sems.at[2])

    @pl.when(t == 0)
    def _():
        load.start()

    fetch_turn(native, meta, groups, weight, sems, t)
    width = acc.shape[1]
    quarter = width // 4
    rows = flat(weight[t % 2])
    each = width // calls
    product = 0.0
    for part in range(3):
        for call in range(calls):
            first = part * width + call * each
            product += nt(grads[call][part], rows[:, first : first + each])
    acc[:, pl.ds(pl.multiple_of(meta[t] * quarter, quarter), quarter)] = product

    @pl.when(t == 3)
    def _():
        load.wait()
        sum_ref[...] = jnp.zeros_like(sum_ref)
        rows = 256

        def part(i, _):
            at = pl.ds(pl.multiple_of(i * rows, rows), rows)
            back, gain_grad = norm_grad(acc[at, :], tok_ref[at, :].astype(F32), lines_ref[1:2, :])
            out_ref[at, :] = (middle[at, :] + back).astype(BF16)
            sum_ref[0:1, :] += gain_grad
            return 0

        lax.fori_loop(0, acc.shape[0] // rows, part, 0)


def input_grad(ladder, grads, tokens, grad_middle, lines, groups):
    length, width = tokens.shape
    calls = len(grads)
    whole = lambda t, meta: (0, 0)
    square = pl.BlockSpec((length, width), whole)
    return pl.pallas_call(
        functools.partial(input_grad_kernel, ladder.native, calls),
        grid_spec=pltpu.PrefetchScalarGridSpec(
            num_scalar_prefetch=1, grid=(4,),
            in_specs=[pl.BlockSpec((3, length, width // calls), lambda t, meta: (0, 0, 0))] * calls + [square, ANY, pl.BlockSpec((4, width), whole)]
            + group_specs(groups),
            out_specs=[square, pl.BlockSpec((8, width), whole)],
            scratch_shapes=[pltpu.VMEM((length, width), F32), pltpu.VMEM((length, width), F32),
                            pltpu.VMEM((2,) + quarter_shape(ladder.native, width, 3 * width), BF16), pltpu.SemaphoreType.DMA((3,))]),
        out_shape=[jax.ShapeDtypeStruct((length, width), BF16), jax.ShapeDtypeStruct((8, width), F32)],
        compiler_params=params(),
        cost_estimate=cost(18),
        name="input_grad",
    )(ladder.meta, *grads, tokens, grad_middle, lines, *groups)


def local(ladder, tokens, cotangent, segment_ids, padding_mask, w_qkv, bias_qv, w_out, bias_out, gain_attn, gain_mlp,
          w_up, bias_up, w_down, bias_down):
    length, width = tokens.shape[1], tokens.shape[2]
    count = ladder.count
    ladder.place()
    tokens, cotangent = tokens[0], cotangent[0]

    def sent(*flows):
        return [value for flow in flows for value in flow.sent]

    sizes = [part.shape[0] for part in (bias_qv, bias_out, gain_attn, gain_mlp, bias_up, bias_down)]
    total = sum(sizes)
    ends = np.cumsum([0] + sizes)
    known = None
    block = None
    if ladder.native:
        every = lambda part: lax.all_gather(part, ladder.axes, axis=0, tiled=True).astype(F32)[None]
        qv = every(bias_qv)
        known = [every(bias_up), jnp.concatenate([qv[:, :width], jnp.zeros((1, width), F32), qv[:, width:]], 1),
                 jnp.concatenate([every(bias_out), every(gain_attn), every(gain_mlp), every(bias_down)], 0)]
    else:
        block = pack_smalls(bias_up, bias_qv, bias_out, gain_attn, gain_mlp, bias_down, w_qkv.shape[0])
    qkv, down = Gather(ladder, w_qkv, True, block), Gather(ladder, w_down, False)
    qkv.start()
    rest = Gather(ladder, jnp.concatenate([w_out, w_up], 1), False)
    masks = mask_inputs(segment_ids[0], padding_mask[0])
    valid = padding_mask[0].astype(F32)[:, None]
    qkv.plane()
    rest.start(*qkv.sent)
    qkv.corner()
    rest.low()
    qkv_groups = qkv.finish()
    rest.plane()
    down.start(*rest.sent)
    projected, normed_in, sq_frames, up_bias, lines = project(ladder, tie(tokens, *sent(rest), *masks, *ladder.tables), valid, qkv_groups, known)
    per = width // 128
    calls = 2
    each = per // calls

    down.low(projected)
    projected = tie(projected, *sent(down))
    per = width // 128
    calls = 2
    each = per // calls

    def triple():
        return (projected, 0), (projected, per), (projected, 2 * per)

    heads = None
    for call in range(calls):
        heads = attn_forward(*triple(), masks, call * each, each, heads)
        if call == 0:
            rest.corner(heads[0])
            projected = tie(projected, heads[0], *sent(rest), *down.others)
    mixed, lse = heads
    rest_groups = rest.finish(mixed)
    down.plane(*rest.sent)
    middle, normed_mid, sq_middle, act, slope = expand(
        ladder, tie(mixed, *sent(down)), tokens, lines, valid, up_bias, rest_groups)

    down.corner(act)
    *down_parts, sum_down = down_grad(ladder, tie(act, *sent(down)), cotangent)
    flow_down = Scatter(ladder, down_parts)
    down_groups = down.finish(sum_down)
    *first_parts, first_acc, first_sum = back(
        ladder, tie(cotangent, sum_down), slope, normed_mid, lines, middle, mixed, down_groups, rest_groups)
    flow_down.corner(first_acc)
    *rest_parts, grad_middle, grad_branch, grad_mixed, sum_middle, second_sum = back(
        ladder, tie(cotangent, *sent(flow_down)), slope, normed_mid, lines, middle, mixed, down_groups, rest_groups,
        [first_acc, *first_parts])
    sum_up = jnp.concatenate([first_sum, second_sum], 1).reshape(4, -1)[ladder.order].reshape(1, -1)
    flow_rest = Scatter(ladder, rest_parts)
    flow_down.plane(grad_mixed)
    grad_mixed = tie(grad_mixed, *sent(flow_down))
    heads = None
    for call in range(calls):
        heads = attn_backward(*triple(), grad_mixed, lse, masks, call * each, each, heads)
        if call == 0:
            flow_down.spread(heads[0])
            flow_rest.corner(heads[0])
            grad_mixed = tie(grad_mixed, heads[0], *sent(flow_down, flow_rest))
    grad_projected, sum_qv = heads
    own_down = flow_down.finish(grad_projected)
    flow_qkv = Scatter(ladder, row_grad(ladder, normed_in, tie(grad_projected, *sent(flow_down)), "qkv_grad"))
    flow_rest.plane(*flow_qkv.parts)
    finals = []

    def finish_rows(part, *after):
        out, squares_out = contract(ladder, tie(act, *after), middle, lines, valid, down_groups, part, 2)
        finals.append(squares_out)
        return out

    outputs = [finish_rows(0, *flow_qkv.parts, *sent(flow_rest))]
    flow_rest.spread(outputs[0])
    flow_qkv.corner(outputs[0])
    tail = tie(tokens, *sent(flow_rest, flow_qkv))
    grad_tokens, sum_in = input_grad(ladder, [grad_projected], tail, grad_middle, lines, qkv_groups)
    flow_qkv.plane(grad_tokens)
    outputs.append(finish_rows(1, *sent(flow_qkv)))
    own_rest = flow_rest.finish(outputs[1])
    flow_qkv.spread(outputs[1], own_rest)
    output = jnp.concatenate(outputs, 0)

    sq_final = finals[0] + finals[1]
    members = [sq_frames, sq_middle[1:2], sq_final[1:2], sq_middle[:1], sq_final[:1], valid.reshape(1, -1)]
    members = jnp.sum(jnp.concatenate(members, 0), 1)
    small_grads = [sum_qv[:2].reshape(-1), sum_middle[1], sum_in[0], sum_middle[0], sum_up[0], sum_down[0]]
    table = jnp.concatenate([g.reshape(count, -1) for g in small_grads] + [jnp.broadcast_to(members, (count, 6))], 1)
    table = jnp.pad(table, ((0, 0), (0, -table.shape[1] % 128)))
    own_small = ladder.scatter_small(tie(table, *sent(flow_qkv)))
    own_qkv = flow_qkv.finish(own_small)

    owned = [own_small[ends[i] : ends[i + 1]] for i in range(6)]
    totals = own_small[total : total + 6]
    stats = jnp.sqrt(totals[:5] / (totals[5] * width))
    own_out, own_up = own_rest[:, :width], own_rest[:, width:]
    return (output[None], grad_tokens[None], own_qkv, owned[0], own_out, owned[1], owned[2], owned[3], own_up, owned[4],
            own_down, owned[5], stats, totals[5:6])


def solution(mesh):
    rows, wide, flat = P(("dp", "fsdp"), None, None), P(("dp", "fsdp"), None), P(("dp", "fsdp"))
    return jax.shard_map(
        functools.partial(local, Ladder(mesh)),
        mesh=mesh,
        in_specs=(rows, rows, wide, wide, wide, flat, wide, flat, flat, flat, wide, flat, wide, flat),
        out_specs=(rows, rows, wide, flat, wide, flat, flat, flat, wide, flat, wide, flat, P(), P()),
        check_vma=False,
    )
```

```python
import functools

import jax
import jax.numpy as jnp
import numpy as np
from jax import lax
from jax.experimental import pallas as pl
from jax.experimental.pallas import tpu as pltpu
from jax.sharding import PartitionSpec as P

HD = 64
QB = 128
SPAN = 512
MANY = 4
WEIGH = 2
PARTS = 1
F32 = jnp.float32
BF16 = jnp.bfloat16

CORE = 1
Z_HOPS = (2, 4, 6)
MIX = ((0, 1, 2, 3), (0, 2, 1, 3))
FLIP = (0, 2, 1, 3)
HOPS = ((4, 2, 8, 16), (4, 2, 16, 8))


def tie(value, *others):
    return lax.optimization_barrier((value,) + others)[0]


def add_up(*terms):
    return sum(term.astype(F32) for term in terms)


def cost(microseconds):
    return pl.CostEstimate(flops=int(WEIGH * microseconds * 1.15e9), transcendentals=0, bytes_accessed=0)


class Ladder:
    def __init__(self, mesh):
        self.count = int(np.prod(list(mesh.shape.values())))
        self.native = dict(mesh.shape) != {"dp": 4, "fsdp": 8}
        self.axes = ("dp", "fsdp")

    def place(self):
        if self.native:
            self.meta = jnp.array([0, 1, 2, 3, 0, 0], jnp.int32)
            return
        me = lax.axis_index(self.axes)
        odd = (me & CORE) == 1
        mix = jnp.where(odd, jnp.array(MIX[1], jnp.int32), jnp.array(MIX[0], jnp.int32))
        self.meta = jnp.concatenate([(me >> 3) ^ mix, (me & CORE)[None], ((me >> 1) & 3)[None]])

    def flip(self, value, even, odd):
        bits = (even, odd)
        return lax.ppermute(value, self.axes, [(i, i ^ bits[i & CORE]) for i in range(self.count)])

    def step(self, value, level):
        return self.flip(value, HOPS[0][level], HOPS[1][level])

    def across(self, value):
        return self.flip(value, CORE, CORE)

    def scatter_small(self, table):
        return jnp.sum(lax.all_to_all(table, self.axes, 0, 0, tiled=True), 0)


def place_kernel(meta, *refs):
    pieces, beside, out_ref = refs[:4], refs[4:-1], refs[-1]
    columns = pieces[0].shape[1]
    for k in range(4):
        out_ref[meta[5] ^ k, :, :columns] = pieces[k][...]
        if beside:
            out_ref[meta[5] ^ k, :, columns:] = beside[k][...]


def place_group(meta, pieces, beside):
    rows = pieces[0].shape[0]
    operands = list(pieces) + list(beside)
    columns = sum(part[0].shape[1] for part in (pieces, beside) if part)
    whole = lambda n, meta: (0, 0)
    return pl.pallas_call(
        place_kernel,
        grid_spec=pltpu.PrefetchScalarGridSpec(
            num_scalar_prefetch=1, grid=(1,), in_specs=[pl.BlockSpec(part.shape, whole) for part in operands],
            out_specs=pl.BlockSpec((4, rows, columns), lambda n, meta: (0, 0, 0))),
        out_shape=jax.ShapeDtypeStruct((4, rows, columns), pieces[0].dtype),
        cost_estimate=cost(2),
        name="place_group",
    )(meta, *operands)


def spread_kernel(meta, *refs):
    parts, outs = refs[:16], refs[16:]
    for k in range(4):
        total = sum(part[...].astype(F32) for part in parts[4 * k : 4 * k + 4])
        outs[k][...] = total.astype(outs[k].dtype)


def spread_sums(meta, keep, near, third, second):
    _, rows, columns = second.shape
    tile = columns // PARTS
    specs, operands = [], []
    for k in range(4):
        group = pl.BlockSpec((None, rows, tile), lambda n, meta, k=k: (meta[5] ^ k, 0, n))
        pair = pl.BlockSpec((None, None, rows, tile), lambda n, meta, k=k: (0, meta[5] ^ k, 0, n))
        specs += [pair, pair, pair, group]
        operands += [keep, near, third, second]
    out = pl.BlockSpec((rows, tile), lambda n, meta: (0, n))
    return pl.pallas_call(
        spread_kernel,
        grid_spec=pltpu.PrefetchScalarGridSpec(num_scalar_prefetch=1, grid=(columns // tile,), in_specs=specs, out_specs=[out] * 4),
        out_shape=[jax.ShapeDtypeStruct((rows, columns), F32)] + [jax.ShapeDtypeStruct((rows, columns), BF16)] * 3,
        cost_estimate=cost(3),
        name="spread_sums",
    )(meta, *operands)


class Gather:
    def __init__(self, ladder, shard, direct, beside=None):
        self.beside = beside
        self.ladder, self.shard, self.native, self.direct = ladder, shard, ladder.native, direct
        self.sent, self.others = (), []

    def start(self, *after):
        if not self.native:
            self.shard = tie(self.shard, *after)
            self.sent = (self.shard,)
            bits = Z_HOPS if self.direct else Z_HOPS[1:2]
            self.others = [self.ladder.flip(self.shard, bit, bit) for bit in bits]
            self.sides = []
            if self.beside is not None:
                beside = tie(self.beside, self.others[0])
                self.sides = [beside] + [self.ladder.flip(beside, bit, bit) for bit in bits]

    def low(self, *after):
        if not self.native:
            one, two = tie(self.others[0], *after), self.shard
            high = (self.ladder.meta[5] >> 1) == 1
            self.pair = jnp.where(high, jnp.stack([one, two]), jnp.stack([two, one]))
            self.sent = (self.pair,)
            self.others = [self.ladder.flip(self.pair, Z_HOPS[0], Z_HOPS[0])]

    def plane(self, *after):
        if not self.native:
            others = [tie(other, *after) for other in self.others]
            if self.direct:
                self.own = place_group(self.ladder.meta, [self.shard] + others, self.sides)
            else:
                one, two = others[0], self.pair
                low = (self.ladder.meta[5] & 1) == 1
                own = jnp.where(low, jnp.stack([one, two], 1), jnp.stack([two, one], 1))
                self.own = own.reshape((4,) + self.shard.shape)
            self.sent = (self.own,)
            self.second = self.ladder.step(self.own, 2)
            self.third = self.ladder.step(self.own, 3)
            self.far = [self.ladder.across(self.own)]

    def corner(self, *after):
        if not self.native:
            self.second, self.third = tie(self.second, *after), tie(self.third, *after)
            self.sent = (self.second, self.third)
            self.fourth = self.ladder.step(self.second, 3)
            self.far += [self.ladder.across(self.third), self.ladder.across(self.second)]

    def finish(self, *after):
        if self.native:
            self.groups = [lax.all_gather(self.shard, self.ladder.axes, axis=0, tiled=True)]
        else:
            self.fourth = tie(self.fourth, *after)
            self.sent = (self.fourth,)
            self.far += [self.ladder.across(self.fourth)]
            self.groups = [self.own, self.second, self.third, self.fourth] + self.far
        return self.groups


class Scatter:
    def __init__(self, ladder, parts):
        self.ladder, self.native, self.parts = ladder, ladder.native, parts
        self.sent = ()
        if not self.native:
            self.keep = parts[0]
            self.near = ladder.across(parts[1])

    def corner(self, *after):
        if not self.native:
            self.near = tie(self.near, *after)
            total = add_up(self.keep[2:], self.near[2:]).astype(BF16)
            self.sent = (total,)
            self.third = self.ladder.step(total, 3)

    def plane(self, *after):
        if not self.native:
            self.third = tie(self.third, *after)
            total = add_up(self.keep[1], self.near[1], self.third[1]).astype(BF16)
            self.sent = (total,)
            self.second = self.ladder.step(total, 2)

    def spread(self, *after):
        if not self.native:
            second = tie(self.second, *after)
            self.mine, *away = spread_sums(self.ladder.meta, self.keep, self.near, self.third, second)
            self.sent = tuple(away)
            self.last = [self.ladder.flip(part, bit, bit) for part, bit in zip(away, Z_HOPS)]

    def finish(self, *after):
        if self.native:
            return lax.psum_scatter(self.parts[0].astype(F32), self.ladder.axes, scatter_dimension=0, tiled=True)
        total = add_up(self.mine, *[tie(part, *after) for part in self.last])
        self.sent = (total,)
        return total


def nt(a, b):
    return lax.dot_general(a, b, (((1,), (1,)), ((), ())), preferred_element_type=F32)


def nn(a, b):
    return lax.dot_general(a, b, (((1,), (0,)), ((), ())), preferred_element_type=F32)


def fill_bias(lo_ref, segc_ref, padc_ref, segr_ref, bias_ref, nblocks, most):
    def one(qb, _):
        lo = lo_ref[qb]
        q0 = pl.multiple_of(qb * QB, QB)
        segq = segr_ref[pl.ds(qb, 1), :]
        qpos = q0 + lax.broadcasted_iota(jnp.int32, (QB, QB), 1)

        def part(j, _):
            k0 = pl.multiple_of((lo + j) * QB, QB)
            kpos = k0 + lax.broadcasted_iota(jnp.int32, (QB, QB), 0)
            segk = segc_ref[pl.ds(k0, QB), :]
            padk = padc_ref[pl.ds(k0, QB), :]
            ok = (segk == segq) & (kpos <= qpos) & ((padk == 1) | (kpos == qpos))
            bias_ref[qb, pl.ds(pl.multiple_of(j * QB, QB), QB), :] = jnp.where(ok, 0.0, -1e30)
            return 0

        lax.fori_loop(0, qb - lo + 1, part, 0)
        return 0

    lax.fori_loop(0, nblocks, one, 0)


def head_pair(x, scale):
    lane = lax.broadcasted_iota(jnp.int32, x.shape, 1)
    first = jnp.where(lane < HD, scale, 0.0).astype(x.dtype)
    second = jnp.where(lane < HD, 0.0, scale).astype(x.dtype)
    return jnp.concatenate([x * first, x * second], 0)


def attn_fwd_kernel(nblocks, most, many, lo_ref, segc_ref, padc_ref, segr_ref, q_ref, k_ref, v_ref, o_ref, lse_ref, bias_ref, vt_ref):
    @pl.when(pl.program_id(0) == 0)
    def _():
        fill_bias(lo_ref, segc_ref, padc_ref, segr_ref, bias_ref, nblocks, most)

    vt_ref[...] = v_ref[...].T

    def block(qb, _):
        lo = lo_ref[qb]
        q0 = pl.multiple_of(qb * QB, QB)
        k0 = pl.multiple_of(lo * QB, QB)
        for n in range(1, most + 1):
            @pl.when(qb - lo + 1 == n)
            def _(n=n):
                w = n * QB
                bias = bias_ref[qb, 0:w, :]
                bias = jnp.concatenate([bias, bias], 1)
                cols = [slice(128 * i, 128 * (i + 1)) for i in range(many)]
                scores = [nt(k_ref[pl.ds(k0, w), c], head_pair(q_ref[pl.ds(q0, QB), c], HD ** -0.5)) + bias for c in cols]
                tops = [jnp.max(s, 0, keepdims=True) for s in scores]
                parts = [jnp.exp(s - m) for s, m in zip(scores, tops)]
                totals = [jnp.sum(p, 0, keepdims=True) for p in parts]
                outs = [nn(vt_ref[c, pl.ds(k0, w)], (p * (1.0 / t)).astype(BF16)) for c, p, t in zip(cols, parts, totals)]
                for i, (c, o, m, t) in enumerate(zip(cols, outs, tops, totals)):
                    o = jnp.concatenate([o[:HD, :QB], o[HD:, QB:]], 0)
                    o_ref[pl.ds(q0, QB), c] = o.T.astype(BF16)
                    lse_ref[i, pl.ds(qb, 1), :] = m + jnp.log(t)
        return 0

    lax.fori_loop(0, nblocks, block, 0)


def attn_bwd_kernel(nblocks, most, many, lo_ref, segc_ref, padc_ref, segr_ref, q_ref, k_ref, v_ref, do_ref, lse_ref,
                    out_ref, sums_ref, bias_ref, kt_ref, dk_acc, dv_acc):
    @pl.when(pl.program_id(0) == 0)
    def _():
        fill_bias(lo_ref, segc_ref, padc_ref, segr_ref, bias_ref, nblocks, most)

    kt_ref[...] = k_ref[...].T
    dk_acc[...] = jnp.zeros_like(dk_acc)
    dv_acc[...] = jnp.zeros_like(dv_acc)
    sums_ref[...] = jnp.zeros_like(sums_ref)

    def block(qb, _):
        lo = lo_ref[qb]
        q0 = pl.multiple_of(qb * QB, QB)
        k0 = pl.multiple_of(lo * QB, QB)
        for n in range(1, most + 1):
            @pl.when(qb - lo + 1 == n)
            def _(n=n):
                w = n * QB
                bias = bias_ref[qb, 0:w, :]
                bias = jnp.concatenate([bias, bias], 1)
                cols = [slice(128 * i, 128 * (i + 1)) for i in range(many)]
                rows, keys = pl.ds(q0, QB), pl.ds(k0, w)
                q2 = [head_pair(q_ref[rows, c], HD ** -0.5) for c in cols]
                do2 = [head_pair(do_ref[rows, c], 1.0) for c in cols]
                probs = [jnp.exp(nt(k_ref[keys, c], q) + bias - lse_ref[i, pl.ds(qb, 1), :]) for i, (c, q) in enumerate(zip(cols, q2))]
                dprobs = [nt(v_ref[keys, c], do) for c, do in zip(cols, do2)]
                inner = [jnp.sum(p * dp, 0, keepdims=True) for p, dp in zip(probs, dprobs)]
                ds = [(p * (dp - i)).astype(BF16) for p, dp, i in zip(probs, dprobs, inner)]
                for c, p, d, q, do in zip(cols, probs, ds, q2, do2):
                    dv_acc[keys, c] += nn(p.astype(BF16), do)
                    dk_acc[keys, c] += nn(d, q)
                    dq = nn(kt_ref[c, keys], d)
                    dq = jnp.concatenate([dq[:HD, :QB], dq[HD:, QB:]], 0) * (HD ** -0.5)
                    dq = dq.T.astype(BF16)
                    out_ref[0, rows, c] = dq
                    sums_ref[0:1, c] += jnp.sum(dq.astype(F32), 0, keepdims=True)
        return 0

    lax.fori_loop(0, nblocks, block, 0)
    out_ref[1] = dk_acc[...].astype(BF16)
    dv = dv_acc[...].astype(BF16)
    out_ref[2] = dv
    sums_ref[1:2, :] = jnp.sum(dv.astype(F32), 0, keepdims=True)


def mask_inputs(segment_ids, padding_mask):
    length = segment_ids.shape[0]
    nblocks = length // QB
    first = segment_ids.reshape(nblocks, QB)[:, 0]
    start = jnp.sum((segment_ids[None, :] < first[:, None]).astype(jnp.int32), 1)
    lo = start // QB
    segc = jnp.broadcast_to(segment_ids[:, None], (length, QB))
    padc = jnp.broadcast_to(padding_mask[:, None], (length, QB))
    return lo.astype(jnp.int32), segc, padc, segment_ids.reshape(nblocks, QB)


def attn_call(kernel, name, each, operands, specs, shapes, out_specs, scratch, masks, first, pairs, before):
    lo, segc, padc, segr = masks
    length = segc.shape[0]
    nblocks = length // QB
    most = min(nblocks, SPAN // QB + 1)
    whole = lambda p, lo: (0, 0)
    in_specs = [pl.BlockSpec((length, QB), whole), pl.BlockSpec((length, QB), whole), pl.BlockSpec((nblocks, QB), whole)] + specs
    arguments = [lo, segc, padc, segr] + operands
    aliases = {}
    if before is not None:
        aliases = {len(arguments) + i: i for i in range(len(before))}
        in_specs, arguments = in_specs + [pl.BlockSpec(memory_space=pl.ANY)] * len(before), arguments + list(before)

    def body(*refs):
        inputs, rest = refs[: len(arguments) - len(aliases)], refs[len(arguments) :]
        kernel(nblocks, most, MANY, *inputs, *rest)

    return pl.pallas_call(
        body,
        grid_spec=pltpu.PrefetchScalarGridSpec(
            num_scalar_prefetch=1, grid=(pairs // MANY,), in_specs=in_specs, out_specs=out_specs,
            scratch_shapes=[pltpu.VMEM((nblocks, most * QB, QB), F32)] + scratch),
        out_shape=shapes,
        input_output_aliases=aliases,
        compiler_params=pltpu.CompilerParams(vmem_limit_bytes=48 << 20),
        cost_estimate=cost(each * pairs),
        name=name,
    )(*arguments)


def attn_forward(q, k, v, masks, first, pairs, before=None):
    (qa, qo), (ka, ko), (va, vo) = q, k, v
    length, width = qa.shape[0], 128 * MANY
    at = first // MANY
    col = lambda off: pl.BlockSpec((length, width), lambda p, lo: (0, off // MANY + at + p))
    stat = pl.BlockSpec((MANY, length // QB, 2 * QB), lambda p, lo: (at + p, 0, 0))
    total = ko - qo
    return attn_call(
        attn_fwd_kernel, "attn_forward", 2.7, [qa, ka, va], [col(qo), col(ko), col(vo)],
        [jax.ShapeDtypeStruct((length, 128 * total), BF16), jax.ShapeDtypeStruct((total, length // QB, 2 * QB), F32)],
        [col(0), stat], [pltpu.VMEM((width, length), BF16)], masks, first, pairs, before)


def attn_backward(q, k, v, do, lse, masks, first, pairs, before=None):
    (qa, qo), (ka, ko), (va, vo) = q, k, v
    length, width = qa.shape[0], 128 * MANY
    at = first // MANY
    col = lambda off: pl.BlockSpec((length, width), lambda p, lo: (0, off // MANY + at + p))
    stat = pl.BlockSpec((MANY, length // QB, 2 * QB), lambda p, lo: (at + p, 0, 0))
    total = ko - qo
    return attn_call(
        attn_bwd_kernel, "attn_backward", 3.4, [qa, ka, va, do, lse], [col(qo), col(ko), col(vo), col(0), stat],
        [jax.ShapeDtypeStruct((3, length, 128 * total), BF16), jax.ShapeDtypeStruct((8, 128 * total), F32)],
        [pl.BlockSpec((3, length, width), lambda p, lo: (0, 0, at + p)), pl.BlockSpec((8, width), lambda p, lo: (0, at + p))],
        [pltpu.VMEM((width, length), BF16), pltpu.VMEM((length, width), F32), pltpu.VMEM((length, width), F32)],
        masks, first, pairs, before)


ANY = pl.BlockSpec(memory_space=pl.ANY)
META = 1


def params(megabytes=56):
    return pltpu.CompilerParams(vmem_limit_bytes=megabytes << 20)


def tile_shape(native, rows, columns):
    return (1, 1, 1, rows, columns) if native else (4, 4, 2, rows // 32, columns)


def fetch_columns(native, meta, groups, target, start, columns, sem):
    cols = pl.ds(start, columns)
    if native:
        pltpu.make_async_copy(groups[0].at[:, cols], target.at[0, 0, 0], sem).start()
        return
    core = meta[4]
    for t in range(4):
        pltpu.make_async_copy(groups[t].at[:, :, cols], target.at[meta[t], :, core], sem).start()
        pltpu.make_async_copy(groups[4 + t].at[:, :, cols], target.at[meta[t], :, 1 - core], sem).start()


def quarter_shape(native, rows, columns):
    return (1, 1, rows // 4, columns) if native else (4, 2, rows // 32, columns)


def fetch_quarter(native, meta, groups, target, t, sem):
    cols = pl.ds(0, target.shape[-1])
    if native:
        rows = target.shape[-2]
        pltpu.make_async_copy(groups[0].at[pl.ds(t * rows, rows), cols], target.at[0, 0], sem).start()
        return
    core = meta[4]
    pltpu.make_async_copy(groups[t].at[:, :, cols], target.at[:, core], sem).start()
    pltpu.make_async_copy(groups[4 + t].at[:, :, cols], target.at[:, 1 - core], sem).start()


def arrive(target, sem):
    pltpu.make_async_copy(target, target, sem).wait()


def group_specs(groups):
    return [ANY] * len(groups)


def flat(value):
    return value.reshape(-1, value.shape[-1])


def out_blocks(native, rows, columns):
    if native:
        return [jax.ShapeDtypeStruct((rows, columns), BF16)]
    return [jax.ShapeDtypeStruct((4, 4, rows // 32, columns), BF16)] * 2


def push_columns(native, meta, stage, outs, start, columns, sem):
    cols = pl.ds(start, columns)
    if native:
        pltpu.make_async_copy(stage.at[0, 0, 0], outs[0].at[:, cols], sem).start()
        return
    core = meta[4]
    for t in range(4):
        pltpu.make_async_copy(stage.at[meta[t], :, core], outs[0].at[t, :, :, cols], sem).start()
        pltpu.make_async_copy(stage.at[meta[t], :, 1 - core], outs[1].at[FLIP[t], :, :, cols], sem).start()


def each_rows(total, rows, body):
    def step(i, _):
        body(i, pl.ds(pl.multiple_of(i * rows, rows), rows))
        return 0

    lax.fori_loop(0, total // rows, step, 0)


def squares(values, valid):
    return jnp.sum(values * values * valid, 0, keepdims=True)


def scale_of(values):
    return lax.rsqrt(jnp.mean(values * values, -1, keepdims=True) + 1e-05)


SMALL = 16


def pack_smalls(bias_up, bias_qv, bias_out, gain_attn, gain_mlp, bias_down, rows):
    at = lax.broadcasted_iota(jnp.int32, (rows, 128), 0)
    block = jnp.zeros((rows, 128), bias_up.dtype)
    for row, part in enumerate((bias_up, bias_qv, bias_out, gain_attn, gain_mlp, bias_down)):
        block = jnp.where(at == row, jnp.pad(part, (0, 128 - part.shape[0]))[None], block)
    return block


def unpack_smalls(held, up_ref, qkv_ref, lines_ref):
    width = lines_ref.shape[1]
    for shard in range(32):
        up_ref[0:1, shard * 128 : (shard + 1) * 128] = held[shard, 0:1].astype(F32)
    halves = held[...].astype(F32).reshape(16, 2, SMALL, 128)
    halves = halves[:, 0] + pltpu.roll(halves[:, 1], 64, 2)
    fours = held[...].astype(F32).reshape(8, 4, SMALL, 128)
    fours = fours[:, 0] + sum(pltpu.roll(fours[:, i], 32 * i, 2) for i in range(1, 4))
    qkv_ref[...] = jnp.zeros_like(qkv_ref)
    for i in range(16):
        first = i * 128 + (width if i >= 8 else 0)
        qkv_ref[0:1, first : first + 128] = halves[i, 1:2]
    for i in range(8):
        lines_ref[0:4, i * 128 : (i + 1) * 128] = fours[i, 2:6]


def project_kernel(native, tile, count, meta, tok_ref, valid_ref, *rest):
    groups, rest = rest[:count], rest[count:]
    if native:
        up_in, qkv_in, lines_in, out_ref, normed_ref, sq_ref, weight, sems = rest
    else:
        out_ref, normed_ref, sq_ref, up_ref, lines_ref, weight, held, qkv_in, sems = rest
        lines_in = lines_ref
    n, steps = pl.program_id(0), pl.num_programs(0)
    columns = steps * tile

    @pl.when(n == 0)
    def _():
        if not native:
            last = pl.ds(columns, 128)
            for t in range(4):
                for first, side in ((0, meta[4]), (4, 1 - meta[4])):
                    source = groups[first + t].at[:, pl.ds(0, SMALL), last]
                    pltpu.make_async_copy(source, held.at[meta[t], :, side], sems.at[2]).start()
        fetch_columns(native, meta, groups, weight.at[0], 0, tile, sems.at[0])

    @pl.when(n + 1 < steps)
    def _():
        slot = (n + 1) % 2
        fetch_columns(native, meta, groups, weight.at[slot], pl.multiple_of((n + 1) * tile, tile), tile, sems.at[slot])

    @pl.when(n == 0)
    def _():
        if not native:
            arrive(held, sems.at[2])
            unpack_smalls(held[...].reshape(32, SMALL, 128), up_ref, qkv_in, lines_ref)
        sq_ref[...] = jnp.zeros_like(sq_ref)

        def norm(i, at):
            frames = tok_ref[at, :].astype(F32)
            sq_ref[...] += squares(frames, valid_ref[at, :])
            normed_ref[at, :] = (frames * scale_of(frames) * lines_in[1:2, :]).astype(BF16)

        each_rows(tok_ref.shape[0], 256, norm)

    arrive(weight.at[n % 2], sems.at[n % 2])
    bias = qkv_in[0:1, pl.ds(pl.multiple_of(n * tile, tile), tile)]
    out_ref[...] = (nn(normed_ref[...], flat(weight[n % 2])) + bias).astype(BF16)


def project(ladder, tokens, valid, groups, known=None):
    length, width = tokens.shape
    columns, tile, hidden = 3 * width, 512, 4 * width
    native = ladder.native
    whole = lambda n, meta: (0, 0)
    up, lines = pl.BlockSpec((1, hidden), whole), pl.BlockSpec((4, width), whole)
    out_specs = [pl.BlockSpec((length, tile), lambda n, meta: (0, n)), pl.BlockSpec((length, width), whole), pl.BlockSpec((1, width), whole)]
    out_shape = [jax.ShapeDtypeStruct((length, columns), BF16), jax.ShapeDtypeStruct((length, width), BF16),
                 jax.ShapeDtypeStruct((1, width), F32)]
    scratch = [pltpu.VMEM((2,) + tile_shape(native, width, tile), BF16)]
    vectors = [jax.ShapeDtypeStruct((1, hidden), F32), jax.ShapeDtypeStruct((4, width), F32)]
    extra = []
    if native:
        extra = [up, pl.BlockSpec((1, columns), whole), lines]
    else:
        out_specs, out_shape = out_specs + [up, lines], out_shape + vectors
        scratch += [pltpu.VMEM((4, 4, 2, SMALL, 128), BF16), pltpu.VMEM((1, columns), F32)]
    results = pl.pallas_call(
        functools.partial(project_kernel, native, tile, len(groups)),
        grid_spec=pltpu.PrefetchScalarGridSpec(
            num_scalar_prefetch=1, grid=(columns // tile,),
            in_specs=[pl.BlockSpec((length, width), whole), pl.BlockSpec((length, 1), whole)] + group_specs(groups) + extra,
            out_specs=out_specs, scratch_shapes=scratch + [pltpu.SemaphoreType.DMA((3,))]),
        out_shape=out_shape,
        compiler_params=params(),
        cost_estimate=cost(14),
        name="project",
    )(ladder.meta, tokens, valid, *groups, *(known or ()))
    return results if not native else list(results) + [known[0], known[2]]


def gelu_pair(u):
    c, d = 0.7978845608028654, 0.044715
    square = u * u
    bend = 0.5 * jnp.tanh(u * (c + c * d * square))
    half = 0.5 + bend
    slope = half * (1.0 + (0.5 - bend) * (u * (2.0 * c + 6.0 * c * d * square)))
    return (u * half).astype(BF16), slope.astype(BF16)


def expand_kernel(native, tile, count, meta, mixed_ref, tok_ref, lines_ref, valid_ref, up_bias_ref, *rest):
    groups, rest = rest[:count], rest[count:]
    middle_ref, normed_ref, sq_ref, act_ref, slope_ref, middle, out_weight, weight, sems = rest
    n, steps = pl.program_id(0), pl.num_programs(0)
    half = out_weight.shape[-1]
    first = 2 * half
    store = pltpu.make_async_copy(middle, middle_ref, sems.at[4])

    @pl.when(n == 0)
    def _():
        for side in range(2):
            fetch_columns(native, meta, groups, out_weight.at[side], side * half, half, sems.at[2 + side])
        fetch_columns(native, meta, groups, weight.at[0], first, tile, sems.at[0])

    @pl.when(n + 1 < steps)
    def _():
        slot = (n + 1) % 2
        fetch_columns(native, meta, groups, weight.at[slot], pl.multiple_of(first + (n + 1) * tile, tile), tile, sems.at[slot])

    @pl.when(n == 0)
    def _():
        for side in range(2):
            arrive(out_weight.at[side], sems.at[2 + side])
        sq_ref[...] = jnp.zeros_like(sq_ref)

        def part(i, at):
            branch = jnp.concatenate([nn(mixed_ref[at, :], flat(out_weight[side])) for side in range(2)], 1) + lines_ref[0:1, :]
            total = tok_ref[at, :].astype(F32) + branch
            middle[at, :] = total
            normed_ref[at, :] = (total * scale_of(total) * lines_ref[2:3, :]).astype(BF16)
            sq_ref[0:1, :] += squares(branch, valid_ref[at, :])
            sq_ref[1:2, :] += squares(total, valid_ref[at, :])

        each_rows(middle.shape[0], 256, part)
        store.start()

    arrive(weight.at[n % 2], sems.at[n % 2])
    act_ref[...], slope_ref[...] = gelu_pair(nn(normed_ref[...], flat(weight[n % 2])) + up_bias_ref[...])

    @pl.when(n == steps - 1)
    def _():
        store.wait()


def expand(ladder, mixed, tokens, lines, valid, up_bias, groups):
    length, width = tokens.shape
    columns, tile = up_bias.shape[1], 512
    whole = lambda n, meta: (0, 0)
    column = lambda n, meta: (0, n)
    square = pl.BlockSpec((length, width), whole)
    return pl.pallas_call(
        functools.partial(expand_kernel, ladder.native, tile, len(groups)),
        grid_spec=pltpu.PrefetchScalarGridSpec(
            num_scalar_prefetch=1, grid=(columns // tile,),
            in_specs=[square, square, pl.BlockSpec((4, width), whole), pl.BlockSpec((length, 1), whole), pl.BlockSpec((1, tile), column)]
            + group_specs(groups),
            out_specs=[ANY, square, pl.BlockSpec((8, width), whole), pl.BlockSpec((length, tile), column),
                       pl.BlockSpec((length, tile), column)],
            scratch_shapes=[pltpu.VMEM((length, width), F32),
                            pltpu.VMEM((2,) + tile_shape(ladder.native, width, width // 2), BF16),
                            pltpu.VMEM((2,) + tile_shape(ladder.native, width, tile), BF16), pltpu.SemaphoreType.DMA((5,))]),
        out_shape=[jax.ShapeDtypeStruct((length, width), F32), jax.ShapeDtypeStruct((length, width), BF16),
                   jax.ShapeDtypeStruct((8, width), F32)] + [jax.ShapeDtypeStruct((length, columns), BF16)] * 2,
        compiler_params=params(),
        cost_estimate=cost(29),
        name="expand",
    )(ladder.meta, mixed, tokens, lines, valid, up_bias, *groups)


def fetch_turn(native, meta, groups, weight, sems, t, first=0, last=3):
    for at in range(first, last + 1):
        @pl.when(t == max(at - 1, first))
        def _(at=at):
            fetch_quarter(native, meta, groups, weight.at[at % 2], at, sems.at[at % 2])

    arrive(weight.at[t % 2], sems.at[t % 2])


def tn(a, b):
    return lax.dot_general(a, b, (((0,), (0,)), ((), ())), preferred_element_type=F32)


def down_grad_kernel(native, count, meta, act_ref, cot_ref, *rest):
    outs, (sum_ref, stage, sems) = rest[:count], rest[count:]
    t = pl.program_id(0)
    slot = t % 2

    @pl.when(t >= 2)
    def _():
        arrive(stage.at[slot], sems.at[slot])

    stage[slot] = tn(act_ref[...], cot_ref[...]).astype(BF16).reshape(stage.shape[1:])
    if native:
        rows = stage.shape[-2]
        pltpu.make_async_copy(stage.at[slot, 0, 0], outs[0].at[pl.ds(t * rows, rows), :], sems.at[slot]).start()
    else:
        for k in range(4):
            @pl.when(t == k)
            def _(k=k):
                pltpu.make_async_copy(stage.at[slot, :, meta[4]], outs[0].at[k], sems.at[slot]).start()
                pltpu.make_async_copy(stage.at[slot, :, 1 - meta[4]], outs[1].at[FLIP[k]], sems.at[slot]).start()

    @pl.when(t == 0)
    def _():
        sum_ref[...] = jnp.sum(cot_ref[...].astype(F32), 0, keepdims=True)

    @pl.when(t == 3)
    def _():
        arrive(stage.at[1 - slot], sems.at[1 - slot])
        arrive(stage.at[slot], sems.at[slot])


def down_grad(ladder, act, cot):
    length, width = cot.shape
    hidden = act.shape[1]
    outs = out_blocks(ladder.native, hidden, width)
    whole = lambda t, meta: (0, 0)
    return pl.pallas_call(
        functools.partial(down_grad_kernel, ladder.native, len(outs)),
        grid_spec=pltpu.PrefetchScalarGridSpec(
            num_scalar_prefetch=1, grid=(4,),
            in_specs=[pl.BlockSpec((length, hidden // 4), lambda t, meta: (0, meta[t])), pl.BlockSpec((length, width), whole)],
            out_specs=[ANY] * len(outs) + [pl.BlockSpec((1, width), whole)],
            scratch_shapes=[pltpu.VMEM((2,) + quarter_shape(ladder.native, hidden, width), BF16), pltpu.SemaphoreType.DMA((2,))]),
        out_shape=outs + [jax.ShapeDtypeStruct((1, width), F32)],
        compiler_params=params(),
        cost_estimate=cost(14),
        name="down_grad",
    )(ladder.meta, act, cot)


def row_grad_kernel(native, tile, count, meta, left_ref, right_ref, *rest):
    outs, (stage, sems) = rest[:count], rest[count:]
    n, steps = pl.program_id(0), pl.num_programs(0)
    slot = n % 2

    @pl.when(n >= 2)
    def _():
        arrive(stage.at[slot], sems.at[slot])

    stage[slot] = tn(left_ref[...], right_ref[...]).astype(BF16).reshape(stage.shape[1:])
    push_columns(native, meta, stage.at[slot], outs, pl.multiple_of(n * tile, tile), tile, sems.at[slot])

    @pl.when(n == steps - 1)
    def _():
        arrive(stage.at[1 - slot], sems.at[1 - slot])
        arrive(stage.at[slot], sems.at[slot])


def row_grad(ladder, left, right, name):
    length, width = left.shape
    parts, _, each = right.shape
    tile = 512
    per = each // tile
    outs = out_blocks(ladder.native, width, parts * each)
    return pl.pallas_call(
        functools.partial(row_grad_kernel, ladder.native, tile, len(outs)),
        grid_spec=pltpu.PrefetchScalarGridSpec(
            num_scalar_prefetch=1, grid=(parts * per,),
            in_specs=[pl.BlockSpec((length, width), lambda n, meta: (0, 0)),
                      pl.BlockSpec((None, length, tile), lambda n, meta: (n // per, 0, n % per))],
            out_specs=[ANY] * len(outs),
            scratch_shapes=[pltpu.VMEM((2,) + tile_shape(ladder.native, width, tile), BF16), pltpu.SemaphoreType.DMA((2,))]),
        out_shape=outs,
        compiler_params=params(),
        cost_estimate=cost(8),
        name=name,
    )(ladder.meta, left, right)


def norm_grad(grad, source, gain):
    r = scale_of(source)
    hat = source * r
    gain_grad = jnp.sum(grad * hat, 0, keepdims=True)
    scaled = grad * gain
    return r * (scaled - hat * jnp.mean(scaled * hat, -1, keepdims=True)), gain_grad


def back_kernel(native, last, counts, meta, cot_ref, slope_ref, normed_ref, lines_ref, middle_ref, mixed_ref, *rest):
    down_groups, rest = rest[: counts[0]], rest[counts[0] :]
    groups, rest = rest[: counts[0]], rest[counts[0] :]
    if last:
        before, rest = rest[0], rest[2 + counts[1] :]
    pushed, rest = rest[: counts[1]], rest[counts[1] :]
    if last:
        out_ref, branch_ref, mixed_out_ref, sum_ref, up_sum_ref, rest = *rest[:5], rest[5:]
        acc, down_weight, weight, stage, slope, normed, sems, middle, out_weight, mixed = rest
    else:
        after, up_sum_ref, acc, down_weight, weight, stage, slope, normed, sems = rest
    base = 2 if last else 0
    step = pl.program_id(0)
    t = step + base
    width, tile = normed.shape[1], slope.shape[2]
    slot = step

    def columns(at):
        return pl.multiple_of(width + meta[at] * tile, 512)

    loads = [pltpu.make_async_copy(slope_ref.at[:, pl.ds(pl.multiple_of(meta[base + at] * tile, 512), tile)], slope.at[at], sems.at[9 + at])
             for at in range(2)]
    loads.append(pltpu.make_async_copy(normed_ref, normed, sems.at[11]))
    if last:
        loads.append(pltpu.make_async_copy(mixed_ref, mixed, sems.at[12]))

    @pl.when(step == 0)
    def _():
        fetch_quarter(native, meta, down_groups, down_weight.at[0], base, sems.at[0])
        loads[0].start()
        loads[2].start()
        fetch_quarter(native, meta, down_groups, down_weight.at[1], base + 1, sems.at[1])
        loads[1].start()
        for at in range(2):
            fetch_columns(native, meta, groups, weight.at[at], columns(base + at), tile, sems.at[2 + at])
        if last:
            pltpu.make_async_copy(before, acc, sems.at[6]).start()
            pltpu.make_async_copy(middle_ref, middle, sems.at[7]).start()
            fetch_columns(native, meta, groups, out_weight, 0, width, sems.at[8])
            loads[3].start()

    arrive(down_weight.at[slot], sems.at[slot])
    length = acc.shape[0]
    product = nt(cot_ref[...], flat(down_weight[slot]))
    arrive(slope.at[slot], sems.at[9 + slot])
    grad = (product * slope[slot].astype(F32)).astype(BF16)
    up_sum_ref[...] = jnp.sum(grad.astype(F32), 0, keepdims=True)

    @pl.when(step == 0)
    def _():
        loads[2].wait()

    stage[slot] = tn(normed[...], grad).astype(BF16).reshape(stage.shape[1:])
    push_columns(native, meta, stage.at[slot], pushed, columns(t), tile, sems.at[4 + slot])
    arrive(weight.at[slot], sems.at[2 + slot])
    product = nt(grad, flat(weight[slot]))

    @pl.when(step == 0)
    def _():
        if last:
            pltpu.make_async_copy(before, acc, sems.at[6]).wait()
            acc[...] += product
        else:
            acc[...] = product

    @pl.when(step == 1)
    def _():
        acc[...] += product
        if last:
            pltpu.make_async_copy(middle_ref, middle, sems.at[7]).wait()
            sum_ref[...] = jnp.zeros_like(sum_ref)

            def part(i, at):
                back, gain_grad = norm_grad(acc[at, :], middle[at, :], lines_ref[2:3, :])
                total = cot_ref[at, :].astype(F32) + back
                acc[at, :] = total
                branch = total.astype(BF16)
                branch_ref[at, :] = branch
                sum_ref[0:1, :] += gain_grad
                sum_ref[1:2, :] += jnp.sum(branch.astype(F32), 0, keepdims=True)

            each_rows(length, 256, part)
            pltpu.make_async_copy(acc, out_ref, sems.at[6]).start()
            arrive(stage.at[0], sems.at[4])
            loads[3].wait()
            stage[0] = tn(mixed[...], branch_ref[...]).astype(BF16).reshape(stage.shape[1:])
            push_columns(native, meta, stage.at[0], pushed, 0, width, sems.at[4])
            arrive(out_weight, sems.at[8])
            mixed_out_ref[...] = nt(branch_ref[...], flat(out_weight[...])).astype(BF16)
            pltpu.make_async_copy(acc, out_ref, sems.at[6]).wait()
        else:
            pltpu.make_async_copy(acc, after, sems.at[6]).start()
            pltpu.make_async_copy(acc, after, sems.at[6]).wait()
        for at in range(2):
            arrive(stage.at[at], sems.at[4 + at])


def back(ladder, cot, slope, normed, lines, middle, mixed, down_groups, groups, before=None):
    length, width = cot.shape
    hidden, tile = slope.shape[1], slope.shape[1] // 4
    last = before is not None
    base = 2 if last else 0
    whole = lambda t, meta: (0, 0)
    part = lambda t, meta: (0, meta[t + base])
    square = pl.BlockSpec((length, width), whole)
    once = pl.BlockSpec((length, width), whole, pipeline_mode=pl.Buffered(1))
    outs = out_blocks(ladder.native, width, hidden + width)
    counts = (len(groups), len(outs))
    full, wide = jax.ShapeDtypeStruct((length, width), F32), jax.ShapeDtypeStruct((length, width), BF16)
    sums = jax.ShapeDtypeStruct((1, hidden), F32)
    in_specs = [once, ANY, ANY, pl.BlockSpec((4, width), whole), ANY, ANY]
    in_specs += [ANY] * (2 * counts[0])
    operands = [ladder.meta, cot, slope, normed, lines, middle, mixed, *down_groups, *groups]
    scratch = [pltpu.VMEM((length, width), F32), pltpu.VMEM((2,) + quarter_shape(ladder.native, hidden, width), BF16),
               pltpu.VMEM((2,) + tile_shape(ladder.native, width, tile), BF16),
               pltpu.VMEM((2,) + tile_shape(ladder.native, width, tile), BF16), pltpu.VMEM((2, length, tile), BF16),
               pltpu.VMEM((length, width), BF16), pltpu.SemaphoreType.DMA((13,))]
    aliases = {}
    if last:
        aliases = {len(operands) + 1 + i: i for i in range(counts[1])}
        aliases[len(operands) + 1 + counts[1]] = counts[1] + 4
        operands += list(before)
        in_specs += [ANY] * (2 + counts[1])
        out_specs = [ANY] * counts[1] + [ANY, square, square, pl.BlockSpec((8, width), whole)]
        out_shape = outs + [full, wide, wide, jax.ShapeDtypeStruct((8, width), F32)]
        scratch += [pltpu.VMEM((length, width), F32), pltpu.VMEM(tile_shape(ladder.native, width, width), BF16),
                    pltpu.VMEM((length, width), BF16)]
    else:
        out_specs, out_shape = [ANY] * counts[1] + [ANY], outs + [full]
    return pl.pallas_call(
        functools.partial(back_kernel, ladder.native, last, counts),
        grid_spec=pltpu.PrefetchScalarGridSpec(
            num_scalar_prefetch=1, grid=(2,), in_specs=in_specs, out_specs=out_specs + [pl.BlockSpec((1, tile), part)],
            scratch_shapes=scratch),
        out_shape=out_shape + [jax.ShapeDtypeStruct((1, hidden), F32)],
        input_output_aliases=aliases,
        compiler_params=params(),
        cost_estimate=cost(30 if last else 20),
        name="back",
    )(*operands)


def contract_kernel(native, first, meta, act_ref, lines_ref, valid_ref, middle_ref, *rest):
    groups, (out_ref, sq_ref, acc, middle, weight, sems) = rest[:-6], rest[-6:]
    t = pl.program_id(0)
    load = pltpu.make_async_copy(middle_ref.at[pl.ds(first, acc.shape[0]), :], middle, sems.at[2])

    @pl.when(t == 0)
    def _():
        load.start()

    fetch_turn(native, meta, groups, weight, sems, t)
    product = nn(act_ref[...], flat(weight[t % 2]))

    @pl.when(t == 0)
    def _():
        acc[...] = product

    @pl.when(t > 0)
    def _():
        acc[...] += product

    @pl.when(t == 3)
    def _():
        load.wait()
        sq_ref[...] = jnp.zeros_like(sq_ref)
        rows = 256

        def part(i, _):
            at = pl.ds(pl.multiple_of(i * rows, rows), rows)
            branch = acc[at, :] + lines_ref[3:4, :]
            final = middle[at, :] + branch
            out_ref[at, :] = final.astype(BF16)
            sq_ref[0:1, :] += squares(branch, valid_ref[at, :])
            sq_ref[1:2, :] += squares(final, valid_ref[at, :])
            return 0

        lax.fori_loop(0, acc.shape[0] // rows, part, 0)


def contract(ladder, act, middle, lines, valid, groups, part, parts):
    length, width = middle.shape
    length //= parts
    hidden = act.shape[1]
    whole = lambda t, meta: (0, 0)
    return pl.pallas_call(
        functools.partial(contract_kernel, ladder.native, part * length),
        grid_spec=pltpu.PrefetchScalarGridSpec(
            num_scalar_prefetch=1, grid=(4,),
            in_specs=[pl.BlockSpec((length, hidden // 4), lambda t, meta: (part, meta[t])), pl.BlockSpec((4, width), whole),
                      pl.BlockSpec((length, 1), lambda t, meta: (part, 0)), ANY] + group_specs(groups),
            out_specs=[pl.BlockSpec((length, width), whole), pl.BlockSpec((8, width), whole)],
            scratch_shapes=[pltpu.VMEM((length, width), F32), pltpu.VMEM((length, width), F32),
                            pltpu.VMEM((2,) + quarter_shape(ladder.native, hidden, width), BF16), pltpu.SemaphoreType.DMA((3,))]),
        out_shape=[jax.ShapeDtypeStruct((length, width), BF16), jax.ShapeDtypeStruct((8, width), F32)],
        compiler_params=params(),
        cost_estimate=cost(16 // parts),
        name="contract",
    )(ladder.meta, act, lines, valid, middle, *groups)


def input_grad_kernel(native, calls, meta, *rest):
    grads, (tok_ref, middle_ref, lines_ref), rest = rest[:calls], rest[calls : calls + 3], rest[calls + 3 :]
    groups, (out_ref, sum_ref, acc, middle, weight, sems) = rest[:-6], rest[-6:]
    t = pl.program_id(0)
    load = pltpu.make_async_copy(middle_ref, middle, sems.at[2])

    @pl.when(t == 0)
    def _():
        load.start()

    fetch_turn(native, meta, groups, weight, sems, t)
    width = acc.shape[1]
    quarter = width // 4
    rows = flat(weight[t % 2])
    each = width // calls
    product = 0.0
    for part in range(3):
        for call in range(calls):
            first = part * width + call * each
            product += nt(grads[call][part], rows[:, first : first + each])
    acc[:, pl.ds(pl.multiple_of(meta[t] * quarter, quarter), quarter)] = product

    @pl.when(t == 3)
    def _():
        load.wait()
        sum_ref[...] = jnp.zeros_like(sum_ref)
        rows = 256

        def part(i, _):
            at = pl.ds(pl.multiple_of(i * rows, rows), rows)
            back, gain_grad = norm_grad(acc[at, :], tok_ref[at, :].astype(F32), lines_ref[1:2, :])
            out_ref[at, :] = (middle[at, :] + back).astype(BF16)
            sum_ref[0:1, :] += gain_grad
            return 0

        lax.fori_loop(0, acc.shape[0] // rows, part, 0)


def input_grad(ladder, grads, tokens, grad_middle, lines, groups):
    length, width = tokens.shape
    calls = len(grads)
    whole = lambda t, meta: (0, 0)
    square = pl.BlockSpec((length, width), whole)
    return pl.pallas_call(
        functools.partial(input_grad_kernel, ladder.native, calls),
        grid_spec=pltpu.PrefetchScalarGridSpec(
            num_scalar_prefetch=1, grid=(4,),
            in_specs=[pl.BlockSpec((3, length, width // calls), lambda t, meta: (0, 0, 0))] * calls + [square, ANY, pl.BlockSpec((4, width), whole)]
            + group_specs(groups),
            out_specs=[square, pl.BlockSpec((8, width), whole)],
            scratch_shapes=[pltpu.VMEM((length, width), F32), pltpu.VMEM((length, width), F32),
                            pltpu.VMEM((2,) + quarter_shape(ladder.native, width, 3 * width), BF16), pltpu.SemaphoreType.DMA((3,))]),
        out_shape=[jax.ShapeDtypeStruct((length, width), BF16), jax.ShapeDtypeStruct((8, width), F32)],
        compiler_params=params(),
        cost_estimate=cost(18),
        name="input_grad",
    )(ladder.meta, *grads, tokens, grad_middle, lines, *groups)


def local(ladder, tokens, cotangent, segment_ids, padding_mask, w_qkv, bias_qv, w_out, bias_out, gain_attn, gain_mlp,
          w_up, bias_up, w_down, bias_down):
    length, width = tokens.shape[1], tokens.shape[2]
    count = ladder.count
    ladder.place()
    tokens, cotangent = tokens[0], cotangent[0]

    def sent(*flows):
        return [value for flow in flows for value in flow.sent]

    sizes = [part.shape[0] for part in (bias_qv, bias_out, gain_attn, gain_mlp, bias_up, bias_down)]
    total = sum(sizes)
    ends = np.cumsum([0] + sizes)
    known = None
    block = None
    if ladder.native:
        every = lambda part: lax.all_gather(part, ladder.axes, axis=0, tiled=True).astype(F32)[None]
        qv = every(bias_qv)
        known = [every(bias_up), jnp.concatenate([qv[:, :width], jnp.zeros((1, width), F32), qv[:, width:]], 1),
                 jnp.concatenate([every(bias_out), every(gain_attn), every(gain_mlp), every(bias_down)], 0)]
    else:
        block = pack_smalls(bias_up, bias_qv, bias_out, gain_attn, gain_mlp, bias_down, w_qkv.shape[0])
    qkv, down = Gather(ladder, w_qkv, True, block), Gather(ladder, w_down, False)
    qkv.start()
    rest = Gather(ladder, jnp.concatenate([w_out, w_up], 1), False)
    masks = mask_inputs(segment_ids[0], padding_mask[0])
    valid = padding_mask[0].astype(F32)[:, None]
    qkv.plane()
    rest.start(*qkv.sent)
    qkv.corner()
    rest.low()
    qkv_groups = qkv.finish()
    rest.plane()
    down.start(*rest.sent)
    projected, normed_in, sq_frames, up_bias, lines = project(ladder, tie(tokens, *sent(rest), *masks), valid, qkv_groups, known)
    per = width // 128
    calls = 2
    each = per // calls

    down.low(projected)
    projected = tie(projected, *sent(down))
    per = width // 128
    calls = 2
    each = per // calls

    def triple():
        return (projected, 0), (projected, per), (projected, 2 * per)

    heads = None
    for call in range(calls):
        heads = attn_forward(*triple(), masks, call * each, each, heads)
        if call == 0:
            rest.corner(heads[0])
            projected = tie(projected, heads[0], *sent(rest), *down.others)
    mixed, lse = heads
    rest_groups = rest.finish(mixed)
    down.plane(*rest.sent)
    middle, normed_mid, sq_middle, act, slope = expand(
        ladder, tie(mixed, *sent(down)), tokens, lines, valid, up_bias, rest_groups)

    down.corner(act)
    *down_parts, sum_down = down_grad(ladder, tie(act, *sent(down)), cotangent)
    flow_down = Scatter(ladder, down_parts)
    down_groups = down.finish(sum_down)
    *first_parts, first_acc, first_sum = back(
        ladder, tie(cotangent, sum_down), slope, normed_mid, lines, middle, mixed, down_groups, rest_groups)
    flow_down.corner(first_acc)
    *rest_parts, grad_middle, grad_branch, grad_mixed, sum_middle, sum_up = back(
        ladder, tie(cotangent, *sent(flow_down)), slope, normed_mid, lines, middle, mixed, down_groups, rest_groups,
        [first_acc, *first_parts, first_sum])
    flow_rest = Scatter(ladder, rest_parts)
    flow_down.plane(grad_mixed)
    grad_mixed = tie(grad_mixed, *sent(flow_down))
    heads = None
    for call in range(calls):
        heads = attn_backward(*triple(), grad_mixed, lse, masks, call * each, each, heads)
        if call == 0:
            flow_down.spread(heads[0])
            flow_rest.corner(heads[0])
            grad_mixed = tie(grad_mixed, heads[0], *sent(flow_down, flow_rest))
    grad_projected, sum_qv = heads
    own_down = flow_down.finish(grad_projected)
    flow_qkv = Scatter(ladder, row_grad(ladder, normed_in, tie(grad_projected, *sent(flow_down)), "qkv_grad"))
    flow_rest.plane(*flow_qkv.parts)
    finals = []

    def finish_rows(part, *after):
        out, squares_out = contract(ladder, tie(act, *after), middle, lines, valid, down_groups, part, 2)
        finals.append(squares_out)
        return out

    outputs = [finish_rows(0, *flow_qkv.parts, *sent(flow_rest))]
    flow_rest.spread(outputs[0])
    flow_qkv.corner(outputs[0])
    tail = tie(tokens, *sent(flow_rest, flow_qkv))
    grad_tokens, sum_in = input_grad(ladder, [grad_projected], tail, grad_middle, lines, qkv_groups)
    flow_qkv.plane(grad_tokens)
    outputs.append(finish_rows(1, *sent(flow_qkv)))
    own_rest = flow_rest.finish(outputs[1])
    flow_qkv.spread(outputs[1], *([] if ladder.native else flow_rest.last))
    output = jnp.concatenate(outputs, 0)

    sq_final = finals[0] + finals[1]
    members = [sq_frames, sq_middle[1:2], sq_final[1:2], sq_middle[:1], sq_final[:1], valid.reshape(1, -1)]
    members = jnp.sum(jnp.concatenate(members, 0), 1)
    small_grads = [sum_qv[:2], sum_middle[1:2], sum_in[:1], sum_middle[:1], sum_up, sum_down]
    table = jnp.concatenate([g.reshape(count, -1) for g in small_grads] + [jnp.broadcast_to(members, (count, 6))], 1)
    table = jnp.pad(table, ((0, 0), (0, -table.shape[1] % 128)))
    own_small = ladder.scatter_small(tie(table, *sent(flow_qkv)))
    own_qkv = flow_qkv.finish(own_small)

    owned = [own_small[ends[i] : ends[i + 1]] for i in range(6)]
    totals = own_small[total : total + 6]
    stats = jnp.sqrt(totals[:5] / (totals[5] * width))
    own_out, own_up = own_rest[:, :width], own_rest[:, width:]
    return (output[None], grad_tokens[None], own_qkv, owned[0], own_out, owned[1], owned[2], owned[3], own_up, owned[4],
            own_down, owned[5], stats, totals[5:6])


def solution(mesh):
    rows, wide, flat = P(("dp", "fsdp"), None, None), P(("dp", "fsdp"), None), P(("dp", "fsdp"))
    return jax.shard_map(
        functools.partial(local, Ladder(mesh)),
        mesh=mesh,
        in_specs=(rows, rows, wide, wide, wide, flat, wide, flat, flat, flat, wide, flat, wide, flat),
        out_specs=(rows, rows, wide, flat, wide, flat, flat, flat, wide, flat, wide, flat, P(), P()),
        check_vma=False,
    )
```

```python
import functools

import jax
import jax.numpy as jnp
import numpy as np
from jax import lax
from jax.experimental import pallas as pl
from jax.experimental.pallas import tpu as pltpu
from jax.sharding import PartitionSpec as P

HD = 64
QB = 128
SPAN = 512
MANY = 4
WEIGH = 2
PARTS = 1
F32 = jnp.float32
BF16 = jnp.bfloat16

CORE = 1
Z_HOPS = (2, 4, 6)
MIX = ((0, 1, 2, 3), (0, 2, 1, 3))
FLIP = (0, 2, 1, 3)
HOPS = ((4, 2, 8, 16), (4, 2, 16, 8))


def tie(value, *others):
    return lax.optimization_barrier((value,) + others)[0]


def add_up(*terms):
    return sum(term.astype(F32) for term in terms)


def cost(microseconds):
    return pl.CostEstimate(flops=int(WEIGH * microseconds * 1.15e9), transcendentals=0, bytes_accessed=0)


class Ladder:
    def __init__(self, mesh):
        self.count = int(np.prod(list(mesh.shape.values())))
        self.native = dict(mesh.shape) != {"dp": 4, "fsdp": 8}
        self.axes = ("dp", "fsdp")

    def place(self):
        if self.native:
            self.meta = jnp.array([0, 1, 2, 3, 0, 0], jnp.int32)
            return
        me = lax.axis_index(self.axes)
        odd = (me & CORE) == 1
        mix = jnp.where(odd, jnp.array(MIX[1], jnp.int32), jnp.array(MIX[0], jnp.int32))
        self.meta = jnp.concatenate([(me >> 3) ^ mix, (me & CORE)[None], ((me >> 1) & 3)[None]])

    def flip(self, value, even, odd):
        bits = (even, odd)
        return lax.ppermute(value, self.axes, [(i, i ^ bits[i & CORE]) for i in range(self.count)])

    def step(self, value, level):
        return self.flip(value, HOPS[0][level], HOPS[1][level])

    def across(self, value):
        return self.flip(value, CORE, CORE)

    def scatter_small(self, table):
        return jnp.sum(lax.all_to_all(table, self.axes, 0, 0, tiled=True), 0)


def place_kernel(meta, *refs):
    pieces, beside, out_ref = refs[:4], refs[4:-1], refs[-1]
    columns = pieces[0].shape[1]
    for k in range(4):
        out_ref[meta[5] ^ k, :, :columns] = pieces[k][...]
        if beside:
            out_ref[meta[5] ^ k, :, columns:] = beside[k][...]


def place_group(meta, pieces, beside):
    rows = pieces[0].shape[0]
    operands = list(pieces) + list(beside)
    columns = sum(part[0].shape[1] for part in (pieces, beside) if part)
    whole = lambda n, meta: (0, 0)
    return pl.pallas_call(
        place_kernel,
        grid_spec=pltpu.PrefetchScalarGridSpec(
            num_scalar_prefetch=1, grid=(1,), in_specs=[pl.BlockSpec(part.shape, whole) for part in operands],
            out_specs=pl.BlockSpec((4, rows, columns), lambda n, meta: (0, 0, 0))),
        out_shape=jax.ShapeDtypeStruct((4, rows, columns), pieces[0].dtype),
        cost_estimate=cost(2),
        name="place_group",
    )(meta, *operands)


def spread_kernel(meta, *refs):
    parts, outs = refs[:16], refs[16:]
    for k in range(4):
        total = sum(part[...].astype(F32) for part in parts[4 * k : 4 * k + 4])
        outs[k][...] = total.astype(outs[k].dtype)


def spread_sums(meta, keep, near, third, second):
    _, rows, columns = second.shape
    tile = columns // PARTS
    specs, operands = [], []
    for k in range(4):
        group = pl.BlockSpec((None, rows, tile), lambda n, meta, k=k: (meta[5] ^ k, 0, n))
        pair = pl.BlockSpec((None, None, rows, tile), lambda n, meta, k=k: (0, meta[5] ^ k, 0, n))
        specs += [pair, pair, pair, group]
        operands += [keep, near, third, second]
    out = pl.BlockSpec((rows, tile), lambda n, meta: (0, n))
    return pl.pallas_call(
        spread_kernel,
        grid_spec=pltpu.PrefetchScalarGridSpec(num_scalar_prefetch=1, grid=(columns // tile,), in_specs=specs, out_specs=[out] * 4),
        out_shape=[jax.ShapeDtypeStruct((rows, columns), F32)] + [jax.ShapeDtypeStruct((rows, columns), BF16)] * 3,
        cost_estimate=cost(3),
        name="spread_sums",
    )(meta, *operands)


class Gather:
    def __init__(self, ladder, shard, direct, beside=None):
        self.beside = beside
        self.ladder, self.shard, self.native, self.direct = ladder, shard, ladder.native, direct
        self.sent, self.others = (), []

    def start(self, *after):
        if not self.native:
            self.shard = tie(self.shard, *after)
            self.sent = (self.shard,)
            bits = Z_HOPS if self.direct else Z_HOPS[1:2]
            self.others = [self.ladder.flip(self.shard, bit, bit) for bit in bits]
            self.sides = []
            if self.beside is not None:
                beside = tie(self.beside, self.others[0])
                self.sides = [beside] + [self.ladder.flip(beside, bit, bit) for bit in bits]

    def low(self, *after):
        if not self.native:
            one, two = tie(self.others[0], *after), self.shard
            high = (self.ladder.meta[5] >> 1) == 1
            self.pair = jnp.where(high, jnp.stack([one, two]), jnp.stack([two, one]))
            self.sent = (self.pair,)
            self.others = [self.ladder.flip(self.pair, Z_HOPS[0], Z_HOPS[0])]

    def plane(self, *after):
        if not self.native:
            others = [tie(other, *after) for other in self.others]
            if self.direct:
                self.own = place_group(self.ladder.meta, [self.shard] + others, self.sides)
            else:
                one, two = others[0], self.pair
                low = (self.ladder.meta[5] & 1) == 1
                own = jnp.where(low, jnp.stack([one, two], 1), jnp.stack([two, one], 1))
                self.own = own.reshape((4,) + self.shard.shape)
            self.sent = (self.own,)
            self.second = self.ladder.step(self.own, 2)
            self.third = self.ladder.step(self.own, 3)
            self.far = [self.ladder.across(self.own)]

    def corner(self, *after):
        if not self.native:
            self.second, self.third = tie(self.second, *after), tie(self.third, *after)
            self.sent = (self.second, self.third)
            self.fourth = self.ladder.step(self.second, 3)
            self.far += [self.ladder.across(self.third), self.ladder.across(self.second)]

    def finish(self, *after):
        if self.native:
            self.groups = [lax.all_gather(self.shard, self.ladder.axes, axis=0, tiled=True)]
        else:
            self.fourth = tie(self.fourth, *after)
            self.sent = (self.fourth,)
            self.far += [self.ladder.across(self.fourth)]
            self.groups = [self.own, self.second, self.third, self.fourth] + self.far
        return self.groups


class Scatter:
    def __init__(self, ladder, parts):
        self.ladder, self.native, self.parts = ladder, ladder.native, parts
        self.sent = ()
        if not self.native:
            self.keep = parts[0]
            self.near = ladder.across(parts[1])

    def corner(self, *after):
        if not self.native:
            self.near = tie(self.near, *after)
            total = add_up(self.keep[2:], self.near[2:]).astype(BF16)
            self.sent = (total,)
            self.third = self.ladder.step(total, 3)

    def plane(self, *after):
        if not self.native:
            self.third = tie(self.third, *after)
            total = add_up(self.keep[1], self.near[1], self.third[1]).astype(BF16)
            self.sent = (total,)
            self.second = self.ladder.step(total, 2)

    def spread(self, *after):
        if not self.native:
            second = tie(self.second, *after)
            self.mine, *away = spread_sums(self.ladder.meta, self.keep, self.near, self.third, second)
            self.sent = tuple(away)
            self.last = [self.ladder.flip(part, bit, bit) for part, bit in zip(away, Z_HOPS)]

    def finish(self, *after):
        if self.native:
            return lax.psum_scatter(self.parts[0].astype(F32), self.ladder.axes, scatter_dimension=0, tiled=True)
        total = add_up(self.mine, *[tie(part, *after) for part in self.last])
        self.sent = (total,)
        return total


def nt(a, b):
    return lax.dot_general(a, b, (((1,), (1,)), ((), ())), preferred_element_type=F32)


def nn(a, b):
    return lax.dot_general(a, b, (((1,), (0,)), ((), ())), preferred_element_type=F32)


def fill_bias(lo_ref, segc_ref, padc_ref, segr_ref, bias_ref, nblocks, most):
    def one(qb, _):
        lo = lo_ref[qb]
        q0 = pl.multiple_of(qb * QB, QB)
        segq = segr_ref[pl.ds(qb, 1), :]
        qpos = q0 + lax.broadcasted_iota(jnp.int32, (QB, QB), 1)

        def part(j, _):
            k0 = pl.multiple_of((lo + j) * QB, QB)
            kpos = k0 + lax.broadcasted_iota(jnp.int32, (QB, QB), 0)
            segk = segc_ref[pl.ds(k0, QB), :]
            padk = padc_ref[pl.ds(k0, QB), :]
            ok = (segk == segq) & (kpos <= qpos) & ((padk == 1) | (kpos == qpos))
            bias_ref[qb, pl.ds(pl.multiple_of(j * QB, QB), QB), :] = jnp.where(ok, 0.0, -1e30)
            return 0

        lax.fori_loop(0, qb - lo + 1, part, 0)
        return 0

    lax.fori_loop(0, nblocks, one, 0)


def head_pair(x, scale):
    lane = lax.broadcasted_iota(jnp.int32, x.shape, 1)
    first = jnp.where(lane < HD, scale, 0.0).astype(x.dtype)
    second = jnp.where(lane < HD, 0.0, scale).astype(x.dtype)
    return jnp.concatenate([x * first, x * second], 0)


def attn_fwd_kernel(nblocks, most, many, lo_ref, segc_ref, padc_ref, segr_ref, q_ref, k_ref, v_ref, o_ref, lse_ref, bias_ref, vt_ref):
    @pl.when(pl.program_id(0) == 0)
    def _():
        fill_bias(lo_ref, segc_ref, padc_ref, segr_ref, bias_ref, nblocks, most)

    vt_ref[...] = v_ref[...].T

    def block(qb, _):
        lo = lo_ref[qb]
        q0 = pl.multiple_of(qb * QB, QB)
        k0 = pl.multiple_of(lo * QB, QB)
        for n in range(1, most + 1):
            @pl.when(qb - lo + 1 == n)
            def _(n=n):
                w = n * QB
                bias = bias_ref[qb, 0:w, :]
                bias = jnp.concatenate([bias, bias], 1)
                cols = [slice(128 * i, 128 * (i + 1)) for i in range(many)]
                scores = [nt(k_ref[pl.ds(k0, w), c], head_pair(q_ref[pl.ds(q0, QB), c], HD ** -0.5)) + bias for c in cols]
                tops = [jnp.max(s, 0, keepdims=True) for s in scores]
                parts = [jnp.exp(s - m) for s, m in zip(scores, tops)]
                totals = [jnp.sum(p, 0, keepdims=True) for p in parts]
                outs = [nn(vt_ref[c, pl.ds(k0, w)], (p * (1.0 / t)).astype(BF16)) for c, p, t in zip(cols, parts, totals)]
                for i, (c, o, m, t) in enumerate(zip(cols, outs, tops, totals)):
                    o = jnp.concatenate([o[:HD, :QB], o[HD:, QB:]], 0)
                    o_ref[pl.ds(q0, QB), c] = o.T.astype(BF16)
                    lse_ref[i, pl.ds(qb, 1), :] = m + jnp.log(t)
        return 0

    lax.fori_loop(0, nblocks, block, 0)


def attn_bwd_kernel(nblocks, most, many, lo_ref, segc_ref, padc_ref, segr_ref, q_ref, k_ref, v_ref, do_ref, lse_ref,
                    out_ref, sums_ref, bias_ref, kt_ref, dk_acc, dv_acc):
    @pl.when(pl.program_id(0) == 0)
    def _():
        fill_bias(lo_ref, segc_ref, padc_ref, segr_ref, bias_ref, nblocks, most)

    kt_ref[...] = k_ref[...].T
    dk_acc[...] = jnp.zeros_like(dk_acc)
    dv_acc[...] = jnp.zeros_like(dv_acc)
    sums_ref[...] = jnp.zeros_like(sums_ref)

    def block(qb, _):
        lo = lo_ref[qb]
        q0 = pl.multiple_of(qb * QB, QB)
        k0 = pl.multiple_of(lo * QB, QB)
        for n in range(1, most + 1):
            @pl.when(qb - lo + 1 == n)
            def _(n=n):
                w = n * QB
                bias = bias_ref[qb, 0:w, :]
                bias = jnp.concatenate([bias, bias], 1)
                cols = [slice(128 * i, 128 * (i + 1)) for i in range(many)]
                rows, keys = pl.ds(q0, QB), pl.ds(k0, w)
                q2 = [head_pair(q_ref[rows, c], HD ** -0.5) for c in cols]
                do2 = [head_pair(do_ref[rows, c], 1.0) for c in cols]
                probs = [jnp.exp(nt(k_ref[keys, c], q) + bias - lse_ref[i, pl.ds(qb, 1), :]) for i, (c, q) in enumerate(zip(cols, q2))]
                dprobs = [nt(v_ref[keys, c], do) for c, do in zip(cols, do2)]
                inner = [jnp.sum(p * dp, 0, keepdims=True) for p, dp in zip(probs, dprobs)]
                ds = [(p * (dp - i)).astype(BF16) for p, dp, i in zip(probs, dprobs, inner)]
                for c, p, d, q, do in zip(cols, probs, ds, q2, do2):
                    dv_acc[keys, c] += nn(p.astype(BF16), do)
                    dk_acc[keys, c] += nn(d, q)
                    dq = nn(kt_ref[c, keys], d)
                    dq = jnp.concatenate([dq[:HD, :QB], dq[HD:, QB:]], 0) * (HD ** -0.5)
                    dq = dq.T.astype(BF16)
                    out_ref[0, rows, c] = dq
                    sums_ref[0:1, c] += jnp.sum(dq.astype(F32), 0, keepdims=True)
        return 0

    lax.fori_loop(0, nblocks, block, 0)
    out_ref[1] = dk_acc[...].astype(BF16)
    dv = dv_acc[...].astype(BF16)
    out_ref[2] = dv
    sums_ref[1:2, :] = jnp.sum(dv.astype(F32), 0, keepdims=True)


def mask_inputs(segment_ids, padding_mask):
    length = segment_ids.shape[0]
    nblocks = length // QB
    first = segment_ids.reshape(nblocks, QB)[:, 0]
    start = jnp.sum((segment_ids[None, :] < first[:, None]).astype(jnp.int32), 1)
    lo = start // QB
    segc = jnp.broadcast_to(segment_ids[:, None], (length, QB))
    padc = jnp.broadcast_to(padding_mask[:, None], (length, QB))
    return lo.astype(jnp.int32), segc, padc, segment_ids.reshape(nblocks, QB)


def attn_call(kernel, name, each, operands, specs, shapes, out_specs, scratch, masks, first, pairs, before):
    lo, segc, padc, segr = masks
    length = segc.shape[0]
    nblocks = length // QB
    most = min(nblocks, SPAN // QB + 1)
    whole = lambda p, lo: (0, 0)
    in_specs = [pl.BlockSpec((length, QB), whole), pl.BlockSpec((length, QB), whole), pl.BlockSpec((nblocks, QB), whole)] + specs
    arguments = [lo, segc, padc, segr] + operands
    aliases = {}
    if before is not None:
        aliases = {len(arguments) + i: i for i in range(len(before))}
        in_specs, arguments = in_specs + [pl.BlockSpec(memory_space=pl.ANY)] * len(before), arguments + list(before)

    def body(*refs):
        inputs, rest = refs[: len(arguments) - len(aliases)], refs[len(arguments) :]
        kernel(nblocks, most, MANY, *inputs, *rest)

    return pl.pallas_call(
        body,
        grid_spec=pltpu.PrefetchScalarGridSpec(
            num_scalar_prefetch=1, grid=(pairs // MANY,), in_specs=in_specs, out_specs=out_specs,
            scratch_shapes=[pltpu.VMEM((nblocks, most * QB, QB), F32)] + scratch),
        out_shape=shapes,
        input_output_aliases=aliases,
        compiler_params=pltpu.CompilerParams(vmem_limit_bytes=48 << 20),
        cost_estimate=cost(each * pairs),
        name=name,
    )(*arguments)


def attn_forward(q, k, v, masks, first, pairs, before=None):
    (qa, qo), (ka, ko), (va, vo) = q, k, v
    length, width = qa.shape[0], 128 * MANY
    at = first // MANY
    col = lambda off: pl.BlockSpec((length, width), lambda p, lo: (0, off // MANY + at + p))
    stat = pl.BlockSpec((MANY, length // QB, 2 * QB), lambda p, lo: (at + p, 0, 0))
    total = ko - qo
    return attn_call(
        attn_fwd_kernel, "attn_forward", 2.7, [qa, ka, va], [col(qo), col(ko), col(vo)],
        [jax.ShapeDtypeStruct((length, 128 * total), BF16), jax.ShapeDtypeStruct((total, length // QB, 2 * QB), F32)],
        [col(0), stat], [pltpu.VMEM((width, length), BF16)], masks, first, pairs, before)


def attn_backward(q, k, v, do, lse, masks, first, pairs, before=None):
    (qa, qo), (ka, ko), (va, vo) = q, k, v
    length, width = qa.shape[0], 128 * MANY
    at = first // MANY
    col = lambda off: pl.BlockSpec((length, width), lambda p, lo: (0, off // MANY + at + p))
    stat = pl.BlockSpec((MANY, length // QB, 2 * QB), lambda p, lo: (at + p, 0, 0))
    total = ko - qo
    return attn_call(
        attn_bwd_kernel, "attn_backward", 3.4, [qa, ka, va, do, lse], [col(qo), col(ko), col(vo), col(0), stat],
        [jax.ShapeDtypeStruct((3, length, 128 * total), BF16), jax.ShapeDtypeStruct((8, 128 * total), F32)],
        [pl.BlockSpec((3, length, width), lambda p, lo: (0, 0, at + p)), pl.BlockSpec((8, width), lambda p, lo: (0, at + p))],
        [pltpu.VMEM((width, length), BF16), pltpu.VMEM((length, width), F32), pltpu.VMEM((length, width), F32)],
        masks, first, pairs, before)


ANY = pl.BlockSpec(memory_space=pl.ANY)
META = 1


def params(megabytes=56):
    return pltpu.CompilerParams(vmem_limit_bytes=megabytes << 20)


def tile_shape(native, rows, columns):
    return (1, 1, 1, rows, columns) if native else (4, 4, 2, rows // 32, columns)


def fetch_columns(native, meta, groups, target, start, columns, sem):
    cols = pl.ds(start, columns)
    if native:
        pltpu.make_async_copy(groups[0].at[:, cols], target.at[0, 0, 0], sem).start()
        return
    core = meta[4]
    for t in range(4):
        pltpu.make_async_copy(groups[t].at[:, :, cols], target.at[meta[t], :, core], sem).start()
        pltpu.make_async_copy(groups[4 + t].at[:, :, cols], target.at[meta[t], :, 1 - core], sem).start()


def quarter_shape(native, rows, columns):
    return (1, 1, rows // 4, columns) if native else (4, 2, rows // 32, columns)


def fetch_quarter(native, meta, groups, target, t, sem):
    cols = pl.ds(0, target.shape[-1])
    if native:
        rows = target.shape[-2]
        pltpu.make_async_copy(groups[0].at[pl.ds(t * rows, rows), cols], target.at[0, 0], sem).start()
        return
    core = meta[4]
    pltpu.make_async_copy(groups[t].at[:, :, cols], target.at[:, core], sem).start()
    pltpu.make_async_copy(groups[4 + t].at[:, :, cols], target.at[:, 1 - core], sem).start()


def arrive(target, sem):
    pltpu.make_async_copy(target, target, sem).wait()


def group_specs(groups):
    return [ANY] * len(groups)


def flat(value):
    return value.reshape(-1, value.shape[-1])


def out_blocks(native, rows, columns):
    if native:
        return [jax.ShapeDtypeStruct((rows, columns), BF16)]
    return [jax.ShapeDtypeStruct((4, 4, rows // 32, columns), BF16)] * 2


def push_columns(native, meta, stage, outs, start, columns, sem):
    cols = pl.ds(start, columns)
    if native:
        pltpu.make_async_copy(stage.at[0, 0, 0], outs[0].at[:, cols], sem).start()
        return
    core = meta[4]
    for t in range(4):
        pltpu.make_async_copy(stage.at[meta[t], :, core], outs[0].at[t, :, :, cols], sem).start()
        pltpu.make_async_copy(stage.at[meta[t], :, 1 - core], outs[1].at[FLIP[t], :, :, cols], sem).start()


def each_rows(total, rows, body):
    def step(i, _):
        body(i, pl.ds(pl.multiple_of(i * rows, rows), rows))
        return 0

    lax.fori_loop(0, total // rows, step, 0)


def squares(values, valid):
    return jnp.sum(values * values * valid, 0, keepdims=True)


def scale_of(values):
    return lax.rsqrt(jnp.mean(values * values, -1, keepdims=True) + 1e-05)


SMALL = 16


def pack_smalls(bias_up, bias_qv, bias_out, gain_attn, gain_mlp, bias_down, rows):
    at = lax.broadcasted_iota(jnp.int32, (rows, 128), 0)
    block = jnp.zeros((rows, 128), bias_up.dtype)
    for row, part in enumerate((bias_up, bias_qv, bias_out, gain_attn, gain_mlp, bias_down)):
        block = jnp.where(at == row, jnp.pad(part, (0, 128 - part.shape[0]))[None], block)
    return block


def unpack_smalls(held, up_ref, qkv_ref, lines_ref):
    width = lines_ref.shape[1]
    for shard in range(32):
        up_ref[0:1, shard * 128 : (shard + 1) * 128] = held[shard, 0:1].astype(F32)
    halves = held[...].astype(F32).reshape(16, 2, SMALL, 128)
    halves = halves[:, 0] + pltpu.roll(halves[:, 1], 64, 2)
    fours = held[...].astype(F32).reshape(8, 4, SMALL, 128)
    fours = fours[:, 0] + sum(pltpu.roll(fours[:, i], 32 * i, 2) for i in range(1, 4))
    qkv_ref[...] = jnp.zeros_like(qkv_ref)
    for i in range(16):
        first = i * 128 + (width if i >= 8 else 0)
        qkv_ref[0:1, first : first + 128] = halves[i, 1:2]
    for i in range(8):
        lines_ref[0:4, i * 128 : (i + 1) * 128] = fours[i, 2:6]


def project_kernel(native, tile, count, meta, tok_ref, valid_ref, *rest):
    groups, rest = rest[:count], rest[count:]
    if native:
        up_in, qkv_in, lines_in, out_ref, normed_ref, sq_ref, weight, sems = rest
    else:
        out_ref, normed_ref, sq_ref, up_ref, lines_ref, weight, held, qkv_in, sems = rest
        lines_in = lines_ref
    n, steps = pl.program_id(0), pl.num_programs(0)
    columns = steps * tile

    @pl.when(n == 0)
    def _():
        if not native:
            last = pl.ds(columns, 128)
            for t in range(4):
                for first, side in ((0, meta[4]), (4, 1 - meta[4])):
                    source = groups[first + t].at[:, pl.ds(0, SMALL), last]
                    pltpu.make_async_copy(source, held.at[meta[t], :, side], sems.at[2]).start()
        fetch_columns(native, meta, groups, weight.at[0], 0, tile, sems.at[0])

    @pl.when(n + 1 < steps)
    def _():
        slot = (n + 1) % 2
        fetch_columns(native, meta, groups, weight.at[slot], pl.multiple_of((n + 1) * tile, tile), tile, sems.at[slot])

    @pl.when(n == 0)
    def _():
        if not native:
            arrive(held, sems.at[2])
            unpack_smalls(held[...].reshape(32, SMALL, 128), up_ref, qkv_in, lines_ref)
        sq_ref[...] = jnp.zeros_like(sq_ref)

        def norm(i, at):
            frames = tok_ref[at, :].astype(F32)
            sq_ref[...] += squares(frames, valid_ref[at, :])
            normed_ref[at, :] = (frames * scale_of(frames) * lines_in[1:2, :]).astype(BF16)

        each_rows(tok_ref.shape[0], 256, norm)

    arrive(weight.at[n % 2], sems.at[n % 2])
    bias = qkv_in[0:1, pl.ds(pl.multiple_of(n * tile, tile), tile)]
    out_ref[...] = (nn(normed_ref[...], flat(weight[n % 2])) + bias).astype(BF16)


def project(ladder, tokens, valid, groups, known=None):
    length, width = tokens.shape
    columns, tile, hidden = 3 * width, 512, 4 * width
    native = ladder.native
    whole = lambda n, meta: (0, 0)
    up, lines = pl.BlockSpec((1, hidden), whole), pl.BlockSpec((4, width), whole)
    out_specs = [pl.BlockSpec((length, tile), lambda n, meta: (0, n)), pl.BlockSpec((length, width), whole), pl.BlockSpec((1, width), whole)]
    out_shape = [jax.ShapeDtypeStruct((length, columns), BF16), jax.ShapeDtypeStruct((length, width), BF16),
                 jax.ShapeDtypeStruct((1, width), F32)]
    scratch = [pltpu.VMEM((2,) + tile_shape(native, width, tile), BF16)]
    vectors = [jax.ShapeDtypeStruct((1, hidden), F32), jax.ShapeDtypeStruct((4, width), F32)]
    extra = []
    if native:
        extra = [up, pl.BlockSpec((1, columns), whole), lines]
    else:
        out_specs, out_shape = out_specs + [up, lines], out_shape + vectors
        scratch += [pltpu.VMEM((4, 4, 2, SMALL, 128), BF16), pltpu.VMEM((1, columns), F32)]
    results = pl.pallas_call(
        functools.partial(project_kernel, native, tile, len(groups)),
        grid_spec=pltpu.PrefetchScalarGridSpec(
            num_scalar_prefetch=1, grid=(columns // tile,),
            in_specs=[pl.BlockSpec((length, width), whole), pl.BlockSpec((length, 1), whole)] + group_specs(groups) + extra,
            out_specs=out_specs, scratch_shapes=scratch + [pltpu.SemaphoreType.DMA((3,))]),
        out_shape=out_shape,
        compiler_params=params(),
        cost_estimate=cost(14),
        name="project",
    )(ladder.meta, tokens, valid, *groups, *(known or ()))
    return results if not native else list(results) + [known[0], known[2]]


def gelu_pair(u):
    c, d = 0.7978845608028654, 0.044715
    square = u * u
    bend = 0.5 * jnp.tanh(u * (c + c * d * square))
    half = 0.5 + bend
    slope = half * (1.0 + (0.5 - bend) * (u * (2.0 * c + 6.0 * c * d * square)))
    return (u * half).astype(BF16), slope.astype(BF16)


def expand_kernel(native, tile, count, meta, mixed_ref, tok_ref, lines_ref, valid_ref, up_bias_ref, *rest):
    groups, rest = rest[:count], rest[count:]
    middle_ref, normed_ref, sq_ref, act_ref, slope_ref, middle, out_weight, weight, sems = rest
    n, steps = pl.program_id(0), pl.num_programs(0)
    half = out_weight.shape[-1]
    first = 2 * half
    store = pltpu.make_async_copy(middle, middle_ref, sems.at[4])

    @pl.when(n == 0)
    def _():
        for side in range(2):
            fetch_columns(native, meta, groups, out_weight.at[side], side * half, half, sems.at[2 + side])
        fetch_columns(native, meta, groups, weight.at[0], first, tile, sems.at[0])

    @pl.when(n + 1 < steps)
    def _():
        slot = (n + 1) % 2
        fetch_columns(native, meta, groups, weight.at[slot], pl.multiple_of(first + (n + 1) * tile, tile), tile, sems.at[slot])

    @pl.when(n == 0)
    def _():
        for side in range(2):
            arrive(out_weight.at[side], sems.at[2 + side])
        sq_ref[...] = jnp.zeros_like(sq_ref)

        def part(i, at):
            branch = jnp.concatenate([nn(mixed_ref[at, :], flat(out_weight[side])) for side in range(2)], 1) + lines_ref[0:1, :]
            total = tok_ref[at, :].astype(F32) + branch
            middle[at, :] = total
            normed_ref[at, :] = (total * scale_of(total) * lines_ref[2:3, :]).astype(BF16)
            sq_ref[0:1, :] += squares(branch, valid_ref[at, :])
            sq_ref[1:2, :] += squares(total, valid_ref[at, :])

        each_rows(middle.shape[0], 256, part)
        store.start()

    arrive(weight.at[n % 2], sems.at[n % 2])
    act_ref[...], slope_ref[...] = gelu_pair(nn(normed_ref[...], flat(weight[n % 2])) + up_bias_ref[...])

    @pl.when(n == steps - 1)
    def _():
        store.wait()


def expand(ladder, mixed, tokens, lines, valid, up_bias, groups):
    length, width = tokens.shape
    columns, tile = up_bias.shape[1], 512
    whole = lambda n, meta: (0, 0)
    column = lambda n, meta: (0, n)
    square = pl.BlockSpec((length, width), whole)
    return pl.pallas_call(
        functools.partial(expand_kernel, ladder.native, tile, len(groups)),
        grid_spec=pltpu.PrefetchScalarGridSpec(
            num_scalar_prefetch=1, grid=(columns // tile,),
            in_specs=[square, square, pl.BlockSpec((4, width), whole), pl.BlockSpec((length, 1), whole), pl.BlockSpec((1, tile), column)]
            + group_specs(groups),
            out_specs=[ANY, square, pl.BlockSpec((8, width), whole), pl.BlockSpec((length, tile), column),
                       pl.BlockSpec((length, tile), column)],
            scratch_shapes=[pltpu.VMEM((length, width), F32),
                            pltpu.VMEM((2,) + tile_shape(ladder.native, width, width // 2), BF16),
                            pltpu.VMEM((2,) + tile_shape(ladder.native, width, tile), BF16), pltpu.SemaphoreType.DMA((5,))]),
        out_shape=[jax.ShapeDtypeStruct((length, width), F32), jax.ShapeDtypeStruct((length, width), BF16),
                   jax.ShapeDtypeStruct((8, width), F32)] + [jax.ShapeDtypeStruct((length, columns), BF16)] * 2,
        compiler_params=params(),
        cost_estimate=cost(29),
        name="expand",
    )(ladder.meta, mixed, tokens, lines, valid, up_bias, *groups)


def fetch_turn(native, meta, groups, weight, sems, t, first=0, last=3):
    for at in range(first, last + 1):
        @pl.when(t == max(at - 1, first))
        def _(at=at):
            fetch_quarter(native, meta, groups, weight.at[at % 2], at, sems.at[at % 2])

    arrive(weight.at[t % 2], sems.at[t % 2])


def tn(a, b):
    return lax.dot_general(a, b, (((0,), (0,)), ((), ())), preferred_element_type=F32)


def down_grad_kernel(native, count, meta, act_ref, cot_ref, *rest):
    outs, (sum_ref, stage, sems) = rest[:count], rest[count:]
    t = pl.program_id(0)
    slot = t % 2

    @pl.when(t >= 2)
    def _():
        arrive(stage.at[slot], sems.at[slot])

    stage[slot] = tn(act_ref[...], cot_ref[...]).astype(BF16).reshape(stage.shape[1:])
    if native:
        rows = stage.shape[-2]
        pltpu.make_async_copy(stage.at[slot, 0, 0], outs[0].at[pl.ds(t * rows, rows), :], sems.at[slot]).start()
    else:
        for k in range(4):
            @pl.when(t == k)
            def _(k=k):
                pltpu.make_async_copy(stage.at[slot, :, meta[4]], outs[0].at[k], sems.at[slot]).start()
                pltpu.make_async_copy(stage.at[slot, :, 1 - meta[4]], outs[1].at[FLIP[k]], sems.at[slot]).start()

    @pl.when(t == 0)
    def _():
        sum_ref[...] = jnp.sum(cot_ref[...].astype(F32), 0, keepdims=True)

    @pl.when(t == 3)
    def _():
        arrive(stage.at[1 - slot], sems.at[1 - slot])
        arrive(stage.at[slot], sems.at[slot])


def down_grad(ladder, act, cot):
    length, width = cot.shape
    hidden = act.shape[1]
    outs = out_blocks(ladder.native, hidden, width)
    whole = lambda t, meta: (0, 0)
    return pl.pallas_call(
        functools.partial(down_grad_kernel, ladder.native, len(outs)),
        grid_spec=pltpu.PrefetchScalarGridSpec(
            num_scalar_prefetch=1, grid=(4,),
            in_specs=[pl.BlockSpec((length, hidden // 4), lambda t, meta: (0, meta[t])), pl.BlockSpec((length, width), whole)],
            out_specs=[ANY] * len(outs) + [pl.BlockSpec((1, width), whole)],
            scratch_shapes=[pltpu.VMEM((2,) + quarter_shape(ladder.native, hidden, width), BF16), pltpu.SemaphoreType.DMA((2,))]),
        out_shape=outs + [jax.ShapeDtypeStruct((1, width), F32)],
        compiler_params=params(),
        cost_estimate=cost(14),
        name="down_grad",
    )(ladder.meta, act, cot)


def row_grad_kernel(native, tile, count, meta, left_ref, right_ref, *rest):
    outs, (stage, sems) = rest[:count], rest[count:]
    n, steps = pl.program_id(0), pl.num_programs(0)
    slot = n % 2

    @pl.when(n >= 2)
    def _():
        arrive(stage.at[slot], sems.at[slot])

    stage[slot] = tn(left_ref[...], right_ref[...]).astype(BF16).reshape(stage.shape[1:])
    push_columns(native, meta, stage.at[slot], outs, pl.multiple_of(n * tile, tile), tile, sems.at[slot])

    @pl.when(n == steps - 1)
    def _():
        arrive(stage.at[1 - slot], sems.at[1 - slot])
        arrive(stage.at[slot], sems.at[slot])


def row_grad(ladder, left, right, name):
    length, width = left.shape
    parts, _, each = right.shape
    tile = 512
    per = each // tile
    outs = out_blocks(ladder.native, width, parts * each)
    return pl.pallas_call(
        functools.partial(row_grad_kernel, ladder.native, tile, len(outs)),
        grid_spec=pltpu.PrefetchScalarGridSpec(
            num_scalar_prefetch=1, grid=(parts * per,),
            in_specs=[pl.BlockSpec((length, width), lambda n, meta: (0, 0)),
                      pl.BlockSpec((None, length, tile), lambda n, meta: (n // per, 0, n % per))],
            out_specs=[ANY] * len(outs),
            scratch_shapes=[pltpu.VMEM((2,) + tile_shape(ladder.native, width, tile), BF16), pltpu.SemaphoreType.DMA((2,))]),
        out_shape=outs,
        compiler_params=params(),
        cost_estimate=cost(8),
        name=name,
    )(ladder.meta, left, right)


def norm_grad(grad, source, gain):
    r = scale_of(source)
    hat = source * r
    gain_grad = jnp.sum(grad * hat, 0, keepdims=True)
    scaled = grad * gain
    return r * (scaled - hat * jnp.mean(scaled * hat, -1, keepdims=True)), gain_grad


def back_kernel(native, last, counts, meta, cot_ref, slope_ref, normed_ref, lines_ref, middle_ref, mixed_ref, *rest):
    down_groups, rest = rest[: counts[0]], rest[counts[0] :]
    groups, rest = rest[: counts[0]], rest[counts[0] :]
    if last:
        before, rest = rest[0], rest[2 + counts[1] :]
    pushed, rest = rest[: counts[1]], rest[counts[1] :]
    if last:
        out_ref, branch_ref, mixed_out_ref, sum_ref, up_sum_ref, rest = *rest[:5], rest[5:]
        acc, down_weight, weight, stage, slope, normed, sems, middle, out_weight, mixed = rest
    else:
        after, up_sum_ref, acc, down_weight, weight, stage, slope, normed, sems = rest
    base = 2 if last else 0
    step = pl.program_id(0)
    t = step + base
    width, tile = normed.shape[1], slope.shape[2]
    slot = step

    def columns(at):
        return pl.multiple_of(width + meta[at] * tile, 512)

    loads = [pltpu.make_async_copy(slope_ref.at[:, pl.ds(pl.multiple_of(meta[base + at] * tile, 512), tile)], slope.at[at], sems.at[9 + at])
             for at in range(2)]
    loads.append(pltpu.make_async_copy(normed_ref, normed, sems.at[11]))
    if last:
        loads.append(pltpu.make_async_copy(mixed_ref, mixed, sems.at[12]))

    @pl.when(step == 0)
    def _():
        fetch_quarter(native, meta, down_groups, down_weight.at[0], base, sems.at[0])
        loads[0].start()
        loads[2].start()
        fetch_quarter(native, meta, down_groups, down_weight.at[1], base + 1, sems.at[1])
        loads[1].start()
        for at in range(2):
            fetch_columns(native, meta, groups, weight.at[at], columns(base + at), tile, sems.at[2 + at])
        if last:
            pltpu.make_async_copy(before, acc, sems.at[6]).start()
            pltpu.make_async_copy(middle_ref, middle, sems.at[7]).start()
            fetch_columns(native, meta, groups, out_weight, 0, width, sems.at[8])
            loads[3].start()

    arrive(down_weight.at[slot], sems.at[slot])
    length = acc.shape[0]
    product = nt(cot_ref[...], flat(down_weight[slot]))
    arrive(slope.at[slot], sems.at[9 + slot])
    grad = (product * slope[slot].astype(F32)).astype(BF16)
    up_sum_ref[...] = jnp.sum(grad.astype(F32), 0, keepdims=True)

    @pl.when(step == 0)
    def _():
        loads[2].wait()

    stage[slot] = tn(normed[...], grad).astype(BF16).reshape(stage.shape[1:])
    push_columns(native, meta, stage.at[slot], pushed, columns(t), tile, sems.at[4 + slot])
    arrive(weight.at[slot], sems.at[2 + slot])
    product = nt(grad, flat(weight[slot]))

    @pl.when(step == 0)
    def _():
        if last:
            pltpu.make_async_copy(before, acc, sems.at[6]).wait()
            acc[...] += product
        else:
            acc[...] = product

    @pl.when(step == 1)
    def _():
        acc[...] += product
        if last:
            pltpu.make_async_copy(middle_ref, middle, sems.at[7]).wait()
            sum_ref[...] = jnp.zeros_like(sum_ref)

            def part(i, at):
                back, gain_grad = norm_grad(acc[at, :], middle[at, :], lines_ref[2:3, :])
                total = cot_ref[at, :].astype(F32) + back
                acc[at, :] = total
                branch = total.astype(BF16)
                branch_ref[at, :] = branch
                sum_ref[0:1, :] += gain_grad
                sum_ref[1:2, :] += jnp.sum(branch.astype(F32), 0, keepdims=True)

            each_rows(length, 256, part)
            pltpu.make_async_copy(acc, out_ref, sems.at[6]).start()
            arrive(stage.at[0], sems.at[4])
            loads[3].wait()
            stage[0] = tn(mixed[...], branch_ref[...]).astype(BF16).reshape(stage.shape[1:])
            push_columns(native, meta, stage.at[0], pushed, 0, width, sems.at[4])
            arrive(out_weight, sems.at[8])
            mixed_out_ref[...] = nt(branch_ref[...], flat(out_weight[...])).astype(BF16)
            pltpu.make_async_copy(acc, out_ref, sems.at[6]).wait()
        else:
            pltpu.make_async_copy(acc, after, sems.at[6]).start()
            pltpu.make_async_copy(acc, after, sems.at[6]).wait()
        for at in range(2):
            arrive(stage.at[at], sems.at[4 + at])


def back(ladder, cot, slope, normed, lines, middle, mixed, down_groups, groups, before=None):
    length, width = cot.shape
    hidden, tile = slope.shape[1], slope.shape[1] // 4
    last = before is not None
    base = 2 if last else 0
    whole = lambda t, meta: (0, 0)
    part = lambda t, meta: (0, meta[t + base])
    square = pl.BlockSpec((length, width), whole)
    once = pl.BlockSpec((length, width), whole, pipeline_mode=pl.Buffered(1))
    outs = out_blocks(ladder.native, width, hidden + width)
    counts = (len(groups), len(outs))
    full, wide = jax.ShapeDtypeStruct((length, width), F32), jax.ShapeDtypeStruct((length, width), BF16)
    sums = jax.ShapeDtypeStruct((1, hidden), F32)
    in_specs = [once, ANY, ANY, pl.BlockSpec((4, width), whole), ANY, ANY]
    in_specs += [ANY] * (2 * counts[0])
    operands = [ladder.meta, cot, slope, normed, lines, middle, mixed, *down_groups, *groups]
    scratch = [pltpu.VMEM((length, width), F32), pltpu.VMEM((2,) + quarter_shape(ladder.native, hidden, width), BF16),
               pltpu.VMEM((2,) + tile_shape(ladder.native, width, tile), BF16),
               pltpu.VMEM((2,) + tile_shape(ladder.native, width, tile), BF16), pltpu.VMEM((2, length, tile), BF16),
               pltpu.VMEM((length, width), BF16), pltpu.SemaphoreType.DMA((13,))]
    aliases = {}
    if last:
        aliases = {len(operands) + 1 + i: i for i in range(counts[1])}
        aliases[len(operands) + 1 + counts[1]] = counts[1] + 4
        operands += list(before)
        in_specs += [ANY] * (2 + counts[1])
        out_specs = [ANY] * counts[1] + [ANY, square, square, pl.BlockSpec((8, width), whole)]
        out_shape = outs + [full, wide, wide, jax.ShapeDtypeStruct((8, width), F32)]
        scratch += [pltpu.VMEM((length, width), F32), pltpu.VMEM(tile_shape(ladder.native, width, width), BF16),
                    pltpu.VMEM((length, width), BF16)]
    else:
        out_specs, out_shape = [ANY] * counts[1] + [ANY], outs + [full]
    return pl.pallas_call(
        functools.partial(back_kernel, ladder.native, last, counts),
        grid_spec=pltpu.PrefetchScalarGridSpec(
            num_scalar_prefetch=1, grid=(2,), in_specs=in_specs, out_specs=out_specs + [pl.BlockSpec((1, tile), part)],
            scratch_shapes=scratch),
        out_shape=out_shape + [jax.ShapeDtypeStruct((1, hidden), F32)],
        input_output_aliases=aliases,
        compiler_params=params(),
        cost_estimate=cost(30 if last else 20),
        name="back",
    )(*operands)


def contract_kernel(native, first, meta, act_ref, lines_ref, valid_ref, middle_ref, *rest):
    groups, (out_ref, sq_ref, acc, middle, weight, sems) = rest[:-6], rest[-6:]
    t = pl.program_id(0)
    load = pltpu.make_async_copy(middle_ref.at[pl.ds(first, acc.shape[0]), :], middle, sems.at[2])

    @pl.when(t == 0)
    def _():
        load.start()

    fetch_turn(native, meta, groups, weight, sems, t)
    product = nn(act_ref[...], flat(weight[t % 2]))

    @pl.when(t == 0)
    def _():
        acc[...] = product

    @pl.when(t > 0)
    def _():
        acc[...] += product

    @pl.when(t == 3)
    def _():
        load.wait()
        sq_ref[...] = jnp.zeros_like(sq_ref)
        rows = 256

        def part(i, _):
            at = pl.ds(pl.multiple_of(i * rows, rows), rows)
            branch = acc[at, :] + lines_ref[3:4, :]
            final = middle[at, :] + branch
            out_ref[at, :] = final.astype(BF16)
            sq_ref[0:1, :] += squares(branch, valid_ref[at, :])
            sq_ref[1:2, :] += squares(final, valid_ref[at, :])
            return 0

        lax.fori_loop(0, acc.shape[0] // rows, part, 0)


def contract(ladder, act, middle, lines, valid, groups, part, parts):
    length, width = middle.shape
    length //= parts
    hidden = act.shape[1]
    whole = lambda t, meta: (0, 0)
    return pl.pallas_call(
        functools.partial(contract_kernel, ladder.native, part * length),
        grid_spec=pltpu.PrefetchScalarGridSpec(
            num_scalar_prefetch=1, grid=(4,),
            in_specs=[pl.BlockSpec((length, hidden // 4), lambda t, meta: (part, meta[t])), pl.BlockSpec((4, width), whole),
                      pl.BlockSpec((length, 1), lambda t, meta: (part, 0)), ANY] + group_specs(groups),
            out_specs=[pl.BlockSpec((length, width), whole), pl.BlockSpec((8, width), whole)],
            scratch_shapes=[pltpu.VMEM((length, width), F32), pltpu.VMEM((length, width), F32),
                            pltpu.VMEM((2,) + quarter_shape(ladder.native, hidden, width), BF16), pltpu.SemaphoreType.DMA((3,))]),
        out_shape=[jax.ShapeDtypeStruct((length, width), BF16), jax.ShapeDtypeStruct((8, width), F32)],
        compiler_params=params(),
        cost_estimate=cost(16 // parts),
        name="contract",
    )(ladder.meta, act, lines, valid, middle, *groups)


def input_grad_kernel(native, calls, meta, *rest):
    grads, (tok_ref, middle_ref, lines_ref), rest = rest[:calls], rest[calls : calls + 3], rest[calls + 3 :]
    groups, (out_ref, sum_ref, acc, middle, weight, sems) = rest[:-6], rest[-6:]
    t = pl.program_id(0)
    load = pltpu.make_async_copy(middle_ref, middle, sems.at[2])

    @pl.when(t == 0)
    def _():
        load.start()

    fetch_turn(native, meta, groups, weight, sems, t)
    width = acc.shape[1]
    quarter = width // 4
    rows = flat(weight[t % 2])
    each = width // calls
    product = 0.0
    for part in range(3):
        for call in range(calls):
            first = part * width + call * each
            product += nt(grads[call][part], rows[:, first : first + each])
    acc[:, pl.ds(pl.multiple_of(meta[t] * quarter, quarter), quarter)] = product

    @pl.when(t == 3)
    def _():
        load.wait()
        sum_ref[...] = jnp.zeros_like(sum_ref)
        rows = 256

        def part(i, _):
            at = pl.ds(pl.multiple_of(i * rows, rows), rows)
            back, gain_grad = norm_grad(acc[at, :], tok_ref[at, :].astype(F32), lines_ref[1:2, :])
            out_ref[at, :] = (middle[at, :] + back).astype(BF16)
            sum_ref[0:1, :] += gain_grad
            return 0

        lax.fori_loop(0, acc.shape[0] // rows, part, 0)


def input_grad(ladder, grads, tokens, grad_middle, lines, groups):
    length, width = tokens.shape
    calls = len(grads)
    whole = lambda t, meta: (0, 0)
    square = pl.BlockSpec((length, width), whole)
    return pl.pallas_call(
        functools.partial(input_grad_kernel, ladder.native, calls),
        grid_spec=pltpu.PrefetchScalarGridSpec(
            num_scalar_prefetch=1, grid=(4,),
            in_specs=[pl.BlockSpec((3, length, width // calls), lambda t, meta: (0, 0, 0))] * calls + [square, ANY, pl.BlockSpec((4, width), whole)]
            + group_specs(groups),
            out_specs=[square, pl.BlockSpec((8, width), whole)],
            scratch_shapes=[pltpu.VMEM((length, width), F32), pltpu.VMEM((length, width), F32),
                            pltpu.VMEM((2,) + quarter_shape(ladder.native, width, 3 * width), BF16), pltpu.SemaphoreType.DMA((3,))]),
        out_shape=[jax.ShapeDtypeStruct((length, width), BF16), jax.ShapeDtypeStruct((8, width), F32)],
        compiler_params=params(),
        cost_estimate=cost(18),
        name="input_grad",
    )(ladder.meta, *grads, tokens, grad_middle, lines, *groups)


def local(ladder, tokens, cotangent, segment_ids, padding_mask, w_qkv, bias_qv, w_out, bias_out, gain_attn, gain_mlp,
          w_up, bias_up, w_down, bias_down):
    length, width = tokens.shape[1], tokens.shape[2]
    count = ladder.count
    ladder.place()
    tokens, cotangent = tokens[0], cotangent[0]

    def sent(*flows):
        return [value for flow in flows for value in flow.sent]

    sizes = [part.shape[0] for part in (bias_qv, bias_out, gain_attn, gain_mlp, bias_up, bias_down)]
    total = sum(sizes)
    ends = np.cumsum([0] + sizes)
    known = None
    block = None
    if ladder.native:
        every = lambda part: lax.all_gather(part, ladder.axes, axis=0, tiled=True).astype(F32)[None]
        qv = every(bias_qv)
        known = [every(bias_up), jnp.concatenate([qv[:, :width], jnp.zeros((1, width), F32), qv[:, width:]], 1),
                 jnp.concatenate([every(bias_out), every(gain_attn), every(gain_mlp), every(bias_down)], 0)]
    else:
        block = pack_smalls(bias_up, bias_qv, bias_out, gain_attn, gain_mlp, bias_down, w_qkv.shape[0])
    qkv, down = Gather(ladder, w_qkv, True, block), Gather(ladder, w_down, False)
    qkv.start()
    rest = Gather(ladder, jnp.concatenate([w_out, w_up], 1), False)
    masks = mask_inputs(segment_ids[0], padding_mask[0])
    valid = padding_mask[0].astype(F32)[:, None]
    qkv.plane()
    rest.start(*qkv.sent)
    qkv.corner()
    rest.low()
    qkv_groups = qkv.finish()
    rest.plane()
    down.start(*rest.sent)
    projected, normed_in, sq_frames, up_bias, lines = project(ladder, tie(tokens, *sent(rest), *masks), valid, qkv_groups, known)
    per = width // 128
    calls = 2
    each = per // calls

    down.low(projected)
    projected = tie(projected, *sent(down))
    per = width // 128
    calls = 2
    each = per // calls

    def triple():
        return (projected, 0), (projected, per), (projected, 2 * per)

    heads = None
    for call in range(calls):
        heads = attn_forward(*triple(), masks, call * each, each, heads)
        if call == 0:
            rest.corner(heads[0])
            projected = tie(projected, heads[0], *sent(rest), *down.others)
    mixed, lse = heads
    rest_groups = rest.finish(mixed)
    down.plane(*rest.sent)
    middle, normed_mid, sq_middle, act, slope = expand(
        ladder, tie(mixed, *sent(down)), tokens, lines, valid, up_bias, rest_groups)

    down.corner(act)
    *down_parts, sum_down = down_grad(ladder, tie(act, *sent(down)), cotangent)
    flow_down = Scatter(ladder, down_parts)
    down_groups = down.finish(sum_down)
    *first_parts, first_acc, first_sum = back(
        ladder, tie(cotangent, sum_down), slope, normed_mid, lines, middle, mixed, down_groups, rest_groups)
    flow_down.corner(first_acc)
    *rest_parts, grad_middle, grad_branch, grad_mixed, sum_middle, sum_up = back(
        ladder, tie(cotangent, *sent(flow_down)), slope, normed_mid, lines, middle, mixed, down_groups, rest_groups,
        [first_acc, *first_parts, first_sum])
    flow_rest = Scatter(ladder, rest_parts)
    flow_down.plane(grad_mixed)
    grad_mixed = tie(grad_mixed, *sent(flow_down))
    heads = None
    for call in range(calls):
        heads = attn_backward(*triple(), grad_mixed, lse, masks, call * each, each, heads)
        if call == 0:
            flow_down.spread(heads[0])
            flow_rest.corner(heads[0])
            grad_mixed = tie(grad_mixed, heads[0], *sent(flow_down, flow_rest))
    grad_projected, sum_qv = heads
    own_down = flow_down.finish(grad_projected)
    flow_qkv = Scatter(ladder, row_grad(ladder, normed_in, tie(grad_projected, *sent(flow_down)), "qkv_grad"))
    flow_rest.plane(*flow_qkv.parts)
    finals = []

    def finish_rows(part, *after):
        out, squares_out = contract(ladder, tie(act, *after), middle, lines, valid, down_groups, part, 2)
        finals.append(squares_out)
        return out

    outputs = [finish_rows(0, *flow_qkv.parts, *sent(flow_rest))]
    flow_rest.spread(outputs[0])
    flow_qkv.corner(outputs[0])
    tail = tie(tokens, *sent(flow_rest, flow_qkv))
    grad_tokens, sum_in = input_grad(ladder, [grad_projected], tail, grad_middle, lines, qkv_groups)
    flow_qkv.plane(grad_tokens)
    outputs.append(finish_rows(1, *sent(flow_qkv)))
    flow_qkv.spread(outputs[1], *([] if ladder.native else flow_rest.last))

    sq_final = finals[0] + finals[1]
    members = [sq_frames, sq_middle[1:2], sq_final[1:2], sq_middle[:1], sq_final[:1], valid.reshape(1, -1)]
    members = jnp.sum(jnp.concatenate(members, 0), 1)
    small_grads = [sum_qv[:2], sum_middle[1:2], sum_in[:1], sum_middle[:1], sum_up, sum_down]
    table = jnp.concatenate([g.reshape(count, -1) for g in small_grads] + [jnp.broadcast_to(members, (count, 6))], 1)
    table = jnp.pad(table, ((0, 0), (0, -table.shape[1] % 128)))
    own_small = ladder.scatter_small(tie(table, *sent(flow_qkv)))
    own_qkv = flow_qkv.finish(own_small)
    own_rest = flow_rest.finish(own_small)
    output = jnp.concatenate([tie(outputs[0], own_small), outputs[1]], 0)

    owned = [own_small[ends[i] : ends[i + 1]] for i in range(6)]
    totals = own_small[total : total + 6]
    stats = jnp.sqrt(totals[:5] / (totals[5] * width))
    own_out, own_up = own_rest[:, :width], own_rest[:, width:]
    return (output[None], grad_tokens[None], own_qkv, owned[0], own_out, owned[1], owned[2], owned[3], own_up, owned[4],
            own_down, owned[5], stats, totals[5:6])


def solution(mesh):
    rows, wide, flat = P(("dp", "fsdp"), None, None), P(("dp", "fsdp"), None), P(("dp", "fsdp"))
    return jax.shard_map(
        functools.partial(local, Ladder(mesh)),
        mesh=mesh,
        in_specs=(rows, rows, wide, wide, wide, flat, wide, flat, flat, flat, wide, flat, wide, flat),
        out_specs=(rows, rows, wide, flat, wide, flat, flat, flat, wide, flat, wide, flat, P(), P()),
        check_vma=False,
    )
```

```python
import functools

import jax
import jax.numpy as jnp
import numpy as np
from jax import lax
from jax.experimental import pallas as pl
from jax.experimental.pallas import tpu as pltpu
from jax.sharding import PartitionSpec as P

HD = 64
QB = 128
SPAN = 512
MANY = 4
WEIGH = 2
PARTS = 1
F32 = jnp.float32
BF16 = jnp.bfloat16

CORE = 1
Z_HOPS = (2, 4, 6)
MIX = ((0, 1, 2, 3), (0, 2, 1, 3))
FLIP = (0, 2, 1, 3)
HOPS = ((4, 2, 8, 16), (4, 2, 16, 8))


def tie(value, *others):
    return lax.optimization_barrier((value,) + others)[0]


def add_up(*terms):
    return sum(term.astype(F32) for term in terms)


def cost(microseconds):
    return pl.CostEstimate(flops=int(WEIGH * microseconds * 1.15e9), transcendentals=0, bytes_accessed=0)


class Ladder:
    def __init__(self, mesh):
        self.count = int(np.prod(list(mesh.shape.values())))
        self.native = dict(mesh.shape) != {"dp": 4, "fsdp": 8}
        self.axes = ("dp", "fsdp")

    def place(self):
        if self.native:
            self.meta = jnp.array([0, 1, 2, 3, 0, 0], jnp.int32)
            return
        me = lax.axis_index(self.axes)
        odd = (me & CORE) == 1
        mix = jnp.where(odd, jnp.array(MIX[1], jnp.int32), jnp.array(MIX[0], jnp.int32))
        self.meta = jnp.concatenate([(me >> 3) ^ mix, (me & CORE)[None], ((me >> 1) & 3)[None]])

    def flip(self, value, even, odd):
        bits = (even, odd)
        return lax.ppermute(value, self.axes, [(i, i ^ bits[i & CORE]) for i in range(self.count)])

    def step(self, value, level):
        return self.flip(value, HOPS[0][level], HOPS[1][level])

    def across(self, value):
        return self.flip(value, CORE, CORE)

    def scatter_small(self, table):
        return jnp.sum(lax.all_to_all(table, self.axes, 0, 0, tiled=True), 0)


def place_kernel(meta, *refs):
    pieces, beside, out_ref = refs[:4], refs[4:-1], refs[-1]
    columns = pieces[0].shape[1]
    for k in range(4):
        out_ref[meta[5] ^ k, :, :columns] = pieces[k][...]
        if beside:
            out_ref[meta[5] ^ k, :, columns:] = beside[k][...]


def place_group(meta, pieces, beside):
    rows = pieces[0].shape[0]
    operands = list(pieces) + list(beside)
    columns = sum(part[0].shape[1] for part in (pieces, beside) if part)
    whole = lambda n, meta: (0, 0)
    return pl.pallas_call(
        place_kernel,
        grid_spec=pltpu.PrefetchScalarGridSpec(
            num_scalar_prefetch=1, grid=(1,), in_specs=[pl.BlockSpec(part.shape, whole) for part in operands],
            out_specs=pl.BlockSpec((4, rows, columns), lambda n, meta: (0, 0, 0))),
        out_shape=jax.ShapeDtypeStruct((4, rows, columns), pieces[0].dtype),
        cost_estimate=cost(2),
        name="place_group",
    )(meta, *operands)


def spread_kernel(meta, *refs):
    parts, outs = refs[:16], refs[16:]
    for k in range(4):
        total = sum(part[...].astype(F32) for part in parts[4 * k : 4 * k + 4])
        outs[k][...] = total.astype(outs[k].dtype)


def spread_sums(meta, keep, near, third, second):
    _, rows, columns = second.shape
    tile = columns // PARTS
    specs, operands = [], []
    for k in range(4):
        group = pl.BlockSpec((None, rows, tile), lambda n, meta, k=k: (meta[5] ^ k, 0, n))
        pair = pl.BlockSpec((None, None, rows, tile), lambda n, meta, k=k: (0, meta[5] ^ k, 0, n))
        specs += [pair, pair, pair, group]
        operands += [keep, near, third, second]
    out = pl.BlockSpec((rows, tile), lambda n, meta: (0, n))
    return pl.pallas_call(
        spread_kernel,
        grid_spec=pltpu.PrefetchScalarGridSpec(num_scalar_prefetch=1, grid=(columns // tile,), in_specs=specs, out_specs=[out] * 4),
        out_shape=[jax.ShapeDtypeStruct((rows, columns), F32)] + [jax.ShapeDtypeStruct((rows, columns), BF16)] * 3,
        cost_estimate=cost(3),
        name="spread_sums",
    )(meta, *operands)


class Gather:
    def __init__(self, ladder, shard, direct, beside=None):
        self.beside = beside
        self.ladder, self.shard, self.native, self.direct = ladder, shard, ladder.native, direct
        self.sent, self.others = (), []

    def start(self, *after):
        if not self.native:
            self.shard = tie(self.shard, *after)
            self.sent = (self.shard,)
            bits = Z_HOPS if self.direct else Z_HOPS[1:2]
            self.others = [self.ladder.flip(self.shard, bit, bit) for bit in bits]
            self.sides = []
            if self.beside is not None:
                beside = tie(self.beside, self.others[0])
                self.sides = [beside] + [self.ladder.flip(beside, bit, bit) for bit in bits]

    def low(self, *after):
        if not self.native:
            one, two = tie(self.others[0], *after), self.shard
            high = (self.ladder.meta[5] >> 1) == 1
            self.pair = jnp.where(high, jnp.stack([one, two]), jnp.stack([two, one]))
            self.sent = (self.pair,)
            self.others = [self.ladder.flip(self.pair, Z_HOPS[0], Z_HOPS[0])]

    def plane(self, *after):
        if not self.native:
            others = [tie(other, *after) for other in self.others]
            if self.direct:
                self.own = place_group(self.ladder.meta, [self.shard] + others, self.sides)
            else:
                one, two = others[0], self.pair
                low = (self.ladder.meta[5] & 1) == 1
                own = jnp.where(low, jnp.stack([one, two], 1), jnp.stack([two, one], 1))
                self.own = own.reshape((4,) + self.shard.shape)
            self.sent = (self.own,)
            self.second = self.ladder.step(self.own, 2)
            self.third = self.ladder.step(self.own, 3)
            self.far = [self.ladder.across(self.own)]

    def corner(self, *after):
        if not self.native:
            self.second, self.third = tie(self.second, *after), tie(self.third, *after)
            self.sent = (self.second, self.third)
            self.fourth = self.ladder.step(self.second, 3)
            self.far += [self.ladder.across(self.third), self.ladder.across(self.second)]

    def finish(self, *after):
        if self.native:
            self.groups = [lax.all_gather(self.shard, self.ladder.axes, axis=0, tiled=True)]
        else:
            self.fourth = tie(self.fourth, *after)
            self.sent = (self.fourth,)
            self.far += [self.ladder.across(self.fourth)]
            self.groups = [self.own, self.second, self.third, self.fourth] + self.far
        return self.groups


class Scatter:
    def __init__(self, ladder, parts):
        self.ladder, self.native, self.parts = ladder, ladder.native, parts
        self.sent = ()
        if not self.native:
            self.keep = parts[0]
            self.near = ladder.across(parts[1])

    def corner(self, *after):
        if not self.native:
            self.near = tie(self.near, *after)
            total = add_up(self.keep[2:], self.near[2:]).astype(BF16)
            self.sent = (total,)
            self.third = self.ladder.step(total, 3)

    def plane(self, *after):
        if not self.native:
            self.third = tie(self.third, *after)
            total = add_up(self.keep[1], self.near[1], self.third[1]).astype(BF16)
            self.sent = (total,)
            self.second = self.ladder.step(total, 2)

    def spread(self, *after):
        if not self.native:
            second = tie(self.second, *after)
            self.mine, *away = spread_sums(self.ladder.meta, self.keep, self.near, self.third, second)
            self.sent = tuple(away)
            self.last = [self.ladder.flip(part, bit, bit) for part, bit in zip(away, Z_HOPS)]

    def finish(self, *after):
        if self.native:
            return lax.psum_scatter(self.parts[0].astype(F32), self.ladder.axes, scatter_dimension=0, tiled=True)
        total = add_up(self.mine, *[tie(part, *after) for part in self.last])
        self.sent = (total,)
        return total


def nt(a, b):
    return lax.dot_general(a, b, (((1,), (1,)), ((), ())), preferred_element_type=F32)


def nn(a, b):
    return lax.dot_general(a, b, (((1,), (0,)), ((), ())), preferred_element_type=F32)


def fill_bias(lo_ref, segc_ref, padc_ref, segr_ref, bias_ref, nblocks, most):
    def one(qb, _):
        lo = lo_ref[qb]
        q0 = pl.multiple_of(qb * QB, QB)
        segq = segr_ref[pl.ds(qb, 1), :]
        qpos = q0 + lax.broadcasted_iota(jnp.int32, (QB, QB), 1)

        def part(j, _):
            k0 = pl.multiple_of((lo + j) * QB, QB)
            kpos = k0 + lax.broadcasted_iota(jnp.int32, (QB, QB), 0)
            segk = segc_ref[pl.ds(k0, QB), :]
            padk = padc_ref[pl.ds(k0, QB), :]
            ok = (segk == segq) & (kpos <= qpos) & ((padk == 1) | (kpos == qpos))
            bias_ref[qb, pl.ds(pl.multiple_of(j * QB, QB), QB), :] = jnp.where(ok, 0.0, -1e30)
            return 0

        lax.fori_loop(0, qb - lo + 1, part, 0)
        return 0

    lax.fori_loop(0, nblocks, one, 0)


def head_pair(x, scale):
    lane = lax.broadcasted_iota(jnp.int32, x.shape, 1)
    first = jnp.where(lane < HD, scale, 0.0).astype(x.dtype)
    second = jnp.where(lane < HD, 0.0, scale).astype(x.dtype)
    return jnp.concatenate([x * first, x * second], 0)


def attn_fwd_kernel(nblocks, most, many, lo_ref, segc_ref, padc_ref, segr_ref, q_ref, k_ref, v_ref, o_ref, lse_ref, bias_ref, vt_ref):
    @pl.when(pl.program_id(0) == 0)
    def _():
        fill_bias(lo_ref, segc_ref, padc_ref, segr_ref, bias_ref, nblocks, most)

    vt_ref[...] = v_ref[...].T

    def block(qb, _):
        lo = lo_ref[qb]
        q0 = pl.multiple_of(qb * QB, QB)
        k0 = pl.multiple_of(lo * QB, QB)
        for n in range(1, most + 1):
            @pl.when(qb - lo + 1 == n)
            def _(n=n):
                w = n * QB
                bias = bias_ref[qb, 0:w, :]
                bias = jnp.concatenate([bias, bias], 1)
                cols = [slice(128 * i, 128 * (i + 1)) for i in range(many)]
                scores = [nt(k_ref[pl.ds(k0, w), c], head_pair(q_ref[pl.ds(q0, QB), c], HD ** -0.5)) + bias for c in cols]
                tops = [jnp.max(s, 0, keepdims=True) for s in scores]
                parts = [jnp.exp(s - m) for s, m in zip(scores, tops)]
                totals = [jnp.sum(p, 0, keepdims=True) for p in parts]
                outs = [nn(vt_ref[c, pl.ds(k0, w)], (p * (1.0 / t)).astype(BF16)) for c, p, t in zip(cols, parts, totals)]
                for i, (c, o, m, t) in enumerate(zip(cols, outs, tops, totals)):
                    o = jnp.concatenate([o[:HD, :QB], o[HD:, QB:]], 0)
                    o_ref[pl.ds(q0, QB), c] = o.T.astype(BF16)
                    lse_ref[i, pl.ds(qb, 1), :] = m + jnp.log(t)
        return 0

    lax.fori_loop(0, nblocks, block, 0)


def attn_bwd_kernel(nblocks, most, many, lo_ref, segc_ref, padc_ref, segr_ref, q_ref, k_ref, v_ref, do_ref, lse_ref,
                    out_ref, sums_ref, bias_ref, kt_ref, dk_acc, dv_acc):
    @pl.when(pl.program_id(0) == 0)
    def _():
        fill_bias(lo_ref, segc_ref, padc_ref, segr_ref, bias_ref, nblocks, most)

    kt_ref[...] = k_ref[...].T
    dk_acc[...] = jnp.zeros_like(dk_acc)
    dv_acc[...] = jnp.zeros_like(dv_acc)
    sums_ref[...] = jnp.zeros_like(sums_ref)

    def block(qb, _):
        lo = lo_ref[qb]
        q0 = pl.multiple_of(qb * QB, QB)
        k0 = pl.multiple_of(lo * QB, QB)
        for n in range(1, most + 1):
            @pl.when(qb - lo + 1 == n)
            def _(n=n):
                w = n * QB
                bias = bias_ref[qb, 0:w, :]
                bias = jnp.concatenate([bias, bias], 1)
                cols = [slice(128 * i, 128 * (i + 1)) for i in range(many)]
                rows, keys = pl.ds(q0, QB), pl.ds(k0, w)
                q2 = [head_pair(q_ref[rows, c], HD ** -0.5) for c in cols]
                do2 = [head_pair(do_ref[rows, c], 1.0) for c in cols]
                probs = [jnp.exp(nt(k_ref[keys, c], q) + bias - lse_ref[i, pl.ds(qb, 1), :]) for i, (c, q) in enumerate(zip(cols, q2))]
                dprobs = [nt(v_ref[keys, c], do) for c, do in zip(cols, do2)]
                inner = [jnp.sum(p * dp, 0, keepdims=True) for p, dp in zip(probs, dprobs)]
                ds = [(p * (dp - i)).astype(BF16) for p, dp, i in zip(probs, dprobs, inner)]
                for c, p, d, q, do in zip(cols, probs, ds, q2, do2):
                    dv_acc[keys, c] += nn(p.astype(BF16), do)
                    dk_acc[keys, c] += nn(d, q)
                    dq = nn(kt_ref[c, keys], d)
                    dq = jnp.concatenate([dq[:HD, :QB], dq[HD:, QB:]], 0) * (HD ** -0.5)
                    dq = dq.T.astype(BF16)
                    out_ref[0, rows, c] = dq
                    sums_ref[0:1, c] += jnp.sum(dq.astype(F32), 0, keepdims=True)
        return 0

    lax.fori_loop(0, nblocks, block, 0)
    out_ref[1] = dk_acc[...].astype(BF16)
    dv = dv_acc[...].astype(BF16)
    out_ref[2] = dv
    sums_ref[1:2, :] = jnp.sum(dv.astype(F32), 0, keepdims=True)


def mask_inputs(segment_ids, padding_mask):
    length = segment_ids.shape[0]
    nblocks = length // QB
    first = segment_ids.reshape(nblocks, QB)[:, 0]
    start = jnp.sum((segment_ids[None, :] < first[:, None]).astype(jnp.int32), 1)
    lo = start // QB
    segc = jnp.broadcast_to(segment_ids[:, None], (length, QB))
    padc = jnp.broadcast_to(padding_mask[:, None], (length, QB))
    return lo.astype(jnp.int32), segc, padc, segment_ids.reshape(nblocks, QB)


def attn_call(kernel, name, each, operands, specs, shapes, out_specs, scratch, masks, first, pairs, before):
    lo, segc, padc, segr = masks
    length = segc.shape[0]
    nblocks = length // QB
    most = min(nblocks, SPAN // QB + 1)
    whole = lambda p, lo: (0, 0)
    in_specs = [pl.BlockSpec((length, QB), whole), pl.BlockSpec((length, QB), whole), pl.BlockSpec((nblocks, QB), whole)] + specs
    arguments = [lo, segc, padc, segr] + operands
    aliases = {}
    if before is not None:
        aliases = {len(arguments) + i: i for i in range(len(before))}
        in_specs, arguments = in_specs + [pl.BlockSpec(memory_space=pl.ANY)] * len(before), arguments + list(before)

    def body(*refs):
        inputs, rest = refs[: len(arguments) - len(aliases)], refs[len(arguments) :]
        kernel(nblocks, most, MANY, *inputs, *rest)

    return pl.pallas_call(
        body,
        grid_spec=pltpu.PrefetchScalarGridSpec(
            num_scalar_prefetch=1, grid=(pairs // MANY,), in_specs=in_specs, out_specs=out_specs,
            scratch_shapes=[pltpu.VMEM((nblocks, most * QB, QB), F32)] + scratch),
        out_shape=shapes,
        input_output_aliases=aliases,
        compiler_params=pltpu.CompilerParams(vmem_limit_bytes=48 << 20),
        cost_estimate=cost(each * pairs),
        name=name,
    )(*arguments)


def attn_forward(q, k, v, masks, first, pairs, before=None):
    (qa, qo), (ka, ko), (va, vo) = q, k, v
    length, width = qa.shape[0], 128 * MANY
    at = first // MANY
    col = lambda off: pl.BlockSpec((length, width), lambda p, lo: (0, off // MANY + at + p))
    stat = pl.BlockSpec((MANY, length // QB, 2 * QB), lambda p, lo: (at + p, 0, 0))
    total = ko - qo
    return attn_call(
        attn_fwd_kernel, "attn_forward", 2.7, [qa, ka, va], [col(qo), col(ko), col(vo)],
        [jax.ShapeDtypeStruct((length, 128 * total), BF16), jax.ShapeDtypeStruct((total, length // QB, 2 * QB), F32)],
        [col(0), stat], [pltpu.VMEM((width, length), BF16)], masks, first, pairs, before)


def attn_backward(q, k, v, do, lse, masks, first, pairs, before=None):
    (qa, qo), (ka, ko), (va, vo) = q, k, v
    length, width = qa.shape[0], 128 * MANY
    at = first // MANY
    col = lambda off: pl.BlockSpec((length, width), lambda p, lo: (0, off // MANY + at + p))
    stat = pl.BlockSpec((MANY, length // QB, 2 * QB), lambda p, lo: (at + p, 0, 0))
    total = ko - qo
    return attn_call(
        attn_bwd_kernel, "attn_backward", 3.4, [qa, ka, va, do, lse], [col(qo), col(ko), col(vo), col(0), stat],
        [jax.ShapeDtypeStruct((3, length, 128 * total), BF16), jax.ShapeDtypeStruct((8, 128 * total), F32)],
        [pl.BlockSpec((3, length, width), lambda p, lo: (0, 0, at + p)), pl.BlockSpec((8, width), lambda p, lo: (0, at + p))],
        [pltpu.VMEM((width, length), BF16), pltpu.VMEM((length, width), F32), pltpu.VMEM((length, width), F32)],
        masks, first, pairs, before)


ANY = pl.BlockSpec(memory_space=pl.ANY)
META = 1


def params(megabytes=56):
    return pltpu.CompilerParams(vmem_limit_bytes=megabytes << 20)


def tile_shape(native, rows, columns):
    return (1, 1, 1, rows, columns) if native else (4, 4, 2, rows // 32, columns)


def fetch_columns(native, meta, groups, target, start, columns, sem):
    cols = pl.ds(start, columns)
    if native:
        pltpu.make_async_copy(groups[0].at[:, cols], target.at[0, 0, 0], sem).start()
        return
    core = meta[4]
    for t in range(4):
        pltpu.make_async_copy(groups[t].at[:, :, cols], target.at[meta[t], :, core], sem).start()
        pltpu.make_async_copy(groups[4 + t].at[:, :, cols], target.at[meta[t], :, 1 - core], sem).start()


def quarter_shape(native, rows, columns):
    return (1, 1, rows // 4, columns) if native else (4, 2, rows // 32, columns)


def fetch_quarter(native, meta, groups, target, t, sem):
    cols = pl.ds(0, target.shape[-1])
    if native:
        rows = target.shape[-2]
        pltpu.make_async_copy(groups[0].at[pl.ds(t * rows, rows), cols], target.at[0, 0], sem).start()
        return
    core = meta[4]
    pltpu.make_async_copy(groups[t].at[:, :, cols], target.at[:, core], sem).start()
    pltpu.make_async_copy(groups[4 + t].at[:, :, cols], target.at[:, 1 - core], sem).start()


def arrive(target, sem):
    pltpu.make_async_copy(target, target, sem).wait()


def group_specs(groups):
    return [ANY] * len(groups)


def flat(value):
    return value.reshape(-1, value.shape[-1])


def out_blocks(native, rows, columns):
    if native:
        return [jax.ShapeDtypeStruct((rows, columns), BF16)]
    return [jax.ShapeDtypeStruct((4, 4, rows // 32, columns), BF16)] * 2


def push_columns(native, meta, stage, outs, start, columns, sem):
    cols = pl.ds(start, columns)
    if native:
        pltpu.make_async_copy(stage.at[0, 0, 0], outs[0].at[:, cols], sem).start()
        return
    core = meta[4]
    for t in range(4):
        pltpu.make_async_copy(stage.at[meta[t], :, core], outs[0].at[t, :, :, cols], sem).start()
        pltpu.make_async_copy(stage.at[meta[t], :, 1 - core], outs[1].at[FLIP[t], :, :, cols], sem).start()


def each_rows(total, rows, body):
    def step(i, _):
        body(i, pl.ds(pl.multiple_of(i * rows, rows), rows))
        return 0

    lax.fori_loop(0, total // rows, step, 0)


def squares(values, valid):
    return jnp.sum(values * values * valid, 0, keepdims=True)


def scale_of(values):
    return lax.rsqrt(jnp.mean(values * values, -1, keepdims=True) + 1e-05)


SMALL = 16


def pack_smalls(bias_up, bias_qv, bias_out, gain_attn, gain_mlp, bias_down, rows):
    at = lax.broadcasted_iota(jnp.int32, (rows, 128), 0)
    block = jnp.zeros((rows, 128), bias_up.dtype)
    for row, part in enumerate((bias_up, bias_qv, bias_out, gain_attn, gain_mlp, bias_down)):
        block = jnp.where(at == row, jnp.pad(part, (0, 128 - part.shape[0]))[None], block)
    return block


def unpack_smalls(held, up_ref, qkv_ref, lines_ref):
    width = lines_ref.shape[1]
    for shard in range(32):
        up_ref[0:1, shard * 128 : (shard + 1) * 128] = held[shard, 0:1].astype(F32)
    halves = held[...].astype(F32).reshape(16, 2, SMALL, 128)
    halves = halves[:, 0] + pltpu.roll(halves[:, 1], 64, 2)
    fours = held[...].astype(F32).reshape(8, 4, SMALL, 128)
    fours = fours[:, 0] + sum(pltpu.roll(fours[:, i], 32 * i, 2) for i in range(1, 4))
    qkv_ref[...] = jnp.zeros_like(qkv_ref)
    for i in range(16):
        first = i * 128 + (width if i >= 8 else 0)
        qkv_ref[0:1, first : first + 128] = halves[i, 1:2]
    for i in range(8):
        lines_ref[0:4, i * 128 : (i + 1) * 128] = fours[i, 2:6]


def project_kernel(native, tile, count, meta, tok_ref, valid_ref, *rest):
    groups, rest = rest[:count], rest[count:]
    if native:
        up_in, qkv_in, lines_in, out_ref, normed_ref, sq_ref, weight, sems = rest
    else:
        out_ref, normed_ref, sq_ref, up_ref, lines_ref, weight, held, qkv_in, sems = rest
        lines_in = lines_ref
    n, steps = pl.program_id(0), pl.num_programs(0)
    columns = steps * tile

    @pl.when(n == 0)
    def _():
        if not native:
            last = pl.ds(columns, 128)
            for t in range(4):
                for first, side in ((0, meta[4]), (4, 1 - meta[4])):
                    source = groups[first + t].at[:, pl.ds(0, SMALL), last]
                    pltpu.make_async_copy(source, held.at[meta[t], :, side], sems.at[2]).start()
        fetch_columns(native, meta, groups, weight.at[0], 0, tile, sems.at[0])

    @pl.when(n + 1 < steps)
    def _():
        slot = (n + 1) % 2
        fetch_columns(native, meta, groups, weight.at[slot], pl.multiple_of((n + 1) * tile, tile), tile, sems.at[slot])

    @pl.when(n == 0)
    def _():
        if not native:
            arrive(held, sems.at[2])
            unpack_smalls(held[...].reshape(32, SMALL, 128), up_ref, qkv_in, lines_ref)
        sq_ref[...] = jnp.zeros_like(sq_ref)

        def norm(i, at):
            frames = tok_ref[at, :].astype(F32)
            sq_ref[...] += squares(frames, valid_ref[at, :])
            normed_ref[at, :] = (frames * scale_of(frames) * lines_in[1:2, :]).astype(BF16)

        each_rows(tok_ref.shape[0], 256, norm)

    arrive(weight.at[n % 2], sems.at[n % 2])
    bias = qkv_in[0:1, pl.ds(pl.multiple_of(n * tile, tile), tile)]
    out_ref[...] = (nn(normed_ref[...], flat(weight[n % 2])) + bias).astype(BF16)


def project(ladder, tokens, valid, groups, known=None):
    length, width = tokens.shape
    columns, tile, hidden = 3 * width, 512, 4 * width
    native = ladder.native
    whole = lambda n, meta: (0, 0)
    up, lines = pl.BlockSpec((1, hidden), whole), pl.BlockSpec((4, width), whole)
    out_specs = [pl.BlockSpec((length, tile), lambda n, meta: (0, n)), pl.BlockSpec((length, width), whole), pl.BlockSpec((1, width), whole)]
    out_shape = [jax.ShapeDtypeStruct((length, columns), BF16), jax.ShapeDtypeStruct((length, width), BF16),
                 jax.ShapeDtypeStruct((1, width), F32)]
    scratch = [pltpu.VMEM((2,) + tile_shape(native, width, tile), BF16)]
    vectors = [jax.ShapeDtypeStruct((1, hidden), F32), jax.ShapeDtypeStruct((4, width), F32)]
    extra = []
    if native:
        extra = [up, pl.BlockSpec((1, columns), whole), lines]
    else:
        out_specs, out_shape = out_specs + [up, lines], out_shape + vectors
        scratch += [pltpu.VMEM((4, 4, 2, SMALL, 128), BF16), pltpu.VMEM((1, columns), F32)]
    results = pl.pallas_call(
        functools.partial(project_kernel, native, tile, len(groups)),
        grid_spec=pltpu.PrefetchScalarGridSpec(
            num_scalar_prefetch=1, grid=(columns // tile,),
            in_specs=[pl.BlockSpec((length, width), whole), pl.BlockSpec((length, 1), whole)] + group_specs(groups) + extra,
            out_specs=out_specs, scratch_shapes=scratch + [pltpu.SemaphoreType.DMA((3,))]),
        out_shape=out_shape,
        compiler_params=params(),
        cost_estimate=cost(14),
        name="project",
    )(ladder.meta, tokens, valid, *groups, *(known or ()))
    return results if not native else list(results) + [known[0], known[2]]


def gelu_pair(u):
    c, d = 0.7978845608028654, 0.044715
    square = u * u
    bend = 0.5 * jnp.tanh(u * (c + c * d * square))
    half = 0.5 + bend
    slope = half * (1.0 + (0.5 - bend) * (u * (2.0 * c + 6.0 * c * d * square)))
    return (u * half).astype(BF16), slope.astype(BF16)


def expand_kernel(native, tile, count, meta, mixed_ref, tok_ref, lines_ref, valid_ref, up_bias_ref, *rest):
    groups, rest = rest[:count], rest[count:]
    middle_ref, normed_ref, sq_ref, act_ref, slope_ref, middle, out_weight, weight, sems = rest
    n, steps = pl.program_id(0), pl.num_programs(0)
    half = out_weight.shape[-1]
    first = 2 * half
    store = pltpu.make_async_copy(middle, middle_ref, sems.at[4])

    @pl.when(n == 0)
    def _():
        for side in range(2):
            fetch_columns(native, meta, groups, out_weight.at[side], side * half, half, sems.at[2 + side])
        fetch_columns(native, meta, groups, weight.at[0], first, tile, sems.at[0])

    @pl.when(n + 1 < steps)
    def _():
        slot = (n + 1) % 2
        fetch_columns(native, meta, groups, weight.at[slot], pl.multiple_of(first + (n + 1) * tile, tile), tile, sems.at[slot])

    @pl.when(n == 0)
    def _():
        for side in range(2):
            arrive(out_weight.at[side], sems.at[2 + side])
        sq_ref[...] = jnp.zeros_like(sq_ref)

        def part(i, at):
            branch = jnp.concatenate([nn(mixed_ref[at, :], flat(out_weight[side])) for side in range(2)], 1) + lines_ref[0:1, :]
            total = tok_ref[at, :].astype(F32) + branch
            middle[at, :] = total
            normed_ref[at, :] = (total * scale_of(total) * lines_ref[2:3, :]).astype(BF16)
            sq_ref[0:1, :] += squares(branch, valid_ref[at, :])
            sq_ref[1:2, :] += squares(total, valid_ref[at, :])

        each_rows(middle.shape[0], 256, part)
        store.start()

    arrive(weight.at[n % 2], sems.at[n % 2])
    act_ref[...], slope_ref[...] = gelu_pair(nn(normed_ref[...], flat(weight[n % 2])) + up_bias_ref[...])

    @pl.when(n == steps - 1)
    def _():
        store.wait()


def expand(ladder, mixed, tokens, lines, valid, up_bias, groups):
    length, width = tokens.shape
    columns, tile = up_bias.shape[1], 512
    whole = lambda n, meta: (0, 0)
    column = lambda n, meta: (0, n)
    square = pl.BlockSpec((length, width), whole)
    return pl.pallas_call(
        functools.partial(expand_kernel, ladder.native, tile, len(groups)),
        grid_spec=pltpu.PrefetchScalarGridSpec(
            num_scalar_prefetch=1, grid=(columns // tile,),
            in_specs=[square, square, pl.BlockSpec((4, width), whole), pl.BlockSpec((length, 1), whole), pl.BlockSpec((1, tile), column)]
            + group_specs(groups),
            out_specs=[ANY, square, pl.BlockSpec((8, width), whole), pl.BlockSpec((length, tile), column),
                       pl.BlockSpec((length, tile), column)],
            scratch_shapes=[pltpu.VMEM((length, width), F32),
                            pltpu.VMEM((2,) + tile_shape(ladder.native, width, width // 2), BF16),
                            pltpu.VMEM((2,) + tile_shape(ladder.native, width, tile), BF16), pltpu.SemaphoreType.DMA((5,))]),
        out_shape=[jax.ShapeDtypeStruct((length, width), F32), jax.ShapeDtypeStruct((length, width), BF16),
                   jax.ShapeDtypeStruct((8, width), F32)] + [jax.ShapeDtypeStruct((length, columns), BF16)] * 2,
        compiler_params=params(),
        cost_estimate=cost(29),
        name="expand",
    )(ladder.meta, mixed, tokens, lines, valid, up_bias, *groups)


def fetch_turn(native, meta, groups, weight, sems, t, first=0, last=3):
    for at in range(first, last + 1):
        @pl.when(t == max(at - 1, first))
        def _(at=at):
            fetch_quarter(native, meta, groups, weight.at[at % 2], at, sems.at[at % 2])

    arrive(weight.at[t % 2], sems.at[t % 2])


def tn(a, b):
    return lax.dot_general(a, b, (((0,), (0,)), ((), ())), preferred_element_type=F32)


def down_grad_kernel(native, count, meta, act_ref, cot_ref, *rest):
    outs, (sum_ref, stage, sems) = rest[:count], rest[count:]
    t = pl.program_id(0)
    slot = t % 2

    @pl.when(t >= 2)
    def _():
        arrive(stage.at[slot], sems.at[slot])

    stage[slot] = tn(act_ref[...], cot_ref[...]).astype(BF16).reshape(stage.shape[1:])
    if native:
        rows = stage.shape[-2]
        pltpu.make_async_copy(stage.at[slot, 0, 0], outs[0].at[pl.ds(t * rows, rows), :], sems.at[slot]).start()
    else:
        for k in range(4):
            @pl.when(t == k)
            def _(k=k):
                pltpu.make_async_copy(stage.at[slot, :, meta[4]], outs[0].at[k], sems.at[slot]).start()
                pltpu.make_async_copy(stage.at[slot, :, 1 - meta[4]], outs[1].at[FLIP[k]], sems.at[slot]).start()

    @pl.when(t == 0)
    def _():
        sum_ref[...] = jnp.sum(cot_ref[...].astype(F32), 0, keepdims=True)

    @pl.when(t == 3)
    def _():
        arrive(stage.at[1 - slot], sems.at[1 - slot])
        arrive(stage.at[slot], sems.at[slot])


def down_grad(ladder, act, cot):
    length, width = cot.shape
    hidden = act.shape[1]
    outs = out_blocks(ladder.native, hidden, width)
    whole = lambda t, meta: (0, 0)
    return pl.pallas_call(
        functools.partial(down_grad_kernel, ladder.native, len(outs)),
        grid_spec=pltpu.PrefetchScalarGridSpec(
            num_scalar_prefetch=1, grid=(4,),
            in_specs=[pl.BlockSpec((length, hidden // 4), lambda t, meta: (0, meta[t])), pl.BlockSpec((length, width), whole)],
            out_specs=[ANY] * len(outs) + [pl.BlockSpec((1, width), whole)],
            scratch_shapes=[pltpu.VMEM((2,) + quarter_shape(ladder.native, hidden, width), BF16), pltpu.SemaphoreType.DMA((2,))]),
        out_shape=outs + [jax.ShapeDtypeStruct((1, width), F32)],
        compiler_params=params(),
        cost_estimate=cost(14),
        name="down_grad",
    )(ladder.meta, act, cot)


def row_grad_kernel(native, tile, count, meta, left_ref, right_ref, *rest):
    outs, (stage, sems) = rest[:count], rest[count:]
    n, steps = pl.program_id(0), pl.num_programs(0)
    slot = n % 2

    @pl.when(n >= 2)
    def _():
        arrive(stage.at[slot], sems.at[slot])

    stage[slot] = tn(left_ref[...], right_ref[...]).astype(BF16).reshape(stage.shape[1:])
    push_columns(native, meta, stage.at[slot], outs, pl.multiple_of(n * tile, tile), tile, sems.at[slot])

    @pl.when(n == steps - 1)
    def _():
        arrive(stage.at[1 - slot], sems.at[1 - slot])
        arrive(stage.at[slot], sems.at[slot])


def row_grad(ladder, left, right, name):
    length, width = left.shape
    parts, _, each = right.shape
    tile = 512
    per = each // tile
    outs = out_blocks(ladder.native, width, parts * each)
    return pl.pallas_call(
        functools.partial(row_grad_kernel, ladder.native, tile, len(outs)),
        grid_spec=pltpu.PrefetchScalarGridSpec(
            num_scalar_prefetch=1, grid=(parts * per,),
            in_specs=[pl.BlockSpec((length, width), lambda n, meta: (0, 0)),
                      pl.BlockSpec((None, length, tile), lambda n, meta: (n // per, 0, n % per))],
            out_specs=[ANY] * len(outs),
            scratch_shapes=[pltpu.VMEM((2,) + tile_shape(ladder.native, width, tile), BF16), pltpu.SemaphoreType.DMA((2,))]),
        out_shape=outs,
        compiler_params=params(),
        cost_estimate=cost(8),
        name=name,
    )(ladder.meta, left, right)


def norm_grad(grad, source, gain):
    r = scale_of(source)
    hat = source * r
    gain_grad = jnp.sum(grad * hat, 0, keepdims=True)
    scaled = grad * gain
    return r * (scaled - hat * jnp.mean(scaled * hat, -1, keepdims=True)), gain_grad


def back_kernel(native, last, counts, meta, cot_ref, slope_ref, normed_ref, lines_ref, middle_ref, mixed_ref, *rest):
    down_groups, rest = rest[: counts[0]], rest[counts[0] :]
    groups, rest = rest[: counts[0]], rest[counts[0] :]
    if last:
        before, rest = rest[0], rest[2 + counts[1] :]
    pushed, rest = rest[: counts[1]], rest[counts[1] :]
    if last:
        out_ref, branch_ref, mixed_out_ref, sum_ref, up_sum_ref, rest = *rest[:5], rest[5:]
        acc, down_weight, weight, stage, slope, normed, sems, middle, out_weight, mixed = rest
    else:
        after, up_sum_ref, acc, down_weight, weight, stage, slope, normed, sems = rest
    base = 2 if last else 0
    step = pl.program_id(0)
    t = step + base
    width, tile = normed.shape[1], slope.shape[2]
    slot = step

    def columns(at):
        return pl.multiple_of(width + meta[at] * tile, 512)

    loads = [pltpu.make_async_copy(slope_ref.at[:, pl.ds(pl.multiple_of(meta[base + at] * tile, 512), tile)], slope.at[at], sems.at[9 + at])
             for at in range(2)]
    loads.append(pltpu.make_async_copy(normed_ref, normed, sems.at[11]))
    if last:
        loads.append(pltpu.make_async_copy(mixed_ref, mixed, sems.at[12]))

    @pl.when(step == 0)
    def _():
        fetch_quarter(native, meta, down_groups, down_weight.at[0], base, sems.at[0])
        loads[0].start()
        loads[2].start()
        fetch_quarter(native, meta, down_groups, down_weight.at[1], base + 1, sems.at[1])
        loads[1].start()
        for at in range(2):
            fetch_columns(native, meta, groups, weight.at[at], columns(base + at), tile, sems.at[2 + at])
        if last:
            pltpu.make_async_copy(before, acc, sems.at[6]).start()
            pltpu.make_async_copy(middle_ref, middle, sems.at[7]).start()
            fetch_columns(native, meta, groups, out_weight, 0, width, sems.at[8])
            loads[3].start()

    arrive(down_weight.at[slot], sems.at[slot])
    length = acc.shape[0]
    product = nt(cot_ref[...], flat(down_weight[slot]))
    arrive(slope.at[slot], sems.at[9 + slot])
    grad = (product * slope[slot].astype(F32)).astype(BF16)
    up_sum_ref[...] = jnp.sum(grad.astype(F32), 0, keepdims=True)

    @pl.when(step == 0)
    def _():
        loads[2].wait()

    stage[slot] = tn(normed[...], grad).astype(BF16).reshape(stage.shape[1:])
    push_columns(native, meta, stage.at[slot], pushed, columns(t), tile, sems.at[4 + slot])
    arrive(weight.at[slot], sems.at[2 + slot])
    product = nt(grad, flat(weight[slot]))

    @pl.when(step == 0)
    def _():
        if last:
            pltpu.make_async_copy(before, acc, sems.at[6]).wait()
            acc[...] += product
        else:
            acc[...] = product

    @pl.when(step == 1)
    def _():
        acc[...] += product
        if last:
            pltpu.make_async_copy(middle_ref, middle, sems.at[7]).wait()
            sum_ref[...] = jnp.zeros_like(sum_ref)

            def part(i, at):
                back, gain_grad = norm_grad(acc[at, :], middle[at, :], lines_ref[2:3, :])
                total = cot_ref[at, :].astype(F32) + back
                acc[at, :] = total
                branch = total.astype(BF16)
                branch_ref[at, :] = branch
                sum_ref[0:1, :] += gain_grad
                sum_ref[1:2, :] += jnp.sum(branch.astype(F32), 0, keepdims=True)

            each_rows(length, 256, part)
            pltpu.make_async_copy(acc, out_ref, sems.at[6]).start()
            arrive(stage.at[0], sems.at[4])
            loads[3].wait()
            stage[0] = tn(mixed[...], branch_ref[...]).astype(BF16).reshape(stage.shape[1:])
            push_columns(native, meta, stage.at[0], pushed, 0, width, sems.at[4])
            arrive(out_weight, sems.at[8])
            mixed_out_ref[...] = nt(branch_ref[...], flat(out_weight[...])).astype(BF16)
            pltpu.make_async_copy(acc, out_ref, sems.at[6]).wait()
        else:
            pltpu.make_async_copy(acc, after, sems.at[6]).start()
            pltpu.make_async_copy(acc, after, sems.at[6]).wait()
        for at in range(2):
            arrive(stage.at[at], sems.at[4 + at])


def back(ladder, cot, slope, normed, lines, middle, mixed, down_groups, groups, before=None):
    length, width = cot.shape
    hidden, tile = slope.shape[1], slope.shape[1] // 4
    last = before is not None
    base = 2 if last else 0
    whole = lambda t, meta: (0, 0)
    part = lambda t, meta: (0, meta[t + base])
    square = pl.BlockSpec((length, width), whole)
    once = pl.BlockSpec((length, width), whole, pipeline_mode=pl.Buffered(1))
    outs = out_blocks(ladder.native, width, hidden + width)
    counts = (len(groups), len(outs))
    full, wide = jax.ShapeDtypeStruct((length, width), F32), jax.ShapeDtypeStruct((length, width), BF16)
    sums = jax.ShapeDtypeStruct((1, hidden), F32)
    in_specs = [once, ANY, ANY, pl.BlockSpec((4, width), whole), ANY, ANY]
    in_specs += [ANY] * (2 * counts[0])
    operands = [ladder.meta, cot, slope, normed, lines, middle, mixed, *down_groups, *groups]
    scratch = [pltpu.VMEM((length, width), F32), pltpu.VMEM((2,) + quarter_shape(ladder.native, hidden, width), BF16),
               pltpu.VMEM((2,) + tile_shape(ladder.native, width, tile), BF16),
               pltpu.VMEM((2,) + tile_shape(ladder.native, width, tile), BF16), pltpu.VMEM((2, length, tile), BF16),
               pltpu.VMEM((length, width), BF16), pltpu.SemaphoreType.DMA((13,))]
    aliases = {}
    if last:
        aliases = {len(operands) + 1 + i: i for i in range(counts[1])}
        aliases[len(operands) + 1 + counts[1]] = counts[1] + 4
        operands += list(before)
        in_specs += [ANY] * (2 + counts[1])
        out_specs = [ANY] * counts[1] + [ANY, square, square, pl.BlockSpec((8, width), whole)]
        out_shape = outs + [full, wide, wide, jax.ShapeDtypeStruct((8, width), F32)]
        scratch += [pltpu.VMEM((length, width), F32), pltpu.VMEM(tile_shape(ladder.native, width, width), BF16),
                    pltpu.VMEM((length, width), BF16)]
    else:
        out_specs, out_shape = [ANY] * counts[1] + [ANY], outs + [full]
    return pl.pallas_call(
        functools.partial(back_kernel, ladder.native, last, counts),
        grid_spec=pltpu.PrefetchScalarGridSpec(
            num_scalar_prefetch=1, grid=(2,), in_specs=in_specs, out_specs=out_specs + [pl.BlockSpec((1, tile), part)],
            scratch_shapes=scratch),
        out_shape=out_shape + [jax.ShapeDtypeStruct((1, hidden), F32)],
        input_output_aliases=aliases,
        compiler_params=params(),
        cost_estimate=cost(30 if last else 20),
        name="back",
    )(*operands)


def contract_kernel(native, first, meta, act_ref, lines_ref, valid_ref, middle_ref, *rest):
    groups, (out_ref, sq_ref, acc, middle, weight, sems) = rest[:-6], rest[-6:]
    t = pl.program_id(0)
    load = pltpu.make_async_copy(middle_ref.at[pl.ds(first, acc.shape[0]), :], middle, sems.at[2])

    @pl.when(t == 0)
    def _():
        load.start()

    fetch_turn(native, meta, groups, weight, sems, t)
    product = nn(act_ref[...], flat(weight[t % 2]))

    @pl.when(t == 0)
    def _():
        acc[...] = product

    @pl.when(t > 0)
    def _():
        acc[...] += product

    @pl.when(t == 3)
    def _():
        load.wait()
        sq_ref[...] = jnp.zeros_like(sq_ref)
        rows = 256

        def part(i, _):
            at = pl.ds(pl.multiple_of(i * rows, rows), rows)
            branch = acc[at, :] + lines_ref[3:4, :]
            final = middle[at, :] + branch
            out_ref[at, :] = final.astype(BF16)
            sq_ref[0:1, :] += squares(branch, valid_ref[at, :])
            sq_ref[1:2, :] += squares(final, valid_ref[at, :])
            return 0

        lax.fori_loop(0, acc.shape[0] // rows, part, 0)


def contract(ladder, act, middle, lines, valid, groups, part, parts):
    length, width = middle.shape
    length //= parts
    hidden = act.shape[1]
    whole = lambda t, meta: (0, 0)
    return pl.pallas_call(
        functools.partial(contract_kernel, ladder.native, part * length),
        grid_spec=pltpu.PrefetchScalarGridSpec(
            num_scalar_prefetch=1, grid=(4,),
            in_specs=[pl.BlockSpec((length, hidden // 4), lambda t, meta: (part, meta[t])), pl.BlockSpec((4, width), whole),
                      pl.BlockSpec((length, 1), lambda t, meta: (part, 0)), ANY] + group_specs(groups),
            out_specs=[pl.BlockSpec((length, width), whole), pl.BlockSpec((8, width), whole)],
            scratch_shapes=[pltpu.VMEM((length, width), F32), pltpu.VMEM((length, width), F32),
                            pltpu.VMEM((2,) + quarter_shape(ladder.native, hidden, width), BF16), pltpu.SemaphoreType.DMA((3,))]),
        out_shape=[jax.ShapeDtypeStruct((length, width), BF16), jax.ShapeDtypeStruct((8, width), F32)],
        compiler_params=params(),
        cost_estimate=cost(16 // parts),
        name="contract",
    )(ladder.meta, act, lines, valid, middle, *groups)


def input_grad_kernel(native, calls, meta, *rest):
    grads, (tok_ref, middle_ref, lines_ref), rest = rest[:calls], rest[calls : calls + 3], rest[calls + 3 :]
    groups, (out_ref, sum_ref, acc, middle, weight, sems) = rest[:-6], rest[-6:]
    t = pl.program_id(0)
    load = pltpu.make_async_copy(middle_ref, middle, sems.at[2])

    @pl.when(t == 0)
    def _():
        load.start()

    fetch_turn(native, meta, groups, weight, sems, t)
    width = acc.shape[1]
    quarter = width // 4
    rows = flat(weight[t % 2])
    each = width // calls
    product = 0.0
    for part in range(3):
        for call in range(calls):
            first = part * width + call * each
            product += nt(grads[call][part], rows[:, first : first + each])
    acc[:, pl.ds(pl.multiple_of(meta[t] * quarter, quarter), quarter)] = product

    @pl.when(t == 3)
    def _():
        load.wait()
        sum_ref[...] = jnp.zeros_like(sum_ref)
        rows = 256

        def part(i, _):
            at = pl.ds(pl.multiple_of(i * rows, rows), rows)
            back, gain_grad = norm_grad(acc[at, :], tok_ref[at, :].astype(F32), lines_ref[1:2, :])
            out_ref[at, :] = (middle[at, :] + back).astype(BF16)
            sum_ref[0:1, :] += gain_grad
            return 0

        lax.fori_loop(0, acc.shape[0] // rows, part, 0)


def input_grad(ladder, grads, tokens, grad_middle, lines, groups):
    length, width = tokens.shape
    calls = len(grads)
    whole = lambda t, meta: (0, 0)
    square = pl.BlockSpec((length, width), whole)
    return pl.pallas_call(
        functools.partial(input_grad_kernel, ladder.native, calls),
        grid_spec=pltpu.PrefetchScalarGridSpec(
            num_scalar_prefetch=1, grid=(4,),
            in_specs=[pl.BlockSpec((3, length, width // calls), lambda t, meta: (0, 0, 0))] * calls + [square, ANY, pl.BlockSpec((4, width), whole)]
            + group_specs(groups),
            out_specs=[square, pl.BlockSpec((8, width), whole)],
            scratch_shapes=[pltpu.VMEM((length, width), F32), pltpu.VMEM((length, width), F32),
                            pltpu.VMEM((2,) + quarter_shape(ladder.native, width, 3 * width), BF16), pltpu.SemaphoreType.DMA((3,))]),
        out_shape=[jax.ShapeDtypeStruct((length, width), BF16), jax.ShapeDtypeStruct((8, width), F32)],
        compiler_params=params(),
        cost_estimate=cost(18),
        name="input_grad",
    )(ladder.meta, *grads, tokens, grad_middle, lines, *groups)


def local(ladder, tokens, cotangent, segment_ids, padding_mask, w_qkv, bias_qv, w_out, bias_out, gain_attn, gain_mlp,
          w_up, bias_up, w_down, bias_down):
    length, width = tokens.shape[1], tokens.shape[2]
    count = ladder.count
    ladder.place()
    tokens, cotangent = tokens[0], cotangent[0]

    def sent(*flows):
        return [value for flow in flows for value in flow.sent]

    sizes = [part.shape[0] for part in (bias_qv, bias_out, gain_attn, gain_mlp, bias_up, bias_down)]
    total = sum(sizes)
    ends = np.cumsum([0] + sizes)
    known = None
    block = None
    if ladder.native:
        every = lambda part: lax.all_gather(part, ladder.axes, axis=0, tiled=True).astype(F32)[None]
        qv = every(bias_qv)
        known = [every(bias_up), jnp.concatenate([qv[:, :width], jnp.zeros((1, width), F32), qv[:, width:]], 1),
                 jnp.concatenate([every(bias_out), every(gain_attn), every(gain_mlp), every(bias_down)], 0)]
    else:
        block = pack_smalls(bias_up, bias_qv, bias_out, gain_attn, gain_mlp, bias_down, w_qkv.shape[0])
    qkv, down = Gather(ladder, w_qkv, True, block), Gather(ladder, w_down, False)
    qkv.start()
    rest = Gather(ladder, jnp.concatenate([w_out, w_up], 1), False)
    masks = mask_inputs(segment_ids[0], padding_mask[0])
    valid = padding_mask[0].astype(F32)[:, None]
    qkv.plane()
    rest.start(*qkv.sent)
    qkv.corner()
    rest.low()
    qkv_groups = qkv.finish()
    rest.plane()
    down.start(*rest.sent)
    projected, normed_in, sq_frames, up_bias, lines = project(ladder, tie(tokens, *sent(rest), *masks), valid, qkv_groups, known)
    per = width // 128
    calls = 2
    each = per // calls

    down.low(projected)
    projected = tie(projected, *sent(down))
    per = width // 128
    calls = 2
    each = per // calls

    def triple():
        return (projected, 0), (projected, per), (projected, 2 * per)

    heads = None
    for call in range(calls):
        heads = attn_forward(*triple(), masks, call * each, each, heads)
        if call == 0:
            rest.corner(heads[0])
            projected = tie(projected, heads[0], *sent(rest), *down.others)
    mixed, lse = heads
    rest_groups = rest.finish(mixed)
    down.plane(*rest.sent)
    middle, normed_mid, sq_middle, act, slope = expand(
        ladder, tie(mixed, *sent(down)), tokens, lines, valid, up_bias, rest_groups)

    down.corner(act)
    *down_parts, sum_down = down_grad(ladder, tie(act, *sent(down)), cotangent)
    flow_down = Scatter(ladder, down_parts)
    down_groups = down.finish(sum_down)
    *first_parts, first_acc, first_sum = back(
        ladder, tie(cotangent, sum_down), slope, normed_mid, lines, middle, mixed, down_groups, rest_groups)
    flow_down.corner(first_acc)
    *rest_parts, grad_middle, grad_branch, grad_mixed, sum_middle, sum_up = back(
        ladder, tie(cotangent, *sent(flow_down)), slope, normed_mid, lines, middle, mixed, down_groups, rest_groups,
        [first_acc, *first_parts, first_sum])
    flow_rest = Scatter(ladder, rest_parts)
    flow_down.plane(grad_mixed)
    grad_mixed = tie(grad_mixed, *sent(flow_down))
    heads = None
    for call in range(calls):
        heads = attn_backward(*triple(), grad_mixed, lse, masks, call * each, each, heads)
        if call == 0:
            flow_down.spread(heads[0])
            flow_rest.corner(heads[0])
            grad_mixed = tie(grad_mixed, heads[0], *sent(flow_down, flow_rest))
    grad_projected, sum_qv = heads
    own_down = flow_down.finish(grad_projected)
    flow_qkv = Scatter(ladder, row_grad(ladder, normed_in, tie(grad_projected, *sent(flow_down)), "qkv_grad"))
    flow_rest.plane(*flow_qkv.parts)
    finals = []

    def finish_rows(part, *after):
        out, squares_out = contract(ladder, tie(act, *after), middle, lines, valid, down_groups, part, 2)
        finals.append(squares_out)
        return out

    outputs = [finish_rows(0, *flow_qkv.parts, *sent(flow_rest))]
    flow_rest.spread(outputs[0])
    flow_qkv.corner(outputs[0])
    tail = tie(tokens, *sent(flow_rest, flow_qkv))
    grad_tokens, sum_in = input_grad(ladder, [grad_projected], tail, grad_middle, lines, qkv_groups)
    flow_qkv.plane(grad_tokens)
    outputs.append(finish_rows(1, *sent(flow_qkv)))
    flow_qkv.spread(outputs[1], *([] if ladder.native else flow_rest.last))

    sq_final = finals[0] + finals[1]
    members = [sq_frames, sq_middle[1:2], sq_final[1:2], sq_middle[:1], sq_final[:1], valid.reshape(1, -1)]
    members = jnp.sum(jnp.concatenate(members, 0), 1)
    small_grads = [sum_qv[:2], sum_middle[1:2], sum_in[:1], sum_middle[:1], sum_up, sum_down]
    table = jnp.concatenate([g.reshape(count, -1) for g in small_grads] + [jnp.broadcast_to(members, (count, 6))], 1)
    table = jnp.pad(table, ((0, 0), (0, -table.shape[1] % 128)))
    own_small = ladder.scatter_small(tie(table, *sent(flow_qkv), *([] if ladder.native else flow_qkv.last[2:])))
    own_qkv = flow_qkv.finish(own_small)
    own_rest = flow_rest.finish(own_small)
    output = jnp.concatenate([tie(outputs[0], own_small), outputs[1]], 0)

    owned = [own_small[ends[i] : ends[i + 1]] for i in range(6)]
    totals = own_small[total : total + 6]
    stats = jnp.sqrt(totals[:5] / (totals[5] * width))
    own_out, own_up = own_rest[:, :width], own_rest[:, width:]
    return (output[None], grad_tokens[None], own_qkv, owned[0], own_out, owned[1], owned[2], owned[3], own_up, owned[4],
            own_down, owned[5], stats, totals[5:6])


def solution(mesh):
    rows, wide, flat = P(("dp", "fsdp"), None, None), P(("dp", "fsdp"), None), P(("dp", "fsdp"))
    return jax.shard_map(
        functools.partial(local, Ladder(mesh)),
        mesh=mesh,
        in_specs=(rows, rows, wide, wide, wide, flat, wide, flat, flat, flat, wide, flat, wide, flat),
        out_specs=(rows, rows, wide, flat, wide, flat, flat, flat, wide, flat, wide, flat, P(), P()),
        check_vma=False,
    )
```
